32 devices in a mesh: dp: 8 (over y, x, core), mp: 4 (over z).
Axes of the slice: x: 2, y: 2, z: 4, core: 2. Of those that a mesh axis runs over, the one named last changes fastest.
Arguments:
- act_in: bfloat16 [1024, 4096], P('dp', 'mp'), may hold values from -6 to 6
- grad_in: bfloat16 [1024, 16384], P('dp'), may hold values from -6 to 6
- query_act: bfloat16 [1024, 4096], P('dp', 'mp'), may hold values from -6 to 6
- query_grad: bfloat16 [1024, 16384], P('dp'), may hold values from -6 to 6
- act_basis: bfloat16 [4096, 128], P('mp'), may hold values from -1.1 to 1.1
- grad_basis: bfloat16 [16384, 128], P('dp'), may hold values from -1.1 to 1.1
- seq_lengths: int32 [4], replicated, may hold values from 1 to 256, 768 in all
Outputs:
- moments: float32 [4096, 16384], P('mp', 'dp')
- scores: float32 [64, 4], replicated
The draws below stay inside these ranges and needn't reach their ends.
Inputs may be any that keep to these rules, and one draw needn't show every extreme that they name: `seq_lengths`: live tokens are the first ones of each sequence, and one sequence is full.
All inputs are finite; a program needn't handle non-finite values.
Results may differ from the reference program's by a relative error of at most 0.0046.
Values may be sent and summed in bfloat16 or wider, within the bound.
A program may use at most 192 MiB of HBM per device.

```python
import math
import jax
import jax.numpy as jnp
import numpy as np
from jax import lax

D = 4096
FF = 16384
BLOCK = 128
SEQS = 4
QUERIES = 64
QUERY_LEN = 16
TOKENS = 1024
SEQ_LEN = 256
QROWS = 1024


def basis_blocks(key, total_rows):
    first_key, second_key = jax.random.split(key)
    base = jnp.clip(jax.random.normal(first_key, (total_rows, BLOCK), jnp.float32), -4.0, 4.0)
    column_scale = jnp.exp(jax.random.uniform(second_key, (total_rows // BLOCK, 1, BLOCK), jnp.float32, math.log(0.3), math.log(3.0)))
    blocks = base.reshape(total_rows // BLOCK, BLOCK, BLOCK) * column_scale / math.sqrt(BLOCK)
    blocks = jnp.clip(blocks, -1.09375, 1.09375)
    return blocks.reshape(total_rows, BLOCK).astype(jnp.bfloat16)


def draw_act_basis(key, part):
    return basis_blocks(jax.random.fold_in(key, 11), D)


def draw_grad_basis(key, part):
    return basis_blocks(jax.random.fold_in(key, 23), FF)


def level_of(key, shape, cuts, smallest, top_value):
    factor_of = 1.0
    for dim, blocks in cuts:
        steps = jax.random.uniform(jax.random.fold_in(jax.random.fold_in(key, 6), dim), (blocks,), jnp.float32, smallest / len(cuts), top_value / len(cuts))
        factor_of = factor_of * jnp.repeat(jnp.exp(steps), shape[dim] // blocks).reshape((-1,) + (1,) * (len(shape) - 1 - dim))
    return factor_of


def split_up(number_of, total, limit, skew):
    portions = [(1 << 20) // math.isqrt(rank ** skew) + 1 for rank in range(2, number_of + 1)]
    spare, given = total - limit - (number_of - 1), [1] * (number_of - 1)
    while spare > 0:
        movable = [i for i in range(number_of - 1) if given[i] < limit]
        whole, remaining = sum([portions[i] for i in movable]), spare
        for i in movable:
            more = min(limit - given[i], max(1, remaining * portions[i] // whole), spare)
            given[i] = given[i] + more
            spare = spare - more
    return np.array([limit] + given)


def uneven(stream_key, amount, total, reach, slope):
    if amount == 2:
        one = jax.random.randint(stream_key, (), max(1, total - reach), min(reach, total - 1) + 1)
        return jnp.stack([one, total - one])
    sizes = jnp.asarray(split_up(amount, total, reach, slope), jnp.int32)
    pairs = (amount - 1) // 2
    donor, sink = sizes[1:1 + 2 * pairs:2], sizes[2:2 + 2 * pairs:2]
    margin = jnp.minimum(donor - 1, reach - sink)
    shifted = jax.random.randint(jax.random.fold_in(stream_key, 1), (pairs,), 0, 1 << 20) % (margin + 1)
    sizes = sizes.at[1:1 + 2 * pairs:2].set(donor - shifted).at[2:2 + 2 * pairs:2].set(sink + shifted)
    return sizes[jax.random.permutation(jax.random.fold_in(stream_key, 2), amount)]


def bell_draw(own_key, shape, width, limit, cuts=(), kind=jnp.bfloat16):
    entries = width * jax.random.normal(own_key, shape, jnp.float32)
    if cuts:
        entries = entries * level_of(own_key, shape, cuts, -0.22, 0.18)
    return jnp.clip(entries, -limit, limit).astype(kind)


def setup_inputs(seed: int = 0) -> dict:
    seeds = jax.random.split(jax.random.key(seed), 8)
    return {
        "act_in": bell_draw(seeds[0], (TOKENS, D), 1.0, 6.0, ((0, 8), (1, 4))),
        "grad_in": bell_draw(seeds[1], (TOKENS, FF), 1.0, 6.0, ((0, 8),)),
        "query_act": bell_draw(seeds[2], (QROWS, D), 1.0, 6.0, ((0, 8), (1, 4))),
        "query_grad": bell_draw(seeds[3], (QROWS, FF), 1.0, 6.0, ((0, 8),)),
        "act_basis": draw_act_basis(jax.random.fold_in(seeds[7], 71), 0),
        "grad_basis": draw_grad_basis(jax.random.fold_in(seeds[7], 71), 0),
        "seq_lengths": uneven(seeds[6], SEQS, SEQS * SEQ_LEN * 3 // 4, SEQ_LEN, 0).astype(jnp.int32),
    }


damping = 0.1

def rotate(rows_in, basis_rows):
    count_rows, full_width = rows_in.shape
    block_size = basis_rows.shape[1]
    blocks = full_width // block_size
    product = jnp.einsum('nbk,bkc->nbc', rows_in.reshape(count_rows, blocks, block_size).astype(jnp.float32), basis_rows.reshape(blocks, block_size, block_size).astype(jnp.float32))
    return product.reshape(count_rows, full_width)

def reference(act_in, grad_in, query_act, query_grad, act_basis, grad_basis, seq_lengths):
    position = jnp.arange(TOKENS, dtype=jnp.int32)
    seq_index = (position // SEQ_LEN).astype(jnp.int32)
    within = position % SEQ_LEN
    live_rows = (within < seq_lengths[seq_index]).astype(jnp.float32)
    act_rot = (rotate(act_in, act_basis) * live_rows[:, None]).astype(jnp.bfloat16)
    grad_rot = rotate(grad_in, grad_basis).astype(jnp.bfloat16)
    query_act_rot = rotate(query_act, act_basis).astype(jnp.bfloat16)
    query_grad_rot = rotate(query_grad, grad_basis).astype(jnp.bfloat16)
    act_square = jnp.square(act_rot.astype(jnp.float32)).astype(jnp.bfloat16)
    grad_square = jnp.square(grad_rot.astype(jnp.float32)).astype(jnp.bfloat16)
    counted = jnp.sum(seq_lengths).astype(jnp.float32)
    moments = jnp.dot(act_square.T, grad_square, preferred_element_type=jnp.float32) / counted
    weights = 1.0 / (moments + damping)
    scale_seq = lax.rsqrt(seq_lengths.astype(jnp.float32))

    def one_sequence(inputs):
        seq_acts, seq_grads, scale_one = inputs
        seq_grad = jnp.dot(seq_acts.T, seq_grads, preferred_element_type=jnp.float32)
        precond = (weights * seq_grad * scale_one).astype(jnp.bfloat16)
        mapped = jnp.dot(query_act_rot, precond, preferred_element_type=jnp.float32)
        per_row = lax.optimization_barrier(jnp.sum(mapped * query_grad_rot.astype(jnp.float32), axis=1))
        return lax.optimization_barrier(jnp.sum(per_row.reshape(QUERIES, QUERY_LEN), axis=1))
    columns = lax.map(one_sequence, (act_rot.reshape(SEQS, SEQ_LEN, D), grad_rot.reshape(SEQS, SEQ_LEN, FF), scale_seq))
    scores = columns.T / math.sqrt(QUERY_LEN * D * FF)
    return (moments, scores)
```

```python
import functools
import math

import jax
import jax.numpy as jnp
from jax import lax
from jax.experimental import pallas as pl
from jax.experimental.pallas import tpu as pltpu
from jax.sharding import PartitionSpec as P

D = 4096
FF = 16384
QUERIES = 64
QUERY_LEN = 16

damping = 0.1
MESH = pl.DeviceIdType.MESH


def flipped(index, mask):
    bit = 1
    while bit <= mask:
        if mask & bit:
            index = index + bit * (1 - 2 * ((index // bit) % 2))
        bit *= 2
    return index


def kernel(
    dp_count, mp_count, chunks, shared_train, shared_query,
    lengths, act_in, grad_in, query_act, query_grad, act_basis_in, grad_basis_in,
    moments, partial,
    act_raw, qact_raw, grad_raw, qgrad_raw, act_basis, grad_basis,
    act_t, q_rot, precond, staged, totals,
    act_send, act_recv, qact_send, qact_recv, grad_send, grad_recv, qgrad_send, qgrad_recv,
    pass_send, pass_recv, qpass_send, qpass_recv, local_sem, out_sem,
    shares, crossing, share_send, share_recv, cross_send, cross_recv,
):
    me = lax.axis_index("dp")
    mine = lax.axis_index("mp")
    seq_count = lengths.shape[0]
    tok_dev, act_width = act_in.shape
    q_dev = query_act.shape[0]
    cols = grad_raw.shape[2]
    block = act_basis_in.shape[1]
    tiles, _, tile = staged.shape
    tokens = tok_dev * dp_count
    seq_len = tokens // seq_count
    q_rows = q_dev * dp_count
    chunk_cols = cols // chunks
    masks = list(range(1, dp_count))
    peers = {k: flipped(me, k) for k in masks}

    barrier = pltpu.get_barrier_semaphore()
    for k in masks:
        pl.semaphore_signal(barrier, inc=1, device_id={"dp": peers[k], "mp": mine}, device_id_type=MESH)
    others = [lax.rem(mine + step, mp_count) for step in range(1, mp_count)]
    for other in others:
        pl.semaphore_signal(barrier, inc=1, device_id={"dp": me, "mp": other}, device_id_type=MESH)

    locals_in = [
        pltpu.make_async_copy(act_in, act_raw.at[me], local_sem.at[0]),
        pltpu.make_async_copy(act_basis_in, act_basis, local_sem.at[1]),
        pltpu.make_async_copy(grad_basis_in, grad_basis, local_sem.at[2]),
        pltpu.make_async_copy(
            grad_in.at[:, pl.ds(pl.multiple_of(me * cols, 128), cols)], grad_raw.at[me], local_sem.at[3]),
        pltpu.make_async_copy(query_act, qact_raw.at[me], local_sem.at[4]),
        pltpu.make_async_copy(
            query_grad.at[:, pl.ds(pl.multiple_of(me * cols, 128), cols)], qgrad_raw.at[me], local_sem.at[5]),
    ]
    for copy in locals_in:
        copy.start()
    pl.semaphore_wait(barrier, len(masks) + len(others))

    def remote(src, dst, send, recv, dp, mp):
        return pltpu.make_async_remote_copy(
            src_ref=src, dst_ref=dst, send_sem=send, recv_sem=recv,
            device_id={"dp": dp, "mp": mp}, device_id_type=MESH)

    sends = []

    def begin(copy):
        copy.start()
        sends.append(copy)

    act_masks = [k for k in masks if k == 1 or k % 2 == 0]

    def send_acts(src, raw, send, recv):
        for k in reversed(act_masks):
            begin(remote(src, raw.at[me], send.at[k], recv.at[k], peers[k], mine))

    def part_of(owner, rows):
        return pl.ds(pl.multiple_of(owner * (rows // mp_count), 16), rows // mp_count)

    def send_shared(src, raw, send, recv, shared):
        rows = part_of(mine, src.shape[0])
        for k in reversed(shared):
            there = pl.ds(pl.multiple_of(peers[k] * cols, 128), cols)
            begin(remote(
                src.at[rows, there], raw.at[me, rows, :], send.at[0, k], recv.at[0, k], peers[k], mine))

    def send_grads(src, raw, send, recv, shared, start, width, slot):
        for k in reversed(masks):
            if k not in shared:
                there = pl.ds(pl.multiple_of(peers[k] * cols + start, 128), width)
                begin(remote(
                    src.at[:, there], raw.at[me, :, pl.ds(start, width)],
                    send.at[slot, k], recv.at[slot, k], peers[k], mine))

    send_acts(act_in, act_raw, act_send, act_recv)
    send_shared(grad_in, grad_raw, grad_send, grad_recv, shared_train)
    send_shared(query_grad, qgrad_raw, qgrad_send, qgrad_recv, shared_query)
    send_grads(grad_in, grad_raw, grad_send, grad_recv, shared_train, 0, cols, 0)
    send_acts(query_act, qact_raw, qact_send, qact_recv)
    for c in range(chunks):
        send_grads(query_grad, qgrad_raw, qgrad_send, qgrad_recv, shared_query, c * chunk_cols, chunk_cols, c)

    def arrived(ref, send, recv):
        remote(ref, ref, send, recv, peers[1], mine).wait_recv()

    def relay_acts(raw, send, recv):
        for k in reversed(act_masks):
            arrived(raw.at[peers[k]], send.at[k], recv.at[k])
            if k > 1:
                here = raw.at[peers[k]]
                begin(remote(here, here, send.at[k + 1], recv.at[k + 1], peers[1], mine))

    def finish_acts(raw, send, recv):
        for k in masks:
            if k not in act_masks:
                arrived(raw.at[peers[k]], send.at[k], recv.at[k])

    def relay_grads(raw, send, recv, fsend, frecv, shared):
        for n, k in enumerate(reversed(shared)):
            here = raw.at[peers[k], part_of(mine, raw.shape[1]), :]
            arrived(here, send.at[0, k], recv.at[0, k])
            for step, other in enumerate(others):
                begin(remote(here, here, fsend.at[n, step], frecv.at[n, step], me, other))

    def finish_grads(raw, send, recv, shared, start, width, slot):
        for k in reversed(masks):
            if k not in shared:
                arrived(raw.at[peers[k], :, pl.ds(start, width)], send.at[slot, k], recv.at[slot, k])

    def finish_shared(raw, fsend, frecv, shared):
        for n, k in enumerate(reversed(shared)):
            for step in range(mp_count - 1):
                owner = lax.rem(mine + (mp_count - 1 - step), mp_count)
                arrived(
                    raw.at[peers[k], part_of(owner, raw.shape[1]), :], fsend.at[n, step], frecv.at[n, step])

    relay_acts(act_raw, act_send, act_recv)
    finish_acts(act_raw, act_send, act_recv)
    relay_grads(grad_raw, grad_send, grad_recv, pass_send, pass_recv, shared_train)
    relay_grads(qgrad_raw, qgrad_send, qgrad_recv, qpass_send, qpass_recv, shared_query)
    for copy in locals_in:
        copy.wait()

    limits = [lengths[s] for s in range(seq_count)]
    counted = limits[0]
    for s in range(1, seq_count):
        counted = counted + limits[s]
    inverse = 1.0 / jnp.full((1, tile), counted.astype(jnp.float32), jnp.float32)

    @pl.loop(0, dp_count)
    def _(e):
        where_tok = e * tok_dev + lax.broadcasted_iota(jnp.int32, (block, tok_dev), 1)
        live = jnp.zeros((block, tok_dev), jnp.float32)
        for s in range(seq_count):
            inside = (where_tok >= s * seq_len) & (where_tok < s * seq_len + limits[s])
            live = jnp.where(inside, 1.0, live)
        for b in range(act_width // block):
            span = pl.ds(b * block, block)
            turned = lax.dot_general(
                act_basis[span, :].T, act_raw[e, :, span], (((1,), (1,)), ((), ())),
                preferred_element_type=jnp.float32)
            act_t[span, pl.ds(pl.multiple_of(e * tok_dev, 128), tok_dev)] = (turned * live).astype(jnp.bfloat16)

    def wide_basis(jt):
        first = grad_basis[pl.ds(pl.multiple_of(jt * tile, 128), block), :]
        rows = []
        count = tile // block
        zero = jnp.zeros_like(first)
        for h in range(count):
            own = grad_basis[pl.ds(pl.multiple_of(jt * tile + h * block, 128), block), :]
            rows.append(jnp.concatenate([own if g == h else zero for g in range(count)], axis=1))
        return jnp.concatenate(rows, axis=0)

    def turned_grads(raw, jt, rows):
        span = pl.ds(pl.multiple_of(jt * tile, 128), tile)
        whole = raw[:, :, span].reshape(rows, tile)
        return jnp.dot(whole, wide_basis(jt), preferred_element_type=jnp.float32).astype(jnp.bfloat16)

    finish_shared(grad_raw, pass_send, pass_recv, shared_train)
    finish_grads(grad_raw, grad_send, grad_recv, shared_train, 0, cols, 0)

    def out_copy(jt):
        span = pl.ds(pl.multiple_of(jt * tile, 128), tile)
        return pltpu.make_async_copy(staged.at[jt], moments.at[:, span], out_sem.at[jt])

    per_chunk = tiles // chunks

    def first_phase(jt):
        grads = turned_grads(grad_raw, jt, tokens)
        total = jnp.zeros((act_width, tile), jnp.float32)
        for s in range(seq_count):
            a = act_t[:, s * seq_len:(s + 1) * seq_len]
            g = grads[s * seq_len:(s + 1) * seq_len, :]
            total = total + jnp.dot(a * a, g * g, preferred_element_type=jnp.float32)
        total = total * inverse
        moments[:, pl.ds(pl.multiple_of(jt * tile, 128), tile)] = total
        weights = 1.0 / (total + damping)
        for s in range(seq_count):
            a = act_t[:, s * seq_len:(s + 1) * seq_len]
            g = grads[s * seq_len:(s + 1) * seq_len, :]
            precond[s, jt] = (weights * jnp.dot(a, g, preferred_element_type=jnp.float32)).astype(jnp.bfloat16)

    half = tiles // 2
    pl.loop(0, half)(first_phase)
    relay_acts(qact_raw, qact_send, qact_recv)
    pl.loop(half, tiles)(first_phase)
    finish_acts(qact_raw, qact_send, qact_recv)

    @pl.loop(0, dp_count)
    def _(e):
        for b in range(act_width // block):
            span = pl.ds(b * block, block)
            turned = jnp.dot(qact_raw[e, :, span], act_basis[span, :], preferred_element_type=jnp.float32)
            q_rot[pl.ds(pl.multiple_of(e * q_dev, 16), q_dev), span] = turned.astype(jnp.bfloat16)

    totals[...] = jnp.zeros_like(totals)
    finish_shared(qgrad_raw, qpass_send, qpass_recv, shared_query)

    def second_phase(jt):
        grads = turned_grads(qgrad_raw, jt, q_rows).astype(jnp.float32)
        for s in range(seq_count):
            mapped = jnp.dot(q_rot[...], precond[s, jt], preferred_element_type=jnp.float32) * grads
            folded = mapped[:, :128]
            for h in range(1, tile // 128):
                folded = folded + mapped[:, h * 128:(h + 1) * 128]
            totals[s] += folded.reshape(QUERIES, q_rows // QUERIES // 8, 8, 128).sum(axis=1)

    for c in range(chunks):
        finish_grads(qgrad_raw, qgrad_send, qgrad_recv, shared_query, c * chunk_cols, chunk_cols, c)
        pl.loop(c * per_chunk, (c + 1) * per_chunk)(second_phase)

    lane = lax.broadcasted_iota(jnp.int32, (QUERIES, 128), 1)
    answer = jnp.zeros((QUERIES, 128), jnp.float32)
    for s in range(seq_count):
        row = jnp.sum(jnp.sum(totals[s], axis=1), axis=1, keepdims=True)
        answer = jnp.where(lane == s, row, answer)
    lens = jnp.ones((QUERIES, 128), jnp.float32)
    for s in range(seq_count):
        lens = jnp.where(lane == s, limits[s].astype(jnp.float32), lens)
    shares[me] = answer * lax.rsqrt(lens) / math.sqrt(QUERY_LEN * D * FF)

    for copy in sends:
        copy.wait_send()
    sends.clear()

    for k in masks:
        begin(remote(shares.at[me], shares.at[me], share_send.at[k], share_recv.at[k], peers[k], mine))
    for k in masks:
        arrived(shares.at[peers[k]], share_send.at[k], share_recv.at[k])
    summed = shares[0]
    for e in range(1, dp_count):
        summed = summed + shares[e]
    crossing[mine] = summed
    for step, other in enumerate(others):
        begin(remote(
            crossing.at[mine], crossing.at[mine], cross_send.at[step], cross_recv.at[step], me, other))
    for step in range(mp_count - 1):
        owner = lax.rem(mine + (mp_count - 1 - step), mp_count)
        arrived(crossing.at[owner], cross_send.at[step], cross_recv.at[step])
    summed = crossing[0]
    for e in range(1, mp_count):
        summed = summed + crossing[e]
    partial[...] = summed
    for copy in sends:
        copy.wait_send()


def local(act_in, grad_in, query_act, query_grad, act_basis, grad_basis, seq_lengths):
    dp_count = lax.axis_size("dp")
    mp_count = lax.axis_size("mp")
    tok_dev, act_width = act_in.shape
    q_dev = query_act.shape[0]
    cols = grad_in.shape[1] // dp_count
    seq_count = seq_lengths.shape[0]
    tokens, q_rows = tok_dev * dp_count, q_dev * dp_count
    tile = min(256, cols)
    tiles = cols // tile
    chunks = min(4, tiles)
    far = [k for k in range(1, dp_count) if bin(k >> 1).count("1") >= 2]
    shared_train = far if tok_dev % (16 * mp_count) == 0 and dp_count <= 2 * tiles else []
    shared_query = far if q_dev % (16 * mp_count) == 0 and dp_count <= 2 * tiles else []
    steps = max(1, mp_count - 1)
    dma = pltpu.SemaphoreType.DMA
    any_space = pl.BlockSpec(memory_space=pl.ANY)
    bf16 = jnp.bfloat16
    raw, scores = pl.pallas_call(
        functools.partial(kernel, dp_count, mp_count, chunks, shared_train, shared_query),
        out_shape=(
            pltpu.VMEM((act_width, cols), jnp.float32),
            pltpu.VMEM((QUERIES, 128), jnp.float32),
        ),
        in_specs=[pl.BlockSpec(memory_space=pltpu.SMEM)] + [any_space] * 6,
        out_specs=(pl.BlockSpec(memory_space=pltpu.VMEM), pl.BlockSpec(memory_space=pltpu.VMEM)),
        scratch_shapes=[
            pltpu.VMEM((dp_count, tok_dev, act_width), bf16),
            pltpu.VMEM((dp_count, q_dev, act_width), bf16),
            pltpu.VMEM((dp_count, tok_dev, cols), bf16),
            pltpu.VMEM((dp_count, q_dev, cols), bf16),
            pltpu.VMEM(act_basis.shape, bf16),
            pltpu.VMEM(grad_basis.shape, bf16),
            pltpu.VMEM((act_width, tokens), bf16),
            pltpu.VMEM((q_rows, act_width), bf16),
            pltpu.VMEM((seq_count, tiles, act_width, tile), bf16),
            pltpu.VMEM((tiles, 8, tile), jnp.float32),
            pltpu.VMEM((seq_count, QUERIES, 8, 128), jnp.float32),
            dma((dp_count,)), dma((dp_count,)), dma((dp_count,)), dma((dp_count,)),
            dma((1, dp_count)), dma((1, dp_count)), dma((chunks, dp_count)), dma((chunks, dp_count)),
            dma((max(1, len(shared_train)), steps)), dma((max(1, len(shared_train)), steps)),
            dma((max(1, len(shared_query)), steps)), dma((max(1, len(shared_query)), steps)),
            dma((6,)), dma((tiles,)),
            pltpu.VMEM((dp_count, QUERIES, 128), jnp.float32),
            pltpu.VMEM((mp_count, QUERIES, 128), jnp.float32),
            dma((dp_count,)), dma((dp_count,)), dma((steps,)), dma((steps,)),
        ],
        compiler_params=pltpu.CompilerParams(
            collective_id=0, has_side_effects=True, vmem_limit_bytes=54 * 1024 * 1024),
    )(seq_lengths, act_in, grad_in, query_act, query_grad, act_basis, grad_basis)
    moments, scores = store(raw, scores, seq_count)
    return moments, scores.T


def store_kernel(raw, scores_in, moments, scores, sems):
    n = sems.shape[0]
    rows = raw.shape[0] // n
    copies = [pltpu.make_async_copy(raw.at[pl.ds(i * rows, rows)], moments.at[pl.ds(i * rows, rows)], sems.at[i])
              for i in range(n)]
    for c in copies:
        c.start()
    scores[...] = scores_in[...].T[:scores.shape[0], :]
    for c in copies:
        c.wait()


def store(raw, scores, seq_count):
    n = 8
    vm = pl.BlockSpec(memory_space=pltpu.VMEM)
    return pl.pallas_call(
        store_kernel,
        out_shape=(jax.ShapeDtypeStruct(raw.shape, raw.dtype), jax.ShapeDtypeStruct((seq_count, scores.shape[0]), scores.dtype)),
        in_specs=[vm, vm], out_specs=(pl.BlockSpec(memory_space=pltpu.HBM), vm),
        scratch_shapes=[pltpu.SemaphoreType.DMA((n,))],
        compiler_params=pltpu.CompilerParams(vmem_limit_bytes=1024*1024),
    )(pltpu.with_memory_space_constraint(raw, pltpu.VMEM), pltpu.with_memory_space_constraint(scores, pltpu.VMEM))


def solution(mesh):
    return jax.shard_map(
        local,
        mesh=mesh,
        in_specs=(
            P("dp", "mp"),
            P("dp", None),
            P("dp", "mp"),
            P("dp", None),
            P("mp", None),
            P("dp", None),
            P(),
        ),
        out_specs=(P("mp", "dp"), P()),
        check_vma=False,
    )
```

```python
import functools
import math

import jax
import jax.numpy as jnp
from jax import lax
from jax.experimental import pallas as pl
from jax.experimental.pallas import tpu as pltpu
from jax.sharding import PartitionSpec as P

D = 4096
FF = 16384
QUERIES = 64
QUERY_LEN = 16

damping = 0.1
MESH = pl.DeviceIdType.MESH


def flipped(index, mask):
    bit = 1
    while bit <= mask:
        if mask & bit:
            index = index + bit * (1 - 2 * ((index // bit) % 2))
        bit *= 2
    return index


def across(columns):
    square = jnp.concatenate([columns, jnp.zeros((128 - columns.shape[0], 128), jnp.float32)], axis=0)
    return square.T[:8, :]


def kernel(
    dp_count, mp_count, chunks, shared_train, shared_query,
    lengths, act_in, grad_in, query_act, query_grad, act_basis_in, grad_basis_in,
    moments, partial,
    act_raw, qact_raw, grad_raw, qgrad_raw, act_basis, grad_basis,
    act_t, q_rot, precond, staged, totals,
    act_send, act_recv, qact_send, qact_recv, grad_send, grad_recv, qgrad_send, qgrad_recv,
    pass_send, pass_recv, qpass_send, qpass_recv, local_sem, out_sem,
    shares, crossing, share_send, share_recv, cross_send, cross_recv,
):
    me = lax.axis_index("dp")
    mine = lax.axis_index("mp")
    seq_count = lengths.shape[0]
    tok_dev, act_width = act_in.shape
    q_dev = query_act.shape[0]
    cols = grad_raw.shape[2]
    block = act_basis_in.shape[1]
    tiles, _, tile = staged.shape
    tokens = tok_dev * dp_count
    seq_len = tokens // seq_count
    q_rows = q_dev * dp_count
    chunk_cols = cols // chunks
    masks = list(range(1, dp_count))
    peers = {k: flipped(me, k) for k in masks}

    barrier = pltpu.get_barrier_semaphore()
    for k in masks:
        pl.semaphore_signal(barrier, inc=1, device_id={"dp": peers[k], "mp": mine}, device_id_type=MESH)
    others = [lax.rem(mine + step, mp_count) for step in range(1, mp_count)]
    for other in others:
        pl.semaphore_signal(barrier, inc=1, device_id={"dp": me, "mp": other}, device_id_type=MESH)

    locals_in = [
        pltpu.make_async_copy(act_in, act_raw.at[me], local_sem.at[0]),
        pltpu.make_async_copy(act_basis_in, act_basis, local_sem.at[1]),
        pltpu.make_async_copy(grad_basis_in, grad_basis, local_sem.at[2]),
        pltpu.make_async_copy(
            grad_in.at[:, pl.ds(pl.multiple_of(me * cols, 128), cols)], grad_raw.at[me], local_sem.at[3]),
        pltpu.make_async_copy(query_act, qact_raw.at[me], local_sem.at[4]),
        pltpu.make_async_copy(
            query_grad.at[:, pl.ds(pl.multiple_of(me * cols, 128), cols)], qgrad_raw.at[me], local_sem.at[5]),
    ]
    for copy in locals_in:
        copy.start()
    pl.semaphore_wait(barrier, len(masks) + len(others))

    def remote(src, dst, send, recv, dp, mp):
        return pltpu.make_async_remote_copy(
            src_ref=src, dst_ref=dst, send_sem=send, recv_sem=recv,
            device_id={"dp": dp, "mp": mp}, device_id_type=MESH)

    sends = []

    def begin(copy):
        copy.start()
        sends.append(copy)

    act_masks = [k for k in masks if k == 1 or k % 2 == 0]

    def send_acts(src, raw, send, recv):
        for k in reversed(act_masks):
            begin(remote(src, raw.at[me], send.at[k], recv.at[k], peers[k], mine))

    def part_of(owner, rows):
        return pl.ds(pl.multiple_of(owner * (rows // mp_count), 16), rows // mp_count)

    def send_shared(src, raw, send, recv, shared):
        rows = part_of(mine, src.shape[0])
        for k in reversed(shared):
            there = pl.ds(pl.multiple_of(peers[k] * cols, 128), cols)
            begin(remote(
                src.at[rows, there], raw.at[me, rows, :], send.at[0, k], recv.at[0, k], peers[k], mine))

    def send_grads(src, raw, send, recv, shared, start, width, slot):
        for k in reversed(masks):
            if k not in shared:
                there = pl.ds(pl.multiple_of(peers[k] * cols + start, 128), width)
                begin(remote(
                    src.at[:, there], raw.at[me, :, pl.ds(start, width)],
                    send.at[slot, k], recv.at[slot, k], peers[k], mine))

    send_acts(act_in, act_raw, act_send, act_recv)
    send_shared(grad_in, grad_raw, grad_send, grad_recv, shared_train)
    send_shared(query_grad, qgrad_raw, qgrad_send, qgrad_recv, shared_query)
    send_grads(grad_in, grad_raw, grad_send, grad_recv, shared_train, 0, cols, 0)
    send_acts(query_act, qact_raw, qact_send, qact_recv)
    for c in range(chunks):
        send_grads(query_grad, qgrad_raw, qgrad_send, qgrad_recv, shared_query, c * chunk_cols, chunk_cols, c)

    def arrived(ref, send, recv):
        remote(ref, ref, send, recv, peers[1], mine).wait_recv()

    def relay_acts(raw, send, recv):
        for k in reversed(act_masks):
            arrived(raw.at[peers[k]], send.at[k], recv.at[k])
            if k > 1:
                here = raw.at[peers[k]]
                begin(remote(here, here, send.at[k + 1], recv.at[k + 1], peers[1], mine))

    def finish_acts(raw, send, recv):
        for k in masks:
            if k not in act_masks:
                arrived(raw.at[peers[k]], send.at[k], recv.at[k])

    def relay_grads(raw, send, recv, fsend, frecv, shared):
        for n, k in enumerate(reversed(shared)):
            here = raw.at[peers[k], part_of(mine, raw.shape[1]), :]
            arrived(here, send.at[0, k], recv.at[0, k])
            for step, other in enumerate(others):
                begin(remote(here, here, fsend.at[n, step], frecv.at[n, step], me, other))

    def finish_grads(raw, send, recv, shared, start, width, slot):
        for k in reversed(masks):
            if k not in shared:
                arrived(raw.at[peers[k], :, pl.ds(start, width)], send.at[slot, k], recv.at[slot, k])

    def finish_shared(raw, fsend, frecv, shared):
        for n, k in enumerate(reversed(shared)):
            for step in range(mp_count - 1):
                owner = lax.rem(mine + (mp_count - 1 - step), mp_count)
                arrived(
                    raw.at[peers[k], part_of(owner, raw.shape[1]), :], fsend.at[n, step], frecv.at[n, step])

    relay_acts(act_raw, act_send, act_recv)
    finish_acts(act_raw, act_send, act_recv)
    relay_grads(grad_raw, grad_send, grad_recv, pass_send, pass_recv, shared_train)
    relay_grads(qgrad_raw, qgrad_send, qgrad_recv, qpass_send, qpass_recv, shared_query)
    for copy in locals_in:
        copy.wait()

    limits = [lengths[s] for s in range(seq_count)]
    counted = limits[0]
    for s in range(1, seq_count):
        counted = counted + limits[s]
    inverse = 1.0 / jnp.full((1, tile), counted.astype(jnp.float32), jnp.float32)

    @pl.loop(0, dp_count)
    def _(e):
        where_tok = e * tok_dev + lax.broadcasted_iota(jnp.int32, (block, tok_dev), 1)
        live = jnp.zeros((block, tok_dev), jnp.float32)
        for s in range(seq_count):
            inside = (where_tok >= s * seq_len) & (where_tok < s * seq_len + limits[s])
            live = jnp.where(inside, 1.0, live)
        for b in range(act_width // block):
            span = pl.ds(b * block, block)
            turned = lax.dot_general(
                act_basis[span, :].T, act_raw[e, :, span], (((1,), (1,)), ((), ())),
                preferred_element_type=jnp.float32)
            act_t[span, pl.ds(pl.multiple_of(e * tok_dev, 128), tok_dev)] = (turned * live).astype(jnp.bfloat16)

    def wide_basis(jt):
        first = grad_basis[pl.ds(pl.multiple_of(jt * tile, 128), block), :]
        rows = []
        count = tile // block
        zero = jnp.zeros_like(first)
        for h in range(count):
            own = grad_basis[pl.ds(pl.multiple_of(jt * tile + h * block, 128), block), :]
            rows.append(jnp.concatenate([own if g == h else zero for g in range(count)], axis=1))
        return jnp.concatenate(rows, axis=0)

    def turned_grads(raw, jt, rows):
        span = pl.ds(pl.multiple_of(jt * tile, 128), tile)
        whole = raw[:, :, span].reshape(rows, tile)
        return jnp.dot(whole, wide_basis(jt), preferred_element_type=jnp.float32).astype(jnp.bfloat16)

    finish_shared(grad_raw, pass_send, pass_recv, shared_train)
    finish_grads(grad_raw, grad_send, grad_recv, shared_train, 0, cols, 0)

    def out_copy(jt):
        span = pl.ds(pl.multiple_of(jt * tile, 128), tile)
        return pltpu.make_async_copy(staged.at[jt], moments.at[:, span], out_sem.at[jt])

    per_chunk = tiles // chunks

    def first_phase(jt):
        grads = turned_grads(grad_raw, jt, tokens)
        total = jnp.zeros((act_width, tile), jnp.float32)
        for s in range(seq_count):
            a = act_t[:, s * seq_len:(s + 1) * seq_len]
            g = grads[s * seq_len:(s + 1) * seq_len, :]
            total = total + jnp.dot(a * a, g * g, preferred_element_type=jnp.float32)
        total = total * inverse
        moments[:, pl.ds(pl.multiple_of(jt * tile, 128), tile)] = total
        weights = 1.0 / (total + damping)
        for s in range(seq_count):
            a = act_t[:, s * seq_len:(s + 1) * seq_len]
            g = grads[s * seq_len:(s + 1) * seq_len, :]
            precond[s, jt] = (weights * jnp.dot(a, g, preferred_element_type=jnp.float32)).astype(jnp.bfloat16)

    half = tiles // 2
    pl.loop(0, half)(first_phase)
    relay_acts(qact_raw, qact_send, qact_recv)
    pl.loop(half, tiles)(first_phase)
    finish_acts(qact_raw, qact_send, qact_recv)

    @pl.loop(0, dp_count)
    def _(e):
        for b in range(act_width // block):
            span = pl.ds(b * block, block)
            turned = jnp.dot(qact_raw[e, :, span], act_basis[span, :], preferred_element_type=jnp.float32)
            q_rot[pl.ds(pl.multiple_of(e * q_dev, 16), q_dev), span] = turned.astype(jnp.bfloat16)

    totals[...] = jnp.zeros_like(totals)
    finish_shared(qgrad_raw, qpass_send, qpass_recv, shared_query)

    def second_phase(jt):
        grads = turned_grads(qgrad_raw, jt, q_rows).astype(jnp.float32)
        for s in range(seq_count):
            mapped = jnp.dot(q_rot[...], precond[s, jt], preferred_element_type=jnp.float32) * grads
            folded = mapped[:, :128]
            for h in range(1, tile // 128):
                folded = folded + mapped[:, h * 128:(h + 1) * 128]
            totals[s] += folded.reshape(QUERIES, q_rows // QUERIES // 8, 8, 128).sum(axis=1)

    for c in range(chunks):
        finish_grads(qgrad_raw, qgrad_send, qgrad_recv, shared_query, c * chunk_cols, chunk_cols, c)
        pl.loop(c * per_chunk, (c + 1) * per_chunk)(second_phase)

    lane = lax.broadcasted_iota(jnp.int32, (QUERIES, 128), 1)
    answer = jnp.zeros((QUERIES, 128), jnp.float32)
    for s in range(seq_count):
        row = jnp.sum(jnp.sum(totals[s], axis=1), axis=1, keepdims=True)
        answer = jnp.where(lane == s, row, answer)
    lens = jnp.ones((QUERIES, 128), jnp.float32)
    for s in range(seq_count):
        lens = jnp.where(lane == s, limits[s].astype(jnp.float32), lens)
    shares[me] = answer * lax.rsqrt(lens) / math.sqrt(QUERY_LEN * D * FF)

    for copy in sends:
        copy.wait_send()
    sends.clear()

    for k in masks:
        begin(remote(shares.at[me], shares.at[me], share_send.at[k], share_recv.at[k], peers[k], mine))
    for k in masks:
        arrived(shares.at[peers[k]], share_send.at[k], share_recv.at[k])
    summed = shares[0]
    for e in range(1, dp_count):
        summed = summed + shares[e]
    crossing[mine] = summed
    for step, other in enumerate(others):
        begin(remote(
            crossing.at[mine], crossing.at[mine], cross_send.at[step], cross_recv.at[step], me, other))
    for step in range(mp_count - 1):
        owner = lax.rem(mine + (mp_count - 1 - step), mp_count)
        arrived(crossing.at[owner], cross_send.at[step], cross_recv.at[step])
    summed = crossing[0]
    for e in range(1, mp_count):
        summed = summed + crossing[e]
    partial[...] = across(summed)
    for copy in sends:
        copy.wait_send()


ENDS = {"a": (0, 5), "b": (5, 7), "c": (7, 8)}
HALVES = {"a": (0, 4), "b": (4, 8)}
NEAR = (2, 4, 3, 5)
FAR = (6, 7)
SETS = {"a": 0, "b": 1, "c": 2}
QCUTS = (0, 2, 4, 6, 8)
TCUTS = (0, 2, 4, 6, 8)


def routed_kernel(
    lengths, act_in, grad_in, query_act, query_grad, act_basis_in, grad_basis_in,
    moments, partial,
    act_raw, qact_raw, grad_raw, qgrad_raw, act_basis, grad_basis,
    act_t, act_sq, q_rot, precond, totals, shares, crossing,
    act_send, act_recv, hop_send, pass_send, grad_recv, side_send, side_recv, local_sem,
    share_send, share_recv, cross_send, cross_recv,
):
    me = lax.axis_index("dp")
    mine = lax.axis_index("mp")
    dp_count, tok_dev, act_width = act_raw.shape
    mp_count = crossing.shape[0]
    seq_count = lengths.shape[0]
    q_dev = qact_raw.shape[1]
    cols = grad_raw.shape[2]
    block = act_basis.shape[1]
    tiles, tile = precond.shape[1], precond.shape[3]
    tokens = tok_dev * dp_count
    seq_len = tokens // seq_count
    q_rows = q_dev * dp_count
    masks = list(range(1, dp_count))
    peers = {k: flipped(me, k) for k in masks}
    others = [lax.rem(mine + step, mp_count) for step in range(1, mp_count)]

    is_end = (mine == 0) | (mine == mp_count - 1)
    is_mid = jnp.logical_not(is_end)
    partner = flipped(mine, 1)
    half = lax.rem(mine + 1, 2)
    far_planes = [partner, mp_count - 1 - mine, mp_count - 1 - partner]

    barrier = pltpu.get_barrier_semaphore()
    for k in masks:
        pl.semaphore_signal(barrier, inc=1, device_id={"dp": peers[k], "mp": mine}, device_id_type=MESH)
    for other in others:
        pl.semaphore_signal(barrier, inc=1, device_id={"dp": me, "mp": other}, device_id_type=MESH)

    own = pl.ds(pl.multiple_of(me * cols, 128), cols)
    locals_in = [
        pltpu.make_async_copy(act_in, act_raw.at[me], local_sem.at[0]),
        pltpu.make_async_copy(act_basis_in, act_basis, local_sem.at[1]),
        pltpu.make_async_copy(grad_basis_in, grad_basis, local_sem.at[2]),
        pltpu.make_async_copy(grad_in.at[:, own], grad_raw.at[me], local_sem.at[3]),
        pltpu.make_async_copy(query_act, qact_raw.at[me], local_sem.at[4]),
        pltpu.make_async_copy(query_grad.at[:, own], qgrad_raw.at[me], local_sem.at[5]),
    ]
    for copy in locals_in:
        copy.start()
    pl.semaphore_wait(barrier, len(masks) + len(others))

    def remote(src, dst, send, recv, dp, mp):
        return pltpu.make_async_remote_copy(
            src_ref=src, dst_ref=dst, send_sem=send, recv_sem=recv,
            device_id={"dp": dp, "mp": mp}, device_id_type=MESH)

    started = {"end": [], "mid": [], "all": []}

    def begin(role, build):
        build().start()
        started[role].append(build)

    def arrived(ref, recv):
        remote(ref, ref, side_send.at[0], recv, peers[1], mine).wait_recv()

    def by_role(act):
        @pl.when(is_end)
        def _():
            act("end")

        @pl.when(is_mid)
        def _():
            act("mid")

    phases = (
        (grad_in, grad_raw, tok_dev, TCUTS),
        (query_grad, qgrad_raw, q_dev, QCUTS),
    )

    def span_of(phase, c):
        cuts = phases[phase][3]
        return cuts[c] * tile, (cuts[c + 1] - cuts[c]) * tile

    def rows_of(phase, k, part):
        eighth = phases[phase][2] // 8
        if k in FAR:
            if part == "own":
                return pl.ds(pl.multiple_of(half * (4 * eighth), 16), 4 * eighth), half
            if part == "other":
                return pl.ds(pl.multiple_of((1 - half) * (4 * eighth), 16), 4 * eighth), 1 - half
            low, high = HALVES[part]
        else:
            low, high = ENDS[part]
        return pl.ds(low * eighth, (high - low) * eighth), SETS[part]

    def place(phase, k, part, c):
        start, width = span_of(phase, c)
        rows, number = rows_of(phase, k, part)
        here = phases[phase][1].at[peers[k], rows, pl.ds(start, width)]
        return here, grad_recv.at[phase, k, number, c]

    def hop(role, phase, part, c):
        def build(k):
            src, raw, _, _ = phases[phase]
            start, width = span_of(phase, c)
            rows, number = rows_of(phase, k, part)
            there = pl.ds(pl.multiple_of(peers[k] * cols + start, 128), width)
            return remote(
                src.at[rows, there], raw.at[me, rows, pl.ds(start, width)],
                hop_send.at[phase, k, 0 if k in FAR else SETS[part], c],
                grad_recv.at[phase, k, number, c], peers[k], mine)

        for k in FAR if part == "own" else NEAR:
            begin(role, functools.partial(build, k))

    def first(role, phase, c):
        if role == "end":
            hop(role, phase, "a", c)
        else:
            hop(role, phase, "own", c)
            hop(role, phase, "c", c)

    def second(role, phase, c):
        hop(role, phase, "b", c)

    def relay(role, phase, c):
        def build(k, part, to, slot):
            here, recv = place(phase, k, part, c)
            return remote(here, here, pass_send.at[phase, slot, c], recv, me, to)

        if role == "end":
            for n, k in enumerate(NEAR):
                arrived(*place(phase, k, "a", c))
                begin(role, functools.partial(build, k, "a", partner, n))
        else:
            for n, k in enumerate(FAR):
                arrived(*place(phase, k, "own", c))
                for m, to in enumerate(far_planes):
                    begin(role, functools.partial(build, k, "own", to, 4 + 3 * n + m))
            for n, k in enumerate(NEAR):
                arrived(*place(phase, k, "c", c))
                begin(role, functools.partial(build, k, "c", partner, n))

    def rest(role, phase, c):
        for k in NEAR:
            arrived(*place(phase, k, "b", c))
        for k in NEAR:
            arrived(*place(phase, k, "c" if role == "end" else "a", c))
        for k in FAR:
            for part in ("a", "b") if role == "end" else ("other",):
                arrived(*place(phase, k, part, c))

    def side(phase):
        src, raw, _, _ = phases[phase]
        there = pl.ds(pl.multiple_of(peers[1] * cols, 128), cols)
        begin("all", lambda: remote(
            src.at[:, there], raw.at[me], side_send.at[phase], side_recv.at[phase], peers[1], mine))

    def finish_side(phase):
        arrived(phases[phase][1].at[peers[1]], side_recv.at[phase])

    def act_copy(phase, src, dst, slot, recv_slot, k):
        return remote(src, dst, act_send.at[phase, slot], act_recv.at[phase, recv_slot], peers[k], mine)

    def send_acts(phase):
        src, raw = ((act_in, act_raw), (query_act, qact_raw))[phase]
        for k in (2, 4, 1):
            begin("all", functools.partial(act_copy, phase, src, raw.at[me], k, k, k))

    def half_rows(raw, n):
        size = raw.shape[1] // 2
        return pl.ds(n * size, size)

    def pass_acts(phase):
        raw = (act_raw, qact_raw)[phase]
        for n, (k, onward) in enumerate(((2, 4), (4, 2))):
            whole = raw.at[peers[k]]
            arrived(whole, act_recv.at[phase, k])
            part = raw.at[peers[k], half_rows(raw, n), :]
            begin("all", functools.partial(act_copy, phase, part, part, 6 + n, 6 + n, onward))
        for k in (2, 4):
            whole = raw.at[peers[k]]
            begin("all", functools.partial(act_copy, phase, whole, whole, k + 1, k + 1, 1))

    def finish_acts(phase):
        raw = (act_raw, qact_raw)[phase]
        for n in range(2):
            part = raw.at[peers[6], half_rows(raw, n), :]
            arrived(part, act_recv.at[phase, 6 + n])
            begin("all", functools.partial(act_copy, phase, part, part, 8 + n, 8 + n, 1))
        for k in (1, 3, 5):
            arrived(raw.at[peers[k]], act_recv.at[phase, k])
        for n in range(2):
            arrived(raw.at[peers[7], half_rows(raw, n), :], act_recv.at[phase, 8 + n])

    limits = [lengths[s] for s in range(seq_count)]
    counted = limits[0]
    for s in range(1, seq_count):
        counted = counted + limits[s]
    inverse = 1.0 / jnp.full((1, tile), counted.astype(jnp.float32), jnp.float32)

    def turn_acts():
        @pl.loop(0, dp_count)
        def _(e):
            where_tok = e * tok_dev + lax.broadcasted_iota(jnp.int32, (block, tok_dev), 1)
            live = jnp.zeros((block, tok_dev), jnp.float32)
            for s in range(seq_count):
                inside = (where_tok >= s * seq_len) & (where_tok < s * seq_len + limits[s])
                live = jnp.where(inside, 1.0, live)
            to = pl.ds(pl.multiple_of(e * tok_dev, 128), tok_dev)
            for b in range(act_width // block):
                span = pl.ds(b * block, block)
                turned = lax.dot_general(
                    act_basis[span, :].T, act_raw[e, :, span], (((1,), (1,)), ((), ())),
                    preferred_element_type=jnp.float32)
                kept = (turned * live).astype(jnp.bfloat16)
                act_t[span, to] = kept
                act_sq[span, to] = kept * kept

    def turn_query_acts():
        @pl.loop(0, dp_count)
        def _(e):
            for b in range(act_width // block):
                span = pl.ds(b * block, block)
                turned = jnp.dot(qact_raw[e, :, span], act_basis[span, :], preferred_element_type=jnp.float32)
                q_rot[pl.ds(pl.multiple_of(e * q_dev, 16), q_dev), span] = turned.astype(jnp.bfloat16)

    def wide_basis(jt):
        rows = []
        count = tile // block
        zero = jnp.zeros((block, block), jnp.bfloat16)
        for h in range(count):
            piece = grad_basis[pl.ds(pl.multiple_of(jt * tile + h * block, 128), block), :]
            rows.append(jnp.concatenate([piece if g == h else zero for g in range(count)], axis=1))
        return jnp.concatenate(rows, axis=0)

    def turned_grads(raw, jt, rows):
        span = pl.ds(pl.multiple_of(jt * tile, 128), tile)
        whole = raw[:, :, span].reshape(rows, tile)
        return jnp.dot(whole, wide_basis(jt), preferred_element_type=jnp.float32).astype(jnp.bfloat16)

    def train_tile(jt):
        grads = turned_grads(grad_raw, jt, tokens)
        total = jnp.dot(act_sq[...], grads * grads, preferred_element_type=jnp.float32) * inverse
        moments[:, pl.ds(pl.multiple_of(jt * tile, 128), tile)] = total
        weights = 1.0 / (total + damping)
        for s in range(seq_count):
            a = act_t[:, s * seq_len:(s + 1) * seq_len]
            g = grads[s * seq_len:(s + 1) * seq_len, :]
            precond[s, jt] = (weights * jnp.dot(a, g, preferred_element_type=jnp.float32)).astype(jnp.bfloat16)

    def query_tile(jt):
        grads = turned_grads(qgrad_raw, jt, q_rows).astype(jnp.float32)
        for s in range(seq_count):
            mapped = jnp.dot(q_rot[...], precond[s, jt], preferred_element_type=jnp.float32) * grads
            folded = mapped[:, :128]
            for h in range(1, tile // 128):
                folded = folded + mapped[:, h * 128:(h + 1) * 128]
            totals[s] += folded.reshape(QUERIES, q_rows // QUERIES // 8, 8, 128).sum(axis=1)

    def opening(role):
        first(role, 0, 0)
        first(role, 0, 1)

    def early(role):
        second(role, 0, 0)
        first(role, 0, 2)

    def middle(role):
        first(role, 0, 3)
        second(role, 0, 1)
        first(role, 1, 0)
        second(role, 0, 2)

    def later(role):
        second(role, 0, 3)
        first(role, 1, 1)

    def closing(role):
        second(role, 1, 0)
        first(role, 1, 2)
        second(role, 1, 1)
        first(role, 1, 3)
        second(role, 1, 2)
        second(role, 1, 3)

    by_role(opening)
    send_acts(0)
    by_role(early)
    side(0)
    by_role(lambda role: relay(role, 0, 0))
    by_role(lambda role: relay(role, 0, 1))
    pass_acts(0)
    by_role(middle)
    send_acts(1)
    by_role(later)
    side(1)
    for copy in locals_in:
        copy.wait()
    by_role(lambda role: relay(role, 0, 2))
    finish_acts(0)
    turn_acts()
    totals[...] = jnp.zeros_like(totals)

    def train_chunk(c):
        by_role(lambda role: rest(role, 0, c))
        pl.loop(TCUTS[c], TCUTS[c + 1])(train_tile)

    finish_side(0)
    train_chunk(0)
    by_role(lambda role: relay(role, 0, 3))
    train_chunk(1)
    by_role(lambda role: relay(role, 1, 0))
    train_chunk(2)
    pass_acts(1)
    by_role(closing)
    train_chunk(3)
    by_role(lambda role: relay(role, 1, 1))
    finish_acts(1)
    turn_query_acts()
    finish_side(1)

    by_role(lambda role: rest(role, 1, 0))
    query_tile(0)
    by_role(lambda role: relay(role, 1, 2))
    query_tile(1)
    by_role(lambda role: rest(role, 1, 1))
    query_tile(2)
    query_tile(3)
    by_role(lambda role: relay(role, 1, 3))
    by_role(lambda role: rest(role, 1, 2))
    pl.loop(4, 6)(query_tile)
    by_role(lambda role: rest(role, 1, 3))
    pl.loop(6, 8)(query_tile)

    lane = lax.broadcasted_iota(jnp.int32, (QUERIES, 128), 1)
    answer = jnp.zeros((QUERIES, 128), jnp.float32)
    for s in range(seq_count):
        row = jnp.sum(jnp.sum(totals[s], axis=1), axis=1, keepdims=True)
        answer = jnp.where(lane == s, row, answer)
    lens = jnp.ones((QUERIES, 128), jnp.float32)
    for s in range(seq_count):
        lens = jnp.where(lane == s, limits[s].astype(jnp.float32), lens)
    shares[me] = across(answer * lax.rsqrt(lens) / math.sqrt(QUERY_LEN * D * FF))

    for k in masks:
        begin("all", functools.partial(
            remote, shares.at[me], shares.at[me], share_send.at[k], share_recv.at[k], peers[k], mine))
    for k in masks:
        arrived(shares.at[peers[k]], share_recv.at[k])
    summed = shares[0]
    for e in range(1, dp_count):
        summed = summed + shares[e]
    crossing[mine] = summed
    for step, other in enumerate(others):
        begin("all", functools.partial(
            remote, crossing.at[mine], crossing.at[mine], cross_send.at[step], cross_recv.at[step], me, other))
    for step in range(mp_count - 1):
        owner = lax.rem(mine + (mp_count - 1 - step), mp_count)
        arrived(crossing.at[owner], cross_recv.at[step])
    summed = crossing[0]
    for e in range(1, mp_count):
        summed = summed + crossing[e]
    partial[...] = summed

    def ended(role):
        for build in started[role]:
            build().wait_send()

    by_role(ended)
    ended("all")


def routed(act_in, grad_in, query_act, query_grad, act_basis, grad_basis, seq_lengths):
    dp_count = lax.axis_size("dp")
    mp_count = lax.axis_size("mp")
    tok_dev, act_width = act_in.shape
    q_dev = query_act.shape[0]
    cols = grad_in.shape[1] // dp_count
    seq_count = seq_lengths.shape[0]
    tokens, q_rows = tok_dev * dp_count, q_dev * dp_count
    tiles = TCUTS[-1]
    tile = cols // tiles
    dma = pltpu.SemaphoreType.DMA
    any_space = pl.BlockSpec(memory_space=pl.ANY)
    bf16 = jnp.bfloat16
    chunks = max(len(TCUTS), len(QCUTS)) - 1
    return pl.pallas_call(
        routed_kernel,
        out_shape=(
            pltpu.VMEM((act_width, cols), jnp.float32),
            pltpu.VMEM((8, 128), jnp.float32),
        ),
        in_specs=[pl.BlockSpec(memory_space=pltpu.SMEM)] + [any_space] * 6,
        out_specs=(pl.BlockSpec(memory_space=pltpu.VMEM), pl.BlockSpec(memory_space=pltpu.VMEM)),
        scratch_shapes=[
            pltpu.VMEM((dp_count, tok_dev, act_width), bf16),
            pltpu.VMEM((dp_count, q_dev, act_width), bf16),
            pltpu.VMEM((dp_count, tok_dev, cols), bf16),
            pltpu.VMEM((dp_count, q_dev, cols), bf16),
            pltpu.VMEM(act_basis.shape, bf16),
            pltpu.VMEM((cols, grad_basis.shape[1]), bf16),
            pltpu.VMEM((act_width, tokens), bf16),
            pltpu.VMEM((act_width, tokens), bf16),
            pltpu.VMEM((q_rows, act_width), bf16),
            pltpu.VMEM((seq_count, tiles, act_width, tile), bf16),
            pltpu.VMEM((seq_count, QUERIES, 8, 128), jnp.float32),
            pltpu.VMEM((dp_count, 8, 128), jnp.float32),
            pltpu.VMEM((mp_count, 8, 128), jnp.float32),
            dma((2, 10)), dma((2, 10)),
            dma((2, dp_count, 3, chunks)), dma((2, 10, chunks)), dma((2, dp_count, 3, chunks)),
            dma((2,)), dma((2,)), dma((6,)),
            dma((dp_count,)), dma((dp_count,)), dma((mp_count - 1,)), dma((mp_count - 1,)),
        ],
        compiler_params=pltpu.CompilerParams(
            collective_id=1, has_side_effects=True, vmem_limit_bytes=54 * 1024 * 1024),
    )(seq_lengths, act_in, grad_in, query_act, query_grad, act_basis, grad_basis)


def local(act_in, grad_in, query_act, query_grad, act_basis, grad_basis, seq_lengths):
    dp_count = lax.axis_size("dp")
    mp_count = lax.axis_size("mp")
    tok_dev, act_width = act_in.shape
    q_dev = query_act.shape[0]
    cols = grad_in.shape[1] // dp_count
    seq_count = seq_lengths.shape[0]
    tokens, q_rows = tok_dev * dp_count, q_dev * dp_count
    if dp_count == 8 and mp_count == 4 and tok_dev % 128 == 0 and q_dev % 128 == 0 and cols % 2048 == 0:
        moments, scores = store(*routed(
            act_in, grad_in, query_act, query_grad, act_basis, grad_basis, seq_lengths), seq_count)
        return moments, scores.T
    tile = min(256, cols)
    tiles = cols // tile
    chunks = min(4, tiles)
    far = [k for k in range(1, dp_count) if bin(k >> 1).count("1") >= 2]
    shared_train = far if tok_dev % (16 * mp_count) == 0 and dp_count <= 2 * tiles else []
    shared_query = far if q_dev % (16 * mp_count) == 0 and dp_count <= 2 * tiles else []
    steps = max(1, mp_count - 1)
    dma = pltpu.SemaphoreType.DMA
    any_space = pl.BlockSpec(memory_space=pl.ANY)
    bf16 = jnp.bfloat16
    raw, scores = pl.pallas_call(
        functools.partial(kernel, dp_count, mp_count, chunks, shared_train, shared_query),
        out_shape=(
            pltpu.VMEM((act_width, cols), jnp.float32),
            pltpu.VMEM((8, 128), jnp.float32),
        ),
        in_specs=[pl.BlockSpec(memory_space=pltpu.SMEM)] + [any_space] * 6,
        out_specs=(pl.BlockSpec(memory_space=pltpu.VMEM), pl.BlockSpec(memory_space=pltpu.VMEM)),
        scratch_shapes=[
            pltpu.VMEM((dp_count, tok_dev, act_width), bf16),
            pltpu.VMEM((dp_count, q_dev, act_width), bf16),
            pltpu.VMEM((dp_count, tok_dev, cols), bf16),
            pltpu.VMEM((dp_count, q_dev, cols), bf16),
            pltpu.VMEM(act_basis.shape, bf16),
            pltpu.VMEM(grad_basis.shape, bf16),
            pltpu.VMEM((act_width, tokens), bf16),
            pltpu.VMEM((q_rows, act_width), bf16),
            pltpu.VMEM((seq_count, tiles, act_width, tile), bf16),
            pltpu.VMEM((tiles, 8, tile), jnp.float32),
            pltpu.VMEM((seq_count, QUERIES, 8, 128), jnp.float32),
            dma((dp_count,)), dma((dp_count,)), dma((dp_count,)), dma((dp_count,)),
            dma((1, dp_count)), dma((1, dp_count)), dma((chunks, dp_count)), dma((chunks, dp_count)),
            dma((max(1, len(shared_train)), steps)), dma((max(1, len(shared_train)), steps)),
            dma((max(1, len(shared_query)), steps)), dma((max(1, len(shared_query)), steps)),
            dma((6,)), dma((tiles,)),
            pltpu.VMEM((dp_count, QUERIES, 128), jnp.float32),
            pltpu.VMEM((mp_count, QUERIES, 128), jnp.float32),
            dma((dp_count,)), dma((dp_count,)), dma((steps,)), dma((steps,)),
        ],
        compiler_params=pltpu.CompilerParams(
            collective_id=0, has_side_effects=True, vmem_limit_bytes=54 * 1024 * 1024),
    )(seq_lengths, act_in, grad_in, query_act, query_grad, act_basis, grad_basis)
    moments, scores = store(raw, scores, seq_count)
    return moments, scores.T


def store_kernel(raw, scores_in, moments, scores, sems):
    n = sems.shape[0]
    rows = raw.shape[0] // n
    copies = [pltpu.make_async_copy(raw.at[pl.ds(i * rows, rows)], moments.at[pl.ds(i * rows, rows)], sems.at[i])
              for i in range(n)]
    for c in copies:
        c.start()
    scores[...] = scores_in[:scores.shape[0], :scores.shape[1]]
    for c in copies:
        c.wait()


def store(raw, scores, seq_count):
    n = 8
    vm = pl.BlockSpec(memory_space=pltpu.VMEM)
    return pl.pallas_call(
        store_kernel,
        out_shape=(jax.ShapeDtypeStruct(raw.shape, raw.dtype), jax.ShapeDtypeStruct((seq_count, QUERIES), scores.dtype)),
        in_specs=[vm, vm], out_specs=(pl.BlockSpec(memory_space=pltpu.HBM), vm),
        scratch_shapes=[pltpu.SemaphoreType.DMA((n,))],
        compiler_params=pltpu.CompilerParams(vmem_limit_bytes=1024*1024),
    )(pltpu.with_memory_space_constraint(raw, pltpu.VMEM), pltpu.with_memory_space_constraint(scores, pltpu.VMEM))


def solution(mesh):
    return jax.shard_map(
        local,
        mesh=mesh,
        in_specs=(
            P("dp", "mp"),
            P("dp", None),
            P("dp", "mp"),
            P("dp", None),
            P("mp", None),
            P("dp", None),
            P(),
        ),
        out_specs=(P("mp", "dp"), P()),
        check_vma=False,
    )
```

```python
import functools
import math

import jax
import jax.numpy as jnp
from jax import lax
from jax.experimental import pallas as pl
from jax.experimental.pallas import tpu as pltpu
from jax.sharding import PartitionSpec as P

D = 4096
FF = 16384
QUERIES = 64
QUERY_LEN = 16

damping = 0.1
MESH = pl.DeviceIdType.MESH


def flipped(index, mask):
    bit = 1
    while bit <= mask:
        if mask & bit:
            index = index + bit * (1 - 2 * ((index // bit) % 2))
        bit *= 2
    return index


def across(columns):
    square = jnp.concatenate([columns, jnp.zeros((128 - columns.shape[0], 128), jnp.float32)], axis=0)
    return square.T[:8, :]


def kernel(
    dp_count, mp_count, chunks, shared_train, shared_query,
    lengths, act_in, grad_in, query_act, query_grad, act_basis_in, grad_basis_in,
    moments, partial,
    act_raw, qact_raw, grad_raw, qgrad_raw, act_basis, grad_basis,
    act_t, q_rot, precond, staged, totals,
    act_send, act_recv, qact_send, qact_recv, grad_send, grad_recv, qgrad_send, qgrad_recv,
    pass_send, pass_recv, qpass_send, qpass_recv, local_sem, out_sem,
    shares, crossing, share_send, share_recv, cross_send, cross_recv,
):
    me = lax.axis_index("dp")
    mine = lax.axis_index("mp")
    seq_count = lengths.shape[0]
    tok_dev, act_width = act_in.shape
    q_dev = query_act.shape[0]
    cols = grad_raw.shape[2]
    block = act_basis_in.shape[1]
    tiles, _, tile = staged.shape
    tokens = tok_dev * dp_count
    seq_len = tokens // seq_count
    q_rows = q_dev * dp_count
    chunk_cols = cols // chunks
    masks = list(range(1, dp_count))
    peers = {k: flipped(me, k) for k in masks}

    barrier = pltpu.get_barrier_semaphore()
    for k in masks:
        pl.semaphore_signal(barrier, inc=1, device_id={"dp": peers[k], "mp": mine}, device_id_type=MESH)
    others = [lax.rem(mine + step, mp_count) for step in range(1, mp_count)]
    for other in others:
        pl.semaphore_signal(barrier, inc=1, device_id={"dp": me, "mp": other}, device_id_type=MESH)

    locals_in = [
        pltpu.make_async_copy(act_in, act_raw.at[me], local_sem.at[0]),
        pltpu.make_async_copy(act_basis_in, act_basis, local_sem.at[1]),
        pltpu.make_async_copy(grad_basis_in, grad_basis, local_sem.at[2]),
        pltpu.make_async_copy(
            grad_in.at[:, pl.ds(pl.multiple_of(me * cols, 128), cols)], grad_raw.at[me], local_sem.at[3]),
        pltpu.make_async_copy(query_act, qact_raw.at[me], local_sem.at[4]),
        pltpu.make_async_copy(
            query_grad.at[:, pl.ds(pl.multiple_of(me * cols, 128), cols)], qgrad_raw.at[me], local_sem.at[5]),
    ]
    for copy in locals_in:
        copy.start()
    pl.semaphore_wait(barrier, len(masks) + len(others))

    def remote(src, dst, send, recv, dp, mp):
        return pltpu.make_async_remote_copy(
            src_ref=src, dst_ref=dst, send_sem=send, recv_sem=recv,
            device_id={"dp": dp, "mp": mp}, device_id_type=MESH)

    sends = []

    def begin(copy):
        copy.start()
        sends.append(copy)

    act_masks = [k for k in masks if k == 1 or k % 2 == 0]

    def send_acts(src, raw, send, recv):
        for k in reversed(act_masks):
            begin(remote(src, raw.at[me], send.at[k], recv.at[k], peers[k], mine))

    def part_of(owner, rows):
        return pl.ds(pl.multiple_of(owner * (rows // mp_count), 16), rows // mp_count)

    def send_shared(src, raw, send, recv, shared):
        rows = part_of(mine, src.shape[0])
        for k in reversed(shared):
            there = pl.ds(pl.multiple_of(peers[k] * cols, 128), cols)
            begin(remote(
                src.at[rows, there], raw.at[me, rows, :], send.at[0, k], recv.at[0, k], peers[k], mine))

    def send_grads(src, raw, send, recv, shared, start, width, slot):
        for k in reversed(masks):
            if k not in shared:
                there = pl.ds(pl.multiple_of(peers[k] * cols + start, 128), width)
                begin(remote(
                    src.at[:, there], raw.at[me, :, pl.ds(start, width)],
                    send.at[slot, k], recv.at[slot, k], peers[k], mine))

    send_acts(act_in, act_raw, act_send, act_recv)
    send_shared(grad_in, grad_raw, grad_send, grad_recv, shared_train)
    send_shared(query_grad, qgrad_raw, qgrad_send, qgrad_recv, shared_query)
    send_grads(grad_in, grad_raw, grad_send, grad_recv, shared_train, 0, cols, 0)
    send_acts(query_act, qact_raw, qact_send, qact_recv)
    for c in range(chunks):
        send_grads(query_grad, qgrad_raw, qgrad_send, qgrad_recv, shared_query, c * chunk_cols, chunk_cols, c)

    def arrived(ref, send, recv):
        remote(ref, ref, send, recv, peers[1], mine).wait_recv()

    def relay_acts(raw, send, recv):
        for k in reversed(act_masks):
            arrived(raw.at[peers[k]], send.at[k], recv.at[k])
            if k > 1:
                here = raw.at[peers[k]]
                begin(remote(here, here, send.at[k + 1], recv.at[k + 1], peers[1], mine))

    def finish_acts(raw, send, recv):
        for k in masks:
            if k not in act_masks:
                arrived(raw.at[peers[k]], send.at[k], recv.at[k])

    def relay_grads(raw, send, recv, fsend, frecv, shared):
        for n, k in enumerate(reversed(shared)):
            here = raw.at[peers[k], part_of(mine, raw.shape[1]), :]
            arrived(here, send.at[0, k], recv.at[0, k])
            for step, other in enumerate(others):
                begin(remote(here, here, fsend.at[n, step], frecv.at[n, step], me, other))

    def finish_grads(raw, send, recv, shared, start, width, slot):
        for k in reversed(masks):
            if k not in shared:
                arrived(raw.at[peers[k], :, pl.ds(start, width)], send.at[slot, k], recv.at[slot, k])

    def finish_shared(raw, fsend, frecv, shared):
        for n, k in enumerate(reversed(shared)):
            for step in range(mp_count - 1):
                owner = lax.rem(mine + (mp_count - 1 - step), mp_count)
                arrived(
                    raw.at[peers[k], part_of(owner, raw.shape[1]), :], fsend.at[n, step], frecv.at[n, step])

    relay_acts(act_raw, act_send, act_recv)
    finish_acts(act_raw, act_send, act_recv)
    relay_grads(grad_raw, grad_send, grad_recv, pass_send, pass_recv, shared_train)
    relay_grads(qgrad_raw, qgrad_send, qgrad_recv, qpass_send, qpass_recv, shared_query)
    for copy in locals_in:
        copy.wait()

    limits = [lengths[s] for s in range(seq_count)]
    counted = limits[0]
    for s in range(1, seq_count):
        counted = counted + limits[s]
    inverse = 1.0 / jnp.full((1, tile), counted.astype(jnp.float32), jnp.float32)

    @pl.loop(0, dp_count)
    def _(e):
        where_tok = e * tok_dev + lax.broadcasted_iota(jnp.int32, (block, tok_dev), 1)
        live = jnp.zeros((block, tok_dev), jnp.float32)
        for s in range(seq_count):
            inside = (where_tok >= s * seq_len) & (where_tok < s * seq_len + limits[s])
            live = jnp.where(inside, 1.0, live)
        for b in range(act_width // block):
            span = pl.ds(b * block, block)
            turned = lax.dot_general(
                act_basis[span, :].T, act_raw[e, :, span], (((1,), (1,)), ((), ())),
                preferred_element_type=jnp.float32)
            act_t[span, pl.ds(pl.multiple_of(e * tok_dev, 128), tok_dev)] = (turned * live).astype(jnp.bfloat16)

    def wide_basis(jt):
        first = grad_basis[pl.ds(pl.multiple_of(jt * tile, 128), block), :]
        rows = []
        count = tile // block
        zero = jnp.zeros_like(first)
        for h in range(count):
            own = grad_basis[pl.ds(pl.multiple_of(jt * tile + h * block, 128), block), :]
            rows.append(jnp.concatenate([own if g == h else zero for g in range(count)], axis=1))
        return jnp.concatenate(rows, axis=0)

    def turned_grads(raw, jt, rows):
        span = pl.ds(pl.multiple_of(jt * tile, 128), tile)
        whole = raw[:, :, span].reshape(rows, tile)
        return jnp.dot(whole, wide_basis(jt), preferred_element_type=jnp.float32).astype(jnp.bfloat16)

    finish_shared(grad_raw, pass_send, pass_recv, shared_train)
    finish_grads(grad_raw, grad_send, grad_recv, shared_train, 0, cols, 0)

    def out_copy(jt):
        span = pl.ds(pl.multiple_of(jt * tile, 128), tile)
        return pltpu.make_async_copy(staged.at[jt], moments.at[:, span], out_sem.at[jt])

    per_chunk = tiles // chunks

    def first_phase(jt):
        grads = turned_grads(grad_raw, jt, tokens)
        total = jnp.zeros((act_width, tile), jnp.float32)
        for s in range(seq_count):
            a = act_t[:, s * seq_len:(s + 1) * seq_len]
            g = grads[s * seq_len:(s + 1) * seq_len, :]
            total = total + jnp.dot(a * a, g * g, preferred_element_type=jnp.float32)
        total = total * inverse
        moments[:, pl.ds(pl.multiple_of(jt * tile, 128), tile)] = total
        weights = 1.0 / (total + damping)
        for s in range(seq_count):
            a = act_t[:, s * seq_len:(s + 1) * seq_len]
            g = grads[s * seq_len:(s + 1) * seq_len, :]
            precond[s, jt] = (weights * jnp.dot(a, g, preferred_element_type=jnp.float32)).astype(jnp.bfloat16)

    half = tiles // 2
    pl.loop(0, half)(first_phase)
    relay_acts(qact_raw, qact_send, qact_recv)
    pl.loop(half, tiles)(first_phase)
    finish_acts(qact_raw, qact_send, qact_recv)

    @pl.loop(0, dp_count)
    def _(e):
        for b in range(act_width // block):
            span = pl.ds(b * block, block)
            turned = jnp.dot(qact_raw[e, :, span], act_basis[span, :], preferred_element_type=jnp.float32)
            q_rot[pl.ds(pl.multiple_of(e * q_dev, 16), q_dev), span] = turned.astype(jnp.bfloat16)

    totals[...] = jnp.zeros_like(totals)
    finish_shared(qgrad_raw, qpass_send, qpass_recv, shared_query)

    def second_phase(jt):
        grads = turned_grads(qgrad_raw, jt, q_rows).astype(jnp.float32)
        for s in range(seq_count):
            mapped = jnp.dot(q_rot[...], precond[s, jt], preferred_element_type=jnp.float32) * grads
            folded = mapped[:, :128]
            for h in range(1, tile // 128):
                folded = folded + mapped[:, h * 128:(h + 1) * 128]
            totals[s] += folded.reshape(QUERIES, q_rows // QUERIES // 8, 8, 128).sum(axis=1)

    for c in range(chunks):
        finish_grads(qgrad_raw, qgrad_send, qgrad_recv, shared_query, c * chunk_cols, chunk_cols, c)
        pl.loop(c * per_chunk, (c + 1) * per_chunk)(second_phase)

    lane = lax.broadcasted_iota(jnp.int32, (QUERIES, 128), 1)
    answer = jnp.zeros((QUERIES, 128), jnp.float32)
    for s in range(seq_count):
        row = jnp.sum(jnp.sum(totals[s], axis=1), axis=1, keepdims=True)
        answer = jnp.where(lane == s, row, answer)
    lens = jnp.ones((QUERIES, 128), jnp.float32)
    for s in range(seq_count):
        lens = jnp.where(lane == s, limits[s].astype(jnp.float32), lens)
    shares[me] = answer * lax.rsqrt(lens) / math.sqrt(QUERY_LEN * D * FF)

    for copy in sends:
        copy.wait_send()
    sends.clear()

    for k in masks:
        begin(remote(shares.at[me], shares.at[me], share_send.at[k], share_recv.at[k], peers[k], mine))
    for k in masks:
        arrived(shares.at[peers[k]], share_send.at[k], share_recv.at[k])
    summed = shares[0]
    for e in range(1, dp_count):
        summed = summed + shares[e]
    crossing[mine] = summed
    for step, other in enumerate(others):
        begin(remote(
            crossing.at[mine], crossing.at[mine], cross_send.at[step], cross_recv.at[step], me, other))
    for step in range(mp_count - 1):
        owner = lax.rem(mine + (mp_count - 1 - step), mp_count)
        arrived(crossing.at[owner], cross_send.at[step], cross_recv.at[step])
    summed = crossing[0]
    for e in range(1, mp_count):
        summed = summed + crossing[e]
    partial[...] = across(summed)
    for copy in sends:
        copy.wait_send()


NEAR = (2, 4, 3, 5)
FAR = (6, 7)
TRAIN_CUTS = (0, 2, 4, 6, 8)
QUERY_CUTS = (0, 2, 4, 6, 7, 8)
TRAIN_SPLITS = ((5, 7), (5, 7), (5, 7), (5, 7))
QUERY_SPLITS = ((5, 7), (5, 7), (5, 7), (4, 7), (4, 7))


def routed_kernel(
    lengths, act_in, grad_in, query_act, query_grad, act_basis_in, grad_basis_in,
    moments, partial,
    act_raw, qact_raw, grad_raw, qgrad_raw, act_basis, grad_basis,
    act_t, act_sq, q_rot, precond, totals, shares,
    act_send, act_recv, grad_send, lead_recv, rest_recv, side_send, side_recv, local_sem,
    share_send, share_recv, ready,
):
    me = lax.axis_index("dp")
    mine = lax.axis_index("mp")
    dp_count = lax.axis_size("dp")
    mp_count = lax.axis_size("mp")
    tok_dev, act_width = act_in.shape
    seq_count = lengths.shape[0]
    q_dev = query_act.shape[0]
    cols = grad_raw.shape[1]
    block = act_basis.shape[1]
    tiles, tile = precond.shape[1], precond.shape[3]
    tokens = tok_dev * dp_count
    seq_len = tokens // seq_count
    q_rows = q_dev * dp_count
    masks = list(range(1, dp_count))
    peers = {k: flipped(me, k) for k in masks}
    others = [lax.rem(mine + step, mp_count) for step in range(1, mp_count)]

    is_end = (mine == 0) | (mine == mp_count - 1)
    is_mid = jnp.logical_not(is_end)
    partner = flipped(mine, 1)
    half = lax.rem(mine + 1, 2)
    far_planes = [partner, mp_count - 1 - mine, mp_count - 1 - partner]

    barrier = pltpu.get_barrier_semaphore()
    for k in masks:
        pl.semaphore_signal(barrier, inc=1, device_id={"dp": peers[k], "mp": mine}, device_id_type=MESH)
    for other in others:
        pl.semaphore_signal(barrier, inc=1, device_id={"dp": me, "mp": other}, device_id_type=MESH)

    own = pl.ds(pl.multiple_of(me * cols, 128), cols)
    own_tok = pl.ds(pl.multiple_of(me * tok_dev, 128), tok_dev)
    own_q = pl.ds(pl.multiple_of(me * q_dev, 128), q_dev)
    locals_in = [
        pltpu.make_async_copy(act_in, act_raw.at[own_tok], local_sem.at[0]),
        pltpu.make_async_copy(act_basis_in, act_basis, local_sem.at[1]),
        pltpu.make_async_copy(grad_basis_in, grad_basis, local_sem.at[2]),
        pltpu.make_async_copy(grad_in.at[:, own], grad_raw.at[own_tok], local_sem.at[3]),
        pltpu.make_async_copy(query_act, qact_raw.at[own_q], local_sem.at[4]),
        pltpu.make_async_copy(query_grad.at[:, own], qgrad_raw.at[own_q], local_sem.at[5]),
    ]
    for copy in locals_in:
        copy.start()
    pl.semaphore_wait(barrier, len(masks) + len(others))

    def remote(src, dst, send, recv, dp, mp):
        return pltpu.make_async_remote_copy(
            src_ref=src, dst_ref=dst, send_sem=send, recv_sem=recv,
            device_id={"dp": dp, "mp": mp}, device_id_type=MESH)

    def arrived(ref, recv):
        remote(ref, ref, side_send.at[0], recv, peers[1], mine).wait_recv()

    def left(ref, send):
        remote(ref, ref, send, side_recv.at[0], peers[1], mine).wait_send()

    def by_role(act):
        @pl.when(is_end)
        def _():
            act("end")

        @pl.when(is_mid)
        def _():
            act("mid")

    phases = (
        (grad_in, grad_raw, tok_dev, TRAIN_CUTS, TRAIN_SPLITS),
        (query_grad, qgrad_raw, q_dev, QUERY_CUTS, QUERY_SPLITS),
    )

    def span_of(phase, c):
        cuts = phases[phase][3]
        return cuts[c] * tile, (cuts[c + 1] - cuts[c]) * tile

    def count_of(phase, part, c):
        first, second = phases[phase][4][c]
        eighth = phases[phase][2] // 8
        return {"a": first, "b": second - first, "c": 8 - second, "own": 4}[part] * eighth

    def rows_of(phase, part, c):
        first, second = phases[phase][4][c]
        eighth = phases[phase][2] // 8
        low = {"a": 0, "b": first, "c": second, "own": half * 4}[part]
        return low * eighth, count_of(phase, part, c)

    def held(phase, k, part, c):
        start, width = span_of(phase, c)
        low, rows = rows_of(phase, part, c)
        here = pl.ds(pl.multiple_of(peers[k] * phases[phase][2] + low, 16), rows)
        return phases[phase][1].at[here, pl.ds(start, width)]

    def bulk(phase, rows, c):
        start, width = span_of(phase, c)
        return phases[phase][1].at[pl.ds(0, rows), pl.ds(start, width)]

    def hop(phase, part, c, ks, recv):
        src, raw, size, _, _ = phases[phase]
        start, width = span_of(phase, c)
        low, rows = rows_of(phase, part, c)
        taken = pl.ds(pl.multiple_of(low, 16), rows)
        put = pl.ds(pl.multiple_of(me * size + low, 16), rows)
        for k in ks:
            there = pl.ds(pl.multiple_of(peers[k] * cols + start, 128), width)
            remote(
                src.at[taken, there], raw.at[put, pl.ds(start, width)],
                grad_send.at[phase, c], recv, peers[k], mine).start()

    def lead(role, phase, c):
        if role == "end":
            hop(phase, "a", c, NEAR[:2], lead_recv.at[phase, c, 0])
            hop(phase, "a", c, NEAR[2:], lead_recv.at[phase, c, 1])
        else:
            hop(phase, "own", c, FAR, lead_recv.at[phase, c, 0])
            hop(phase, "c", c, NEAR, lead_recv.at[phase, c, 1])

    def trail(role, phase, c):
        hop(phase, "b", c, NEAR, rest_recv.at[phase, c])

    def relay(role, phase, c):
        def onward(k, part, to):
            here = held(phase, k, part, c)
            remote(here, here, grad_send.at[phase, c], rest_recv.at[phase, c], me, to).start()

        if role == "end":
            for g, ks in enumerate((NEAR[:2], NEAR[2:])):
                arrived(bulk(phase, 2 * count_of(phase, "a", c), c), lead_recv.at[phase, c, g])
                for k in ks:
                    onward(k, "a", partner)
        else:
            arrived(bulk(phase, 2 * count_of(phase, "own", c), c), lead_recv.at[phase, c, 0])
            for to in far_planes:
                for k in FAR:
                    onward(k, "own", to)
            arrived(bulk(phase, 4 * count_of(phase, "c", c), c), lead_recv.at[phase, c, 1])
            for k in NEAR:
                onward(k, "c", partner)

    def rest(role, phase, c):
        a, b, d, own_half = [count_of(phase, part, c) for part in ("a", "b", "c", "own")]
        rows = 4 * (b + d) + 4 * own_half if role == "end" else 4 * (a + b) + 2 * own_half
        arrived(bulk(phase, rows, c), rest_recv.at[phase, c])

    def gone(role, phase):
        for c in range(len(phases[phase][4])):
            a, b, d, own_half = [count_of(phase, part, c) for part in ("a", "b", "c", "own")]
            rows = 4 * (a + b) + 4 * a if role == "end" else 4 * (b + d) + 2 * own_half + 6 * own_half + 4 * d
            left(bulk(phase, rows, c), grad_send.at[phase, c])

    def side(phase):
        src, raw, size, _, _ = phases[phase]
        there = pl.ds(pl.multiple_of(peers[1] * cols, 128), cols)
        put = pl.ds(pl.multiple_of(me * size, 128), size)
        remote(src.at[:, there], raw.at[put], side_send.at[phase], side_recv.at[phase], peers[1], mine).start()

    def finish_side(phase):
        arrived(phases[phase][1].at[pl.ds(0, phases[phase][2])], side_recv.at[phase])

    acts = ((act_in, act_raw, tok_dev), (query_act, qact_raw, q_dev))

    def act_rows(phase, k, low, rows):
        size = acts[phase][2]
        return acts[phase][1].at[pl.ds(pl.multiple_of(peers[k] * size + low, 16), rows)]

    def act_go(phase, src, dst, recv_slot, k):
        remote(src, dst, act_send.at[phase], act_recv.at[phase, recv_slot], peers[k], mine).start()

    def send_acts(phase):
        src, raw, size = acts[phase]
        put = raw.at[pl.ds(pl.multiple_of(me * size, 16), size)]
        for k, slot in ((2, 0), (4, 1), (1, 3)):
            act_go(phase, src, put, slot, k)

    def pass_acts(phase):
        _, raw, size = acts[phase]
        for n, (k, onward) in enumerate(((2, 4), (4, 2))):
            arrived(raw.at[pl.ds(0, size)], act_recv.at[phase, n])
            part = act_rows(phase, k, n * (size // 2), size // 2)
            act_go(phase, part, part, 2, onward)
        for k in (2, 4):
            whole = act_rows(phase, k, 0, size)
            act_go(phase, whole, whole, 3, 1)

    def finish_acts(phase):
        _, raw, size = acts[phase]
        arrived(raw.at[pl.ds(0, size)], act_recv.at[phase, 2])
        whole = act_rows(phase, 6, 0, size)
        act_go(phase, whole, whole, 3, 1)
        arrived(raw.at[pl.ds(0, 4 * size)], act_recv.at[phase, 3])

    def acts_gone(phase):
        _, raw, size = acts[phase]
        left(raw.at[pl.ds(0, 7 * size)], act_send.at[phase])

    for other in others:
        pl.semaphore_signal(ready, inc=1, device_id={"dp": me, "mp": other}, device_id_type=MESH)

    limits = [lengths[s] for s in range(seq_count)]
    counted = limits[0]
    for s in range(1, seq_count):
        counted = counted + limits[s]
    inverse = 1.0 / jnp.full((1, tile), counted.astype(jnp.float32), jnp.float32)

    def turn_acts():
        @pl.loop(0, dp_count)
        def _(e):
            where_tok = e * tok_dev + lax.broadcasted_iota(jnp.int32, (block, tok_dev), 1)
            live = jnp.zeros((block, tok_dev), jnp.float32)
            for s in range(seq_count):
                inside = (where_tok >= s * seq_len) & (where_tok < s * seq_len + limits[s])
                live = jnp.where(inside, 1.0, live)
            to = pl.ds(pl.multiple_of(e * tok_dev, 128), tok_dev)
            for b in range(act_width // block):
                span = pl.ds(b * block, block)
                turned = lax.dot_general(
                    act_basis[span, :].T, act_raw[to, span], (((1,), (1,)), ((), ())),
                    preferred_element_type=jnp.float32)
                kept = (turned * live).astype(jnp.bfloat16)
                act_t[span, to] = kept
                act_sq[span, to] = kept * kept

    def turn_query_acts():
        @pl.loop(0, dp_count)
        def _(e):
            rows = pl.ds(pl.multiple_of(e * q_dev, 16), q_dev)
            for b in range(act_width // block):
                span = pl.ds(b * block, block)
                turned = jnp.dot(qact_raw[rows, span], act_basis[span, :], preferred_element_type=jnp.float32)
                q_rot[rows, span] = turned.astype(jnp.bfloat16)

    def wide_basis(jt):
        rows = []
        count = tile // block
        zero = jnp.zeros((block, block), jnp.bfloat16)
        for h in range(count):
            piece = grad_basis[pl.ds(pl.multiple_of(jt * tile + h * block, 128), block), :]
            rows.append(jnp.concatenate([piece if g == h else zero for g in range(count)], axis=1))
        return jnp.concatenate(rows, axis=0)

    def turned_grads(raw, jt):
        whole = raw[:, pl.ds(pl.multiple_of(jt * tile, 128), tile)]
        return jnp.dot(whole, wide_basis(jt), preferred_element_type=jnp.float32).astype(jnp.bfloat16)

    def train_tile(jt):
        grads = turned_grads(grad_raw, jt)
        total = jnp.dot(act_sq[...], grads * grads, preferred_element_type=jnp.float32) * inverse
        moments[:, pl.ds(pl.multiple_of(jt * tile, 128), tile)] = total
        weights = 1.0 / (total + damping)
        for s in range(seq_count):
            a = act_t[:, s * seq_len:(s + 1) * seq_len]
            g = grads[s * seq_len:(s + 1) * seq_len, :]
            precond[s, jt] = (weights * jnp.dot(a, g, preferred_element_type=jnp.float32)).astype(jnp.bfloat16)

    def query_tile(jt):
        grads = turned_grads(qgrad_raw, jt).astype(jnp.float32)
        for s in range(seq_count):
            mapped = jnp.dot(q_rot[...], precond[s, jt], preferred_element_type=jnp.float32) * grads
            folded = mapped[:, :128]
            for h in range(1, tile // 128):
                folded = folded + mapped[:, h * 128:(h + 1) * 128]
            totals[s] += folded.reshape(QUERIES, q_rows // QUERIES // 8, 8, 128).sum(axis=1)

    def opening(role):
        lead(role, 0, 0)
        lead(role, 0, 1)

    def early(role):
        trail(role, 0, 0)
        lead(role, 0, 2)

    def middle(role):
        lead(role, 0, 3)
        trail(role, 0, 1)
        lead(role, 1, 0)
        trail(role, 0, 2)

    def later(role):
        trail(role, 0, 3)
        lead(role, 1, 1)

    def closing(role):
        trail(role, 1, 0)
        lead(role, 1, 2)
        trail(role, 1, 1)
        lead(role, 1, 3)
        lead(role, 1, 4)
        trail(role, 1, 2)
        trail(role, 1, 3)
        trail(role, 1, 4)

    def relay_at(phase, c):
        by_role(lambda role: relay(role, phase, c))

    def rest_at(phase, c):
        by_role(lambda role: rest(role, phase, c))

    def train_chunk(c):
        rest_at(0, c)
        pl.loop(TRAIN_CUTS[c], TRAIN_CUTS[c + 1])(train_tile)

    by_role(opening)
    send_acts(0)
    by_role(early)
    side(0)
    relay_at(0, 0)
    relay_at(0, 1)
    pass_acts(0)
    by_role(middle)
    send_acts(1)
    by_role(later)
    side(1)
    for copy in locals_in:
        copy.wait()
    relay_at(0, 2)
    finish_acts(0)
    turn_acts()
    totals[...] = jnp.zeros_like(totals)

    finish_side(0)
    train_chunk(0)
    relay_at(0, 3)
    train_chunk(1)
    relay_at(1, 0)
    train_chunk(2)
    pass_acts(1)
    by_role(closing)
    train_chunk(3)
    relay_at(1, 1)
    finish_acts(1)
    turn_query_acts()
    finish_side(1)

    rest_at(1, 0)
    query_tile(0)
    relay_at(1, 2)
    query_tile(1)
    rest_at(1, 1)
    query_tile(2)
    relay_at(1, 3)
    query_tile(3)
    relay_at(1, 4)
    rest_at(1, 2)
    pl.loop(4, 6)(query_tile)
    rest_at(1, 3)
    query_tile(6)
    rest_at(1, 4)
    query_tile(7)

    lane = lax.broadcasted_iota(jnp.int32, (QUERIES, 128), 1)
    answer = jnp.zeros((QUERIES, 128), jnp.float32)
    for s in range(seq_count):
        row = jnp.sum(jnp.sum(totals[s], axis=1), axis=1, keepdims=True)
        answer = jnp.where(lane == s, row, answer)
    lens = jnp.ones((QUERIES, 128), jnp.float32)
    for s in range(seq_count):
        lens = jnp.where(lane == s, limits[s].astype(jnp.float32), lens)
    slot = mine * dp_count + me
    shares[slot] = across(answer * lax.rsqrt(lens) / math.sqrt(QUERY_LEN * D * FF))

    pl.semaphore_wait(ready, len(others))
    mine_there = shares.at[slot]
    for step in reversed(range(mp_count)):
        plane = lax.rem(mine + step, mp_count)
        for k in reversed(range(dp_count)):
            if k or step:
                remote(
                    mine_there, mine_there, share_send.at[0], share_recv.at[0],
                    peers[k] if k else me, plane).start()

    def ended(role):
        gone(role, 0)
        gone(role, 1)

    by_role(ended)
    for phase in range(2):
        acts_gone(phase)
        left(phases[phase][1].at[pl.ds(0, phases[phase][2])], side_send.at[phase])
    every = shares.at[pl.ds(0, dp_count * mp_count - 1)]
    left(every, share_send.at[0])
    arrived(every, share_recv.at[0])
    summed = shares[0]
    for e in range(1, dp_count * mp_count):
        summed = summed + shares[e]
    partial[...] = summed


def routed(act_in, grad_in, query_act, query_grad, act_basis, grad_basis, seq_lengths):
    dp_count = lax.axis_size("dp")
    mp_count = lax.axis_size("mp")
    tok_dev, act_width = act_in.shape
    q_dev = query_act.shape[0]
    cols = grad_in.shape[1] // dp_count
    seq_count = seq_lengths.shape[0]
    tokens, q_rows = tok_dev * dp_count, q_dev * dp_count
    tiles = TRAIN_CUTS[-1]
    tile = cols // tiles
    dma = pltpu.SemaphoreType.DMA
    any_space = pl.BlockSpec(memory_space=pl.ANY)
    bf16 = jnp.bfloat16
    chunks = max(len(TRAIN_SPLITS), len(QUERY_SPLITS))
    return pl.pallas_call(
        routed_kernel,
        out_shape=(
            pltpu.VMEM((act_width, cols), jnp.float32),
            pltpu.VMEM((8, 128), jnp.float32),
        ),
        in_specs=[pl.BlockSpec(memory_space=pltpu.SMEM)] + [any_space] * 6,
        out_specs=(pl.BlockSpec(memory_space=pltpu.VMEM), pl.BlockSpec(memory_space=pltpu.VMEM)),
        scratch_shapes=[
            pltpu.VMEM((tokens, act_width), bf16),
            pltpu.VMEM((q_rows, act_width), bf16),
            pltpu.VMEM((tokens, cols), bf16),
            pltpu.VMEM((q_rows, cols), bf16),
            pltpu.VMEM(act_basis.shape, bf16),
            pltpu.VMEM((cols, grad_basis.shape[1]), bf16),
            pltpu.VMEM((act_width, tokens), bf16),
            pltpu.VMEM((act_width, tokens), bf16),
            pltpu.VMEM((q_rows, act_width), bf16),
            pltpu.VMEM((seq_count, tiles, act_width, tile), bf16),
            pltpu.VMEM((seq_count, QUERIES, 8, 128), jnp.float32),
            pltpu.VMEM((dp_count * mp_count, 8, 128), jnp.float32),
            dma((2,)), dma((2, 4)), dma((2, chunks)), dma((2, chunks, 2)), dma((2, chunks)),
            dma((2,)), dma((2,)), dma((6,)), dma((1,)), dma((1,)), pltpu.SemaphoreType.REGULAR,
        ],
        compiler_params=pltpu.CompilerParams(
            collective_id=1, has_side_effects=True, vmem_limit_bytes=54 * 1024 * 1024),
    )(seq_lengths, act_in, grad_in, query_act, query_grad, act_basis, grad_basis)


def local(act_in, grad_in, query_act, query_grad, act_basis, grad_basis, seq_lengths):
    dp_count = lax.axis_size("dp")
    mp_count = lax.axis_size("mp")
    tok_dev, act_width = act_in.shape
    q_dev = query_act.shape[0]
    cols = grad_in.shape[1] // dp_count
    seq_count = seq_lengths.shape[0]
    tokens, q_rows = tok_dev * dp_count, q_dev * dp_count
    if dp_count == 8 and mp_count == 4 and tok_dev % 128 == 0 and q_dev % 128 == 0 and cols % 2048 == 0:
        moments, scores = store(*routed(
            act_in, grad_in, query_act, query_grad, act_basis, grad_basis, seq_lengths), seq_count)
        return moments, scores.T
    tile = min(256, cols)
    tiles = cols // tile
    chunks = min(4, tiles)
    far = [k for k in range(1, dp_count) if bin(k >> 1).count("1") >= 2]
    shared_train = far if tok_dev % (16 * mp_count) == 0 and dp_count <= 2 * tiles else []
    shared_query = far if q_dev % (16 * mp_count) == 0 and dp_count <= 2 * tiles else []
    steps = max(1, mp_count - 1)
    dma = pltpu.SemaphoreType.DMA
    any_space = pl.BlockSpec(memory_space=pl.ANY)
    bf16 = jnp.bfloat16
    raw, scores = pl.pallas_call(
        functools.partial(kernel, dp_count, mp_count, chunks, shared_train, shared_query),
        out_shape=(
            pltpu.VMEM((act_width, cols), jnp.float32),
            pltpu.VMEM((8, 128), jnp.float32),
        ),
        in_specs=[pl.BlockSpec(memory_space=pltpu.SMEM)] + [any_space] * 6,
        out_specs=(pl.BlockSpec(memory_space=pltpu.VMEM), pl.BlockSpec(memory_space=pltpu.VMEM)),
        scratch_shapes=[
            pltpu.VMEM((dp_count, tok_dev, act_width), bf16),
            pltpu.VMEM((dp_count, q_dev, act_width), bf16),
            pltpu.VMEM((dp_count, tok_dev, cols), bf16),
            pltpu.VMEM((dp_count, q_dev, cols), bf16),
            pltpu.VMEM(act_basis.shape, bf16),
            pltpu.VMEM(grad_basis.shape, bf16),
            pltpu.VMEM((act_width, tokens), bf16),
            pltpu.VMEM((q_rows, act_width), bf16),
            pltpu.VMEM((seq_count, tiles, act_width, tile), bf16),
            pltpu.VMEM((tiles, 8, tile), jnp.float32),
            pltpu.VMEM((seq_count, QUERIES, 8, 128), jnp.float32),
            dma((dp_count,)), dma((dp_count,)), dma((dp_count,)), dma((dp_count,)),
            dma((1, dp_count)), dma((1, dp_count)), dma((chunks, dp_count)), dma((chunks, dp_count)),
            dma((max(1, len(shared_train)), steps)), dma((max(1, len(shared_train)), steps)),
            dma((max(1, len(shared_query)), steps)), dma((max(1, len(shared_query)), steps)),
            dma((6,)), dma((tiles,)),
            pltpu.VMEM((dp_count, QUERIES, 128), jnp.float32),
            pltpu.VMEM((mp_count, QUERIES, 128), jnp.float32),
            dma((dp_count,)), dma((dp_count,)), dma((steps,)), dma((steps,)),
        ],
        compiler_params=pltpu.CompilerParams(
            collective_id=0, has_side_effects=True, vmem_limit_bytes=54 * 1024 * 1024),
    )(seq_lengths, act_in, grad_in, query_act, query_grad, act_basis, grad_basis)
    moments, scores = store(raw, scores, seq_count)
    return moments, scores.T


def store_kernel(raw, scores_in, moments, scores, sems):
    n = sems.shape[0]
    rows = raw.shape[0] // n
    copies = [pltpu.make_async_copy(raw.at[pl.ds(i * rows, rows)], moments.at[pl.ds(i * rows, rows)], sems.at[i])
              for i in range(n)]
    for c in copies:
        c.start()
    scores[...] = scores_in[:scores.shape[0], :scores.shape[1]]
    for c in copies:
        c.wait()


def store(raw, scores, seq_count):
    n = 8
    vm = pl.BlockSpec(memory_space=pltpu.VMEM)
    return pl.pallas_call(
        store_kernel,
        out_shape=(jax.ShapeDtypeStruct(raw.shape, raw.dtype), jax.ShapeDtypeStruct((seq_count, QUERIES), scores.dtype)),
        in_specs=[vm, vm], out_specs=(pl.BlockSpec(memory_space=pltpu.HBM), vm),
        scratch_shapes=[pltpu.SemaphoreType.DMA((n,))],
        compiler_params=pltpu.CompilerParams(vmem_limit_bytes=1024*1024),
    )(pltpu.with_memory_space_constraint(raw, pltpu.VMEM), pltpu.with_memory_space_constraint(scores, pltpu.VMEM))


def solution(mesh):
    return jax.shard_map(
        local,
        mesh=mesh,
        in_specs=(
            P("dp", "mp"),
            P("dp", None),
            P("dp", "mp"),
            P("dp", None),
            P("mp", None),
            P("dp", None),
            P(),
        ),
        out_specs=(P("mp", "dp"), P()),
        check_vma=False,
    )
```

```python
import functools
import itertools
import math

import jax
import jax.numpy as jnp
from jax import lax
from jax.experimental import pallas as pl
from jax.experimental.pallas import tpu as pltpu
from jax.sharding import PartitionSpec as P

D = 4096
FF = 16384
QUERIES = 64
QUERY_LEN = 16

damping = 0.1
MESH = pl.DeviceIdType.MESH


def flipped(index, mask):
    bit = 1
    while bit <= mask:
        if mask & bit:
            index = index + bit * (1 - 2 * ((index // bit) % 2))
        bit *= 2
    return index


def across(columns):
    square = jnp.concatenate([columns, jnp.zeros((128 - columns.shape[0], 128), jnp.float32)], axis=0)
    return square.T[:8, :]


def kernel(
    dp_count, mp_count, chunks, shared_train, shared_query,
    lengths, act_in, grad_in, query_act, query_grad, act_basis_in, grad_basis_in,
    moments, partial,
    act_raw, qact_raw, grad_raw, qgrad_raw, act_basis, grad_basis,
    act_t, q_rot, precond, staged, totals,
    act_send, act_recv, qact_send, qact_recv, grad_send, grad_recv, qgrad_send, qgrad_recv,
    pass_send, pass_recv, qpass_send, qpass_recv, local_sem, out_sem,
    shares, crossing, share_send, share_recv, cross_send, cross_recv,
):
    me = lax.axis_index("dp")
    mine = lax.axis_index("mp")
    seq_count = lengths.shape[0]
    tok_dev, act_width = act_in.shape
    q_dev = query_act.shape[0]
    cols = grad_raw.shape[2]
    block = act_basis_in.shape[1]
    tiles, _, tile = staged.shape
    tokens = tok_dev * dp_count
    seq_len = tokens // seq_count
    q_rows = q_dev * dp_count
    chunk_cols = cols // chunks
    masks = list(range(1, dp_count))
    peers = {k: flipped(me, k) for k in masks}

    barrier = pltpu.get_barrier_semaphore()
    for k in masks:
        pl.semaphore_signal(barrier, inc=1, device_id={"dp": peers[k], "mp": mine}, device_id_type=MESH)
    others = [lax.rem(mine + step, mp_count) for step in range(1, mp_count)]
    for other in others:
        pl.semaphore_signal(barrier, inc=1, device_id={"dp": me, "mp": other}, device_id_type=MESH)

    locals_in = [
        pltpu.make_async_copy(act_in, act_raw.at[me], local_sem.at[0]),
        pltpu.make_async_copy(act_basis_in, act_basis, local_sem.at[1]),
        pltpu.make_async_copy(grad_basis_in, grad_basis, local_sem.at[2]),
        pltpu.make_async_copy(
            grad_in.at[:, pl.ds(pl.multiple_of(me * cols, 128), cols)], grad_raw.at[me], local_sem.at[3]),
        pltpu.make_async_copy(query_act, qact_raw.at[me], local_sem.at[4]),
        pltpu.make_async_copy(
            query_grad.at[:, pl.ds(pl.multiple_of(me * cols, 128), cols)], qgrad_raw.at[me], local_sem.at[5]),
    ]
    for copy in locals_in:
        copy.start()
    pl.semaphore_wait(barrier, len(masks) + len(others))

    def remote(src, dst, send, recv, dp, mp):
        return pltpu.make_async_remote_copy(
            src_ref=src, dst_ref=dst, send_sem=send, recv_sem=recv,
            device_id={"dp": dp, "mp": mp}, device_id_type=MESH)

    sends = []

    def begin(copy):
        copy.start()
        sends.append(copy)

    act_masks = [k for k in masks if k == 1 or k % 2 == 0]

    def send_acts(src, raw, send, recv):
        for k in reversed(act_masks):
            begin(remote(src, raw.at[me], send.at[k], recv.at[k], peers[k], mine))

    def part_of(owner, rows):
        return pl.ds(pl.multiple_of(owner * (rows // mp_count), 16), rows // mp_count)

    def send_shared(src, raw, send, recv, shared):
        rows = part_of(mine, src.shape[0])
        for k in reversed(shared):
            there = pl.ds(pl.multiple_of(peers[k] * cols, 128), cols)
            begin(remote(
                src.at[rows, there], raw.at[me, rows, :], send.at[0, k], recv.at[0, k], peers[k], mine))

    def send_grads(src, raw, send, recv, shared, start, width, slot):
        for k in reversed(masks):
            if k not in shared:
                there = pl.ds(pl.multiple_of(peers[k] * cols + start, 128), width)
                begin(remote(
                    src.at[:, there], raw.at[me, :, pl.ds(start, width)],
                    send.at[slot, k], recv.at[slot, k], peers[k], mine))

    send_acts(act_in, act_raw, act_send, act_recv)
    send_shared(grad_in, grad_raw, grad_send, grad_recv, shared_train)
    send_shared(query_grad, qgrad_raw, qgrad_send, qgrad_recv, shared_query)
    send_grads(grad_in, grad_raw, grad_send, grad_recv, shared_train, 0, cols, 0)
    send_acts(query_act, qact_raw, qact_send, qact_recv)
    for c in range(chunks):
        send_grads(query_grad, qgrad_raw, qgrad_send, qgrad_recv, shared_query, c * chunk_cols, chunk_cols, c)

    def arrived(ref, send, recv):
        remote(ref, ref, send, recv, peers[1], mine).wait_recv()

    def relay_acts(raw, send, recv):
        for k in reversed(act_masks):
            arrived(raw.at[peers[k]], send.at[k], recv.at[k])
            if k > 1:
                here = raw.at[peers[k]]
                begin(remote(here, here, send.at[k + 1], recv.at[k + 1], peers[1], mine))

    def finish_acts(raw, send, recv):
        for k in masks:
            if k not in act_masks:
                arrived(raw.at[peers[k]], send.at[k], recv.at[k])

    def relay_grads(raw, send, recv, fsend, frecv, shared):
        for n, k in enumerate(reversed(shared)):
            here = raw.at[peers[k], part_of(mine, raw.shape[1]), :]
            arrived(here, send.at[0, k], recv.at[0, k])
            for step, other in enumerate(others):
                begin(remote(here, here, fsend.at[n, step], frecv.at[n, step], me, other))

    def finish_grads(raw, send, recv, shared, start, width, slot):
        for k in reversed(masks):
            if k not in shared:
                arrived(raw.at[peers[k], :, pl.ds(start, width)], send.at[slot, k], recv.at[slot, k])

    def finish_shared(raw, fsend, frecv, shared):
        for n, k in enumerate(reversed(shared)):
            for step in range(mp_count - 1):
                owner = lax.rem(mine + (mp_count - 1 - step), mp_count)
                arrived(
                    raw.at[peers[k], part_of(owner, raw.shape[1]), :], fsend.at[n, step], frecv.at[n, step])

    relay_acts(act_raw, act_send, act_recv)
    finish_acts(act_raw, act_send, act_recv)
    relay_grads(grad_raw, grad_send, grad_recv, pass_send, pass_recv, shared_train)
    relay_grads(qgrad_raw, qgrad_send, qgrad_recv, qpass_send, qpass_recv, shared_query)
    for copy in locals_in:
        copy.wait()

    limits = [lengths[s] for s in range(seq_count)]
    counted = limits[0]
    for s in range(1, seq_count):
        counted = counted + limits[s]
    inverse = 1.0 / jnp.full((1, tile), counted.astype(jnp.float32), jnp.float32)

    @pl.loop(0, dp_count)
    def _(e):
        where_tok = e * tok_dev + lax.broadcasted_iota(jnp.int32, (block, tok_dev), 1)
        live = jnp.zeros((block, tok_dev), jnp.float32)
        for s in range(seq_count):
            inside = (where_tok >= s * seq_len) & (where_tok < s * seq_len + limits[s])
            live = jnp.where(inside, 1.0, live)
        for b in range(act_width // block):
            span = pl.ds(b * block, block)
            turned = lax.dot_general(
                act_basis[span, :].T, act_raw[e, :, span], (((1,), (1,)), ((), ())),
                preferred_element_type=jnp.float32)
            act_t[span, pl.ds(pl.multiple_of(e * tok_dev, 128), tok_dev)] = (turned * live).astype(jnp.bfloat16)

    def wide_basis(jt):
        first = grad_basis[pl.ds(pl.multiple_of(jt * tile, 128), block), :]
        rows = []
        count = tile // block
        zero = jnp.zeros_like(first)
        for h in range(count):
            own = grad_basis[pl.ds(pl.multiple_of(jt * tile + h * block, 128), block), :]
            rows.append(jnp.concatenate([own if g == h else zero for g in range(count)], axis=1))
        return jnp.concatenate(rows, axis=0)

    def turned_grads(raw, jt, rows):
        span = pl.ds(pl.multiple_of(jt * tile, 128), tile)
        whole = raw[:, :, span].reshape(rows, tile)
        return jnp.dot(whole, wide_basis(jt), preferred_element_type=jnp.float32).astype(jnp.bfloat16)

    finish_shared(grad_raw, pass_send, pass_recv, shared_train)
    finish_grads(grad_raw, grad_send, grad_recv, shared_train, 0, cols, 0)

    def out_copy(jt):
        span = pl.ds(pl.multiple_of(jt * tile, 128), tile)
        return pltpu.make_async_copy(staged.at[jt], moments.at[:, span], out_sem.at[jt])

    per_chunk = tiles // chunks

    def first_phase(jt):
        grads = turned_grads(grad_raw, jt, tokens)
        total = jnp.zeros((act_width, tile), jnp.float32)
        for s in range(seq_count):
            a = act_t[:, s * seq_len:(s + 1) * seq_len]
            g = grads[s * seq_len:(s + 1) * seq_len, :]
            total = total + jnp.dot(a * a, g * g, preferred_element_type=jnp.float32)
        total = total * inverse
        moments[:, pl.ds(pl.multiple_of(jt * tile, 128), tile)] = total
        weights = 1.0 / (total + damping)
        for s in range(seq_count):
            a = act_t[:, s * seq_len:(s + 1) * seq_len]
            g = grads[s * seq_len:(s + 1) * seq_len, :]
            precond[s, jt] = (weights * jnp.dot(a, g, preferred_element_type=jnp.float32)).astype(jnp.bfloat16)

    half = tiles // 2
    pl.loop(0, half)(first_phase)
    relay_acts(qact_raw, qact_send, qact_recv)
    pl.loop(half, tiles)(first_phase)
    finish_acts(qact_raw, qact_send, qact_recv)

    @pl.loop(0, dp_count)
    def _(e):
        for b in range(act_width // block):
            span = pl.ds(b * block, block)
            turned = jnp.dot(qact_raw[e, :, span], act_basis[span, :], preferred_element_type=jnp.float32)
            q_rot[pl.ds(pl.multiple_of(e * q_dev, 16), q_dev), span] = turned.astype(jnp.bfloat16)

    totals[...] = jnp.zeros_like(totals)
    finish_shared(qgrad_raw, qpass_send, qpass_recv, shared_query)

    def second_phase(jt):
        grads = turned_grads(qgrad_raw, jt, q_rows).astype(jnp.float32)
        for s in range(seq_count):
            mapped = jnp.dot(q_rot[...], precond[s, jt], preferred_element_type=jnp.float32) * grads
            folded = mapped[:, :128]
            for h in range(1, tile // 128):
                folded = folded + mapped[:, h * 128:(h + 1) * 128]
            totals[s] += folded.reshape(QUERIES, q_rows // QUERIES // 8, 8, 128).sum(axis=1)

    for c in range(chunks):
        finish_grads(qgrad_raw, qgrad_send, qgrad_recv, shared_query, c * chunk_cols, chunk_cols, c)
        pl.loop(c * per_chunk, (c + 1) * per_chunk)(second_phase)

    lane = lax.broadcasted_iota(jnp.int32, (QUERIES, 128), 1)
    answer = jnp.zeros((QUERIES, 128), jnp.float32)
    for s in range(seq_count):
        row = jnp.sum(jnp.sum(totals[s], axis=1), axis=1, keepdims=True)
        answer = jnp.where(lane == s, row, answer)
    lens = jnp.ones((QUERIES, 128), jnp.float32)
    for s in range(seq_count):
        lens = jnp.where(lane == s, limits[s].astype(jnp.float32), lens)
    shares[me] = answer * lax.rsqrt(lens) / math.sqrt(QUERY_LEN * D * FF)

    for copy in sends:
        copy.wait_send()
    sends.clear()

    for k in masks:
        begin(remote(shares.at[me], shares.at[me], share_send.at[k], share_recv.at[k], peers[k], mine))
    for k in masks:
        arrived(shares.at[peers[k]], share_send.at[k], share_recv.at[k])
    summed = shares[0]
    for e in range(1, dp_count):
        summed = summed + shares[e]
    crossing[mine] = summed
    for step, other in enumerate(others):
        begin(remote(
            crossing.at[mine], crossing.at[mine], cross_send.at[step], cross_recv.at[step], me, other))
    for step in range(mp_count - 1):
        owner = lax.rem(mine + (mp_count - 1 - step), mp_count)
        arrived(crossing.at[owner], cross_send.at[step], cross_recv.at[step])
    summed = crossing[0]
    for e in range(1, mp_count):
        summed = summed + crossing[e]
    partial[...] = across(summed)
    for copy in sends:
        copy.wait_send()


NEAR = (2, 4, 3, 5)
FAR = (6, 7)
TRAIN_CUTS = (0, 2, 4, 6, 8)
QUERY_CUTS = (0, 1, 2, 3, 4, 5, 6, 7, 8)
TRAIN_SPLITS = ((5, 7), (5, 7), (5, 7), (5, 7))
PLAN = (
    ("lead", 0, 0),
    ("lead", 0, 1),
    ("acts", 0),
    ("trail", 0, 0),
    ("lead", 0, 2),
    ("side", 0),
    ("relay", 0, 0),
    ("relay", 0, 1),
    ("pass", 0),
    ("lead", 0, 3),
    ("trail", 0, 1),
    ("lead", 1, 0),
    ("lead", 1, 1),
    ("trail", 0, 2),
    ("acts", 1),
    ("trail", 0, 3),
    ("lead", 1, 2),
    ("lead", 1, 3),
    ("side", 1),
    ("relay", 0, 2),
    ("first", 0),
    ("all", 0),
    ("sided", 0),
    ("rest", 0, 0),
    ("tiles", 0, 0, 2),
    ("relay", 0, 3),
    ("rest", 0, 1),
    ("tiles", 0, 2, 4),
    ("relay", 1, 0),
    ("relay", 1, 1),
    ("rest", 0, 2),
    ("tiles", 0, 4, 6),
    ("pass", 1),
    ("trail", 1, 0),
    ("lead", 1, 4),
    ("trail", 1, 1),
    ("lead", 1, 5),
    ("trail", 1, 2),
    ("lead", 1, 6),
    ("trail", 1, 3),
    ("lead", 1, 7),
    ("trail", 1, 4),
    ("trail", 1, 5),
    ("trail", 1, 6),
    ("trail", 1, 7),
    ("rest", 0, 3),
    ("tiles", 0, 6, 8),
    ("relay", 1, 2),
    ("relay", 1, 3),
    ("first", 1),
    ("all", 1),
    ("sided", 1),
    ("rest", 1, 0),
    ("tiles", 1, 0, 1),
    ("relay", 1, 4),
    ("rest", 1, 1),
    ("tiles", 1, 1, 2),
    ("relay", 1, 5),
    ("rest", 1, 2),
    ("tiles", 1, 2, 3),
    ("relay", 1, 6),
    ("rest", 1, 3),
    ("tiles", 1, 3, 4),
    ("relay", 1, 7),
    ("rest", 1, 4),
    ("tiles", 1, 4, 5),
    ("rest", 1, 5),
    ("tiles", 1, 5, 6),
    ("rest", 1, 6),
    ("tiles", 1, 6, 7),
    ("rest", 1, 7),
    ("tiles", 1, 7, 8),
)
QUERY_SPLITS = ((5, 7), (5, 7), (4, 8), (4, 8), (4, 8), (3, 8), (3, 8), (3, 8))


def routed_kernel(
    lengths, act_in, grad_in, query_act, query_grad, act_basis_in, grad_basis_in,
    moments, partial,
    act_raw, qact_raw, grad_raw, qgrad_raw, act_basis, grad_basis,
    act_t, act_sq, q_rot, precond, totals, shares,
    act_send, act_recv, grad_send, lead_recv, rest_recv, side_send, side_recv, local_sem,
    share_send, share_recv, ready,
):
    me = lax.axis_index("dp")
    mine = lax.axis_index("mp")
    dp_count = lax.axis_size("dp")
    mp_count = lax.axis_size("mp")
    tok_dev, act_width = act_in.shape
    seq_count = lengths.shape[0]
    q_dev = query_act.shape[0]
    cols = grad_raw.shape[1]
    block = act_basis.shape[1]
    tile = cols // TRAIN_CUTS[-1]
    tokens = tok_dev * dp_count
    seq_len = tokens // seq_count
    q_rows = q_dev * dp_count
    masks = list(range(1, dp_count))
    peers = {k: flipped(me, k) for k in masks}
    others = [lax.rem(mine + step, mp_count) for step in range(1, mp_count)]

    is_end = (mine == 0) | (mine == mp_count - 1)
    is_mid = jnp.logical_not(is_end)
    partner = flipped(mine, 1)
    half = lax.rem(mine + 1, 2)
    far_planes = [partner, mp_count - 1 - mine, mp_count - 1 - partner]

    barrier = pltpu.get_barrier_semaphore()
    for k in masks:
        pl.semaphore_signal(barrier, inc=1, device_id={"dp": peers[k], "mp": mine}, device_id_type=MESH)
    for other in others:
        pl.semaphore_signal(barrier, inc=1, device_id={"dp": me, "mp": other}, device_id_type=MESH)

    own = pl.ds(pl.multiple_of(me * cols, 128), cols)
    own_tok = pl.ds(pl.multiple_of(me * tok_dev, 128), tok_dev)
    own_q = pl.ds(pl.multiple_of(me * q_dev, 128), q_dev)
    locals_in = [
        pltpu.make_async_copy(act_in, act_raw.at[own_tok], local_sem.at[0]),
        pltpu.make_async_copy(act_basis_in, act_basis, local_sem.at[1]),
        pltpu.make_async_copy(grad_basis_in, grad_basis, local_sem.at[2]),
        pltpu.make_async_copy(grad_in.at[:, own], grad_raw.at[own_tok], local_sem.at[3]),
        pltpu.make_async_copy(query_act, qact_raw.at[own_q], local_sem.at[4]),
        pltpu.make_async_copy(query_grad.at[:, own], qgrad_raw.at[own_q], local_sem.at[5]),
    ]
    for copy in locals_in:
        copy.start()
    pl.semaphore_wait(barrier, len(masks) + len(others))

    def remote(src, dst, send, recv, dp, mp):
        return pltpu.make_async_remote_copy(
            src_ref=src, dst_ref=dst, send_sem=send, recv_sem=recv,
            device_id={"dp": dp, "mp": mp}, device_id_type=MESH)

    def arrived(ref, recv):
        remote(ref, ref, side_send.at[0], recv, peers[1], mine).wait_recv()

    def left(ref, send):
        remote(ref, ref, send, side_recv.at[0], peers[1], mine).wait_send()

    def by_role(act):
        @pl.when(is_end)
        def _():
            act("end")

        @pl.when(is_mid)
        def _():
            act("mid")

    phases = (
        (grad_in, grad_raw, tok_dev, TRAIN_CUTS, TRAIN_SPLITS),
        (query_grad, qgrad_raw, q_dev, QUERY_CUTS, QUERY_SPLITS),
    )

    def span_of(phase, c):
        cuts = phases[phase][3]
        return cuts[c] * tile, (cuts[c + 1] - cuts[c]) * tile

    def count_of(phase, part, c):
        first, second = phases[phase][4][c]
        eighth = phases[phase][2] // 8
        return {"a": first, "b": second - first, "c": 8 - second, "own": 4}[part] * eighth

    def rows_of(phase, part, c):
        first, second = phases[phase][4][c]
        eighth = phases[phase][2] // 8
        low = {"a": 0, "b": first, "c": second, "own": half * 4}[part]
        return low * eighth, count_of(phase, part, c)

    def held(phase, k, part, c):
        start, width = span_of(phase, c)
        low, rows = rows_of(phase, part, c)
        here = pl.ds(pl.multiple_of(peers[k] * phases[phase][2] + low, 16), rows)
        return phases[phase][1].at[here, pl.ds(start, width)]

    def bulk(phase, rows, c):
        start, width = span_of(phase, c)
        return phases[phase][1].at[pl.ds(0, rows), pl.ds(start, width)]

    def hop(phase, part, c, ks, recv):
        src, raw, size, _, _ = phases[phase]
        start, width = span_of(phase, c)
        low, rows = rows_of(phase, part, c)
        if not rows:
            return
        taken = pl.ds(pl.multiple_of(low, 16), rows)
        put = pl.ds(pl.multiple_of(me * size + low, 16), rows)
        for k in ks:
            there = pl.ds(pl.multiple_of(peers[k] * cols + start, 128), width)
            remote(
                src.at[taken, there], raw.at[put, pl.ds(start, width)],
                grad_send.at[phase, c], recv, peers[k], mine).start()

    def lead(role, phase, c):
        if role == "end":
            hop(phase, "a", c, NEAR[:2], lead_recv.at[phase, c, 0])
            hop(phase, "a", c, NEAR[2:], lead_recv.at[phase, c, 1])
        else:
            hop(phase, "own", c, FAR, lead_recv.at[phase, c, 0])
            hop(phase, "c", c, NEAR, lead_recv.at[phase, c, 1])

    def trail(role, phase, c):
        hop(phase, "b", c, NEAR, rest_recv.at[phase, c])

    def relay(role, phase, c):
        def onward(k, part, to):
            here = held(phase, k, part, c)
            remote(here, here, grad_send.at[phase, c], rest_recv.at[phase, c], me, to).start()

        if role == "end":
            for g, ks in enumerate((NEAR[:2], NEAR[2:])):
                arrived(bulk(phase, 2 * count_of(phase, "a", c), c), lead_recv.at[phase, c, g])
                for k in ks:
                    onward(k, "a", partner)
        else:
            arrived(bulk(phase, 2 * count_of(phase, "own", c), c), lead_recv.at[phase, c, 0])
            for to in far_planes:
                for k in FAR:
                    onward(k, "own", to)
            if count_of(phase, "c", c):
                arrived(bulk(phase, 4 * count_of(phase, "c", c), c), lead_recv.at[phase, c, 1])
                for k in NEAR:
                    onward(k, "c", partner)

    def rest(role, phase, c):
        a, b, d, own_half = [count_of(phase, part, c) for part in ("a", "b", "c", "own")]
        rows = 4 * (b + d) + 4 * own_half if role == "end" else 4 * (a + b) + 2 * own_half
        arrived(bulk(phase, rows, c), rest_recv.at[phase, c])

    def gone(role, phase):
        for c in range(len(phases[phase][4])):
            a, b, d, own_half = [count_of(phase, part, c) for part in ("a", "b", "c", "own")]
            rows = 4 * (a + b) + 4 * a if role == "end" else 4 * (b + d) + 2 * own_half + 6 * own_half + 4 * d
            left(bulk(phase, rows, c), grad_send.at[phase, c])

    def side(phase):
        src, raw, size, _, _ = phases[phase]
        there = pl.ds(pl.multiple_of(peers[1] * cols, 128), cols)
        put = pl.ds(pl.multiple_of(me * size, 128), size)
        remote(src.at[:, there], raw.at[put], side_send.at[phase], side_recv.at[phase], peers[1], mine).start()

    def finish_side(phase):
        arrived(phases[phase][1].at[pl.ds(0, phases[phase][2])], side_recv.at[phase])

    acts = ((act_in, act_raw, tok_dev), (query_act, qact_raw, q_dev))

    def act_rows(phase, k, low, rows):
        size = acts[phase][2]
        return acts[phase][1].at[pl.ds(pl.multiple_of(peers[k] * size + low, 16), rows)]

    def act_go(phase, src, dst, recv_slot, k):
        remote(src, dst, act_send.at[phase], act_recv.at[phase, recv_slot], peers[k], mine).start()

    def send_acts(phase):
        src, raw, size = acts[phase]
        put = raw.at[pl.ds(pl.multiple_of(me * size, 16), size)]
        for k, slot in ((2, 0), (4, 1), (1, 3)):
            act_go(phase, src, put, slot, k)

    def pass_acts(phase):
        _, raw, size = acts[phase]
        for n, (k, onward) in enumerate(((2, 4), (4, 2))):
            arrived(raw.at[pl.ds(0, size)], act_recv.at[phase, n])
            part = act_rows(phase, k, n * (size // 2), size // 2)
            act_go(phase, part, part, 2, onward)
        for k in (2, 4):
            whole = act_rows(phase, k, 0, size)
            act_go(phase, whole, whole, 3, 1)

    def finish_acts(phase):
        _, raw, size = acts[phase]
        arrived(raw.at[pl.ds(0, size)], act_recv.at[phase, 2])
        whole = act_rows(phase, 6, 0, size)
        act_go(phase, whole, whole, 4, 1)

    def near_acts(phase):
        _, raw, size = acts[phase]
        arrived(raw.at[pl.ds(0, 3 * size)], act_recv.at[phase, 3])

    def last_acts(phase):
        _, raw, size = acts[phase]
        arrived(raw.at[pl.ds(0, size)], act_recv.at[phase, 4])

    def acts_gone(phase):
        _, raw, size = acts[phase]
        left(raw.at[pl.ds(0, 7 * size)], act_send.at[phase])

    for other in others:
        pl.semaphore_signal(ready, inc=1, device_id={"dp": me, "mp": other}, device_id_type=MESH)

    limits = [lengths[s] for s in range(seq_count)]
    counted = limits[0]
    for s in range(1, seq_count):
        counted = counted + limits[s]
    inverse = 1.0 / jnp.full((1, tile), counted.astype(jnp.float32), jnp.float32)

    def chip_rows(p, rows):
        place, result = 1, 0
        chip = lax.div(me, 2)
        while place < dp_count // 2:
            result = result + place * lax.rem(lax.div(chip, place) + lax.div(p, place), 2)
            place *= 2
        return result * rows

    def wide(basis, start, count):
        rows = []
        zero = jnp.zeros((block, block), jnp.bfloat16)
        for h in range(count):
            piece = basis[pl.ds(start + h * block, block), :]
            rows.append(jnp.concatenate([piece if g == h else zero for g in range(count)], axis=1))
        return jnp.concatenate(rows, axis=0)

    def turn_acts(low, high):
        rows = 2 * tok_dev

        @pl.loop(low // 2, high // 2)
        def _(p):
            first = chip_rows(p, rows)
            where_tok = first + lax.broadcasted_iota(jnp.int32, (2 * block, rows), 1)
            live = jnp.zeros((2 * block, rows), jnp.float32)
            for s in range(seq_count):
                inside = (where_tok >= s * seq_len) & (where_tok < s * seq_len + limits[s])
                live = jnp.where(inside, 1.0, live)
            to = pl.ds(pl.multiple_of(first, 128), rows)
            for b in range(act_width // (2 * block)):
                span = pl.ds(b * 2 * block, 2 * block)
                turned = lax.dot_general(
                    wide(act_basis, b * 2 * block, 2).T, act_raw[to, span], (((1,), (1,)), ((), ())),
                    preferred_element_type=jnp.float32)
                kept = (turned * live).astype(jnp.bfloat16)
                act_t[span, to] = kept
                act_sq[span, to] = kept * kept

    def turn_query_acts(low, high):
        rows = 2 * q_dev

        @pl.loop(low // 2, high // 2)
        def _(p):
            here = pl.ds(pl.multiple_of(chip_rows(p, rows), 128), rows)
            for b in range(act_width // (2 * block)):
                span = pl.ds(b * 2 * block, 2 * block)
                turned = jnp.dot(
                    qact_raw[here, span], wide(act_basis, b * 2 * block, 2), preferred_element_type=jnp.float32)
                q_rot[here, span] = turned.astype(jnp.bfloat16)

    def turned_grads(raw, jt):
        start = pl.multiple_of(jt * tile, 128)
        whole = raw[:, pl.ds(start, tile)]
        return jnp.dot(
            whole, wide(grad_basis, start, tile // block), preferred_element_type=jnp.float32).astype(jnp.bfloat16)

    def train_tile(jt):
        grads = turned_grads(grad_raw, jt)
        total = jnp.dot(act_sq[...], grads * grads, preferred_element_type=jnp.float32) * inverse
        moments[:, pl.ds(pl.multiple_of(jt * tile, 128), tile)] = total
        weights = 1.0 / (total + damping)
        for s in range(seq_count):
            a = act_t[:, s * seq_len:(s + 1) * seq_len]
            g = grads[s * seq_len:(s + 1) * seq_len, :]
            precond[s, :, pl.ds(pl.multiple_of(jt * tile, 128), tile)] = (
                weights * jnp.dot(a, g, preferred_element_type=jnp.float32)).astype(jnp.bfloat16)

    def query_tiles(low, high):
        grads = [turned_grads(qgrad_raw, jt).astype(jnp.float32) for jt in range(low, high)]
        grads = jnp.concatenate(grads, axis=1)
        for s in range(seq_count):
            weights = precond[s, :, pl.ds(low * tile, (high - low) * tile)]
            mapped = jnp.dot(q_rot[...], weights, preferred_element_type=jnp.float32) * grads
            folded = mapped[:, :128]
            for h in range(1, mapped.shape[1] // 128):
                folded = folded + mapped[:, h * 128:(h + 1) * 128]
            totals[s] += folded.reshape(QUERIES, q_rows // QUERIES // 8, 8, 128).sum(axis=1)

    turn = (turn_acts, turn_query_acts)

    def first_acts(phase):
        near_acts(phase)
        if phase == 0:
            for copy in locals_in:
                copy.wait()
            totals[...] = jnp.zeros_like(totals)
        turn[phase](0, 6)

    def all_acts(phase):
        finish_acts(phase)
        last_acts(phase)
        turn[phase](6, dp_count)

    def tiles_now(phase, low, high):
        if phase:
            query_tiles(low, high)
        else:
            pl.loop(low, high)(train_tile)

    by_roles = {"lead": lead, "trail": trail, "relay": relay, "rest": rest}
    plain = {
        "acts": send_acts, "pass": pass_acts, "first": first_acts, "all": all_acts,
        "side": side, "sided": finish_side, "tiles": tiles_now}
    for shared, group in itertools.groupby(PLAN, lambda step: step[0] in by_roles):
        group = list(group)
        if shared:
            by_role(lambda role: [by_roles[name](role, *where) for name, *where in group])
        else:
            for name, *where in group:
                plain[name](*where)

    lane = lax.broadcasted_iota(jnp.int32, (QUERIES, 128), 1)
    answer = jnp.zeros((QUERIES, 128), jnp.float32)
    for s in range(seq_count):
        row = jnp.sum(jnp.sum(totals[s], axis=1), axis=1, keepdims=True)
        answer = jnp.where(lane == s, row, answer)
    lens = jnp.ones((QUERIES, 128), jnp.float32)
    for s in range(seq_count):
        lens = jnp.where(lane == s, limits[s].astype(jnp.float32), lens)
    slot = mine * dp_count + me
    shares[slot] = across(answer * lax.rsqrt(lens) / math.sqrt(QUERY_LEN * D * FF))

    pl.semaphore_wait(ready, len(others))
    mine_there = shares.at[slot]
    for step in reversed(range(mp_count)):
        plane = lax.rem(mine + step, mp_count)
        for k in reversed(range(dp_count)):
            if k or step:
                remote(
                    mine_there, mine_there, share_send.at[0], share_recv.at[0],
                    peers[k] if k else me, plane).start()

    def ended(role):
        gone(role, 0)
        gone(role, 1)

    by_role(ended)
    for phase in range(2):
        acts_gone(phase)
        left(phases[phase][1].at[pl.ds(0, phases[phase][2])], side_send.at[phase])
    every = shares.at[pl.ds(0, dp_count * mp_count - 1)]
    left(every, share_send.at[0])
    arrived(every, share_recv.at[0])
    summed = shares[0]
    for e in range(1, dp_count * mp_count):
        summed = summed + shares[e]
    partial[...] = summed


def routed(act_in, grad_in, query_act, query_grad, act_basis, grad_basis, seq_lengths):
    dp_count = lax.axis_size("dp")
    mp_count = lax.axis_size("mp")
    tok_dev, act_width = act_in.shape
    q_dev = query_act.shape[0]
    cols = grad_in.shape[1] // dp_count
    seq_count = seq_lengths.shape[0]
    tokens, q_rows = tok_dev * dp_count, q_dev * dp_count
    dma = pltpu.SemaphoreType.DMA
    any_space = pl.BlockSpec(memory_space=pl.ANY)
    bf16 = jnp.bfloat16
    chunks = max(len(TRAIN_SPLITS), len(QUERY_SPLITS))
    return pl.pallas_call(
        routed_kernel,
        out_shape=(
            pltpu.VMEM((act_width, cols), jnp.float32),
            pltpu.VMEM((8, 128), jnp.float32),
        ),
        in_specs=[pl.BlockSpec(memory_space=pltpu.SMEM)] + [any_space] * 6,
        out_specs=(pl.BlockSpec(memory_space=pltpu.VMEM), pl.BlockSpec(memory_space=pltpu.VMEM)),
        scratch_shapes=[
            pltpu.VMEM((tokens, act_width), bf16),
            pltpu.VMEM((q_rows, act_width), bf16),
            pltpu.VMEM((tokens, cols), bf16),
            pltpu.VMEM((q_rows, cols), bf16),
            pltpu.VMEM(act_basis.shape, bf16),
            pltpu.VMEM((cols, grad_basis.shape[1]), bf16),
            pltpu.VMEM((act_width, tokens), bf16),
            pltpu.VMEM((act_width, tokens), bf16),
            pltpu.VMEM((q_rows, act_width), bf16),
            pltpu.VMEM((seq_count, act_width, cols), bf16),
            pltpu.VMEM((seq_count, QUERIES, 8, 128), jnp.float32),
            pltpu.VMEM((dp_count * mp_count, 8, 128), jnp.float32),
            dma((2,)), dma((2, 5)), dma((2, chunks)), dma((2, chunks, 2)), dma((2, chunks)),
            dma((2,)), dma((2,)), dma((6,)), dma((1,)), dma((1,)), pltpu.SemaphoreType.REGULAR,
        ],
        compiler_params=pltpu.CompilerParams(
            collective_id=1, has_side_effects=True, vmem_limit_bytes=54 * 1024 * 1024),
    )(seq_lengths, act_in, grad_in, query_act, query_grad, act_basis, grad_basis)


def local(act_in, grad_in, query_act, query_grad, act_basis, grad_basis, seq_lengths):
    dp_count = lax.axis_size("dp")
    mp_count = lax.axis_size("mp")
    tok_dev, act_width = act_in.shape
    q_dev = query_act.shape[0]
    cols = grad_in.shape[1] // dp_count
    seq_count = seq_lengths.shape[0]
    tokens, q_rows = tok_dev * dp_count, q_dev * dp_count
    if dp_count == 8 and mp_count == 4 and tok_dev % 128 == 0 and q_dev % 128 == 0 and cols % 2048 == 0 and (
            2 * tok_dev * seq_count == tokens and act_width == q_rows):
        moments, scores = store(*routed(
            act_in, grad_in, query_act, query_grad, act_basis, grad_basis, seq_lengths), seq_count)
        return moments, scores.T
    tile = min(256, cols)
    tiles = cols // tile
    chunks = min(4, tiles)
    far = [k for k in range(1, dp_count) if bin(k >> 1).count("1") >= 2]
    shared_train = far if tok_dev % (16 * mp_count) == 0 and dp_count <= 2 * tiles else []
    shared_query = far if q_dev % (16 * mp_count) == 0 and dp_count <= 2 * tiles else []
    steps = max(1, mp_count - 1)
    dma = pltpu.SemaphoreType.DMA
    any_space = pl.BlockSpec(memory_space=pl.ANY)
    bf16 = jnp.bfloat16
    raw, scores = pl.pallas_call(
        functools.partial(kernel, dp_count, mp_count, chunks, shared_train, shared_query),
        out_shape=(
            pltpu.VMEM((act_width, cols), jnp.float32),
            pltpu.VMEM((8, 128), jnp.float32),
        ),
        in_specs=[pl.BlockSpec(memory_space=pltpu.SMEM)] + [any_space] * 6,
        out_specs=(pl.BlockSpec(memory_space=pltpu.VMEM), pl.BlockSpec(memory_space=pltpu.VMEM)),
        scratch_shapes=[
            pltpu.VMEM((dp_count, tok_dev, act_width), bf16),
            pltpu.VMEM((dp_count, q_dev, act_width), bf16),
            pltpu.VMEM((dp_count, tok_dev, cols), bf16),
            pltpu.VMEM((dp_count, q_dev, cols), bf16),
            pltpu.VMEM(act_basis.shape, bf16),
            pltpu.VMEM(grad_basis.shape, bf16),
            pltpu.VMEM((act_width, tokens), bf16),
            pltpu.VMEM((q_rows, act_width), bf16),
            pltpu.VMEM((seq_count, tiles, act_width, tile), bf16),
            pltpu.VMEM((tiles, 8, tile), jnp.float32),
            pltpu.VMEM((seq_count, QUERIES, 8, 128), jnp.float32),
            dma((dp_count,)), dma((dp_count,)), dma((dp_count,)), dma((dp_count,)),
            dma((1, dp_count)), dma((1, dp_count)), dma((chunks, dp_count)), dma((chunks, dp_count)),
            dma((max(1, len(shared_train)), steps)), dma((max(1, len(shared_train)), steps)),
            dma((max(1, len(shared_query)), steps)), dma((max(1, len(shared_query)), steps)),
            dma((6,)), dma((tiles,)),
            pltpu.VMEM((dp_count, QUERIES, 128), jnp.float32),
            pltpu.VMEM((mp_count, QUERIES, 128), jnp.float32),
            dma((dp_count,)), dma((dp_count,)), dma((steps,)), dma((steps,)),
        ],
        compiler_params=pltpu.CompilerParams(
            collective_id=0, has_side_effects=True, vmem_limit_bytes=54 * 1024 * 1024),
    )(seq_lengths, act_in, grad_in, query_act, query_grad, act_basis, grad_basis)
    moments, scores = store(raw, scores, seq_count)
    return moments, scores.T


def store_kernel(raw, scores_in, moments, scores, sems):
    n = sems.shape[0]
    rows = raw.shape[0] // n
    copies = [pltpu.make_async_copy(raw.at[pl.ds(i * rows, rows)], moments.at[pl.ds(i * rows, rows)], sems.at[i])
              for i in range(n)]
    for c in copies:
        c.start()
    scores[...] = scores_in[:scores.shape[0], :scores.shape[1]]
    for c in copies:
        c.wait()


def store(raw, scores, seq_count):
    n = 8
    vm = pl.BlockSpec(memory_space=pltpu.VMEM)
    return pl.pallas_call(
        store_kernel,
        out_shape=(jax.ShapeDtypeStruct(raw.shape, raw.dtype), jax.ShapeDtypeStruct((seq_count, QUERIES), scores.dtype)),
        in_specs=[vm, vm], out_specs=(pl.BlockSpec(memory_space=pltpu.HBM), vm),
        scratch_shapes=[pltpu.SemaphoreType.DMA((n,))],
        compiler_params=pltpu.CompilerParams(vmem_limit_bytes=1024*1024),
    )(pltpu.with_memory_space_constraint(raw, pltpu.VMEM), pltpu.with_memory_space_constraint(scores, pltpu.VMEM))


def solution(mesh):
    return jax.shard_map(
        local,
        mesh=mesh,
        in_specs=(
            P("dp", "mp"),
            P("dp", None),
            P("dp", "mp"),
            P("dp", None),
            P("mp", None),
            P("dp", None),
            P(),
        ),
        out_specs=(P("mp", "dp"), P()),
        check_vma=False,
    )
```

```python
import functools
import itertools
import math

import jax
import jax.numpy as jnp
from jax import lax
from jax.experimental import pallas as pl
from jax.experimental.pallas import tpu as pltpu
from jax.sharding import PartitionSpec as P

D = 4096
FF = 16384
QUERIES = 64
QUERY_LEN = 16

damping = 0.1
MESH = pl.DeviceIdType.MESH


def flipped(index, mask):
    bit = 1
    while bit <= mask:
        if mask & bit:
            index = index + bit * (1 - 2 * ((index // bit) % 2))
        bit *= 2
    return index


def across(columns):
    square = jnp.concatenate([columns, jnp.zeros((128 - columns.shape[0], 128), jnp.float32)], axis=0)
    return square.T[:8, :]


def kernel(
    dp_count, mp_count, chunks, shared_train, shared_query,
    lengths, act_in, grad_in, query_act, query_grad, act_basis_in, grad_basis_in,
    moments, partial,
    act_raw, qact_raw, grad_raw, qgrad_raw, act_basis, grad_basis,
    act_t, q_rot, precond, staged, totals,
    act_send, act_recv, qact_send, qact_recv, grad_send, grad_recv, qgrad_send, qgrad_recv,
    pass_send, pass_recv, qpass_send, qpass_recv, local_sem, out_sem,
    shares, crossing, share_send, share_recv, cross_send, cross_recv,
):
    me = lax.axis_index("dp")
    mine = lax.axis_index("mp")
    seq_count = lengths.shape[0]
    tok_dev, act_width = act_in.shape
    q_dev = query_act.shape[0]
    cols = grad_raw.shape[2]
    block = act_basis_in.shape[1]
    tiles, _, tile = staged.shape
    tokens = tok_dev * dp_count
    seq_len = tokens // seq_count
    q_rows = q_dev * dp_count
    chunk_cols = cols // chunks
    masks = list(range(1, dp_count))
    peers = {k: flipped(me, k) for k in masks}

    barrier = pltpu.get_barrier_semaphore()
    for k in masks:
        pl.semaphore_signal(barrier, inc=1, device_id={"dp": peers[k], "mp": mine}, device_id_type=MESH)
    others = [lax.rem(mine + step, mp_count) for step in range(1, mp_count)]
    for other in others:
        pl.semaphore_signal(barrier, inc=1, device_id={"dp": me, "mp": other}, device_id_type=MESH)

    locals_in = [
        pltpu.make_async_copy(act_in, act_raw.at[me], local_sem.at[0]),
        pltpu.make_async_copy(act_basis_in, act_basis, local_sem.at[1]),
        pltpu.make_async_copy(grad_basis_in, grad_basis, local_sem.at[2]),
        pltpu.make_async_copy(
            grad_in.at[:, pl.ds(pl.multiple_of(me * cols, 128), cols)], grad_raw.at[me], local_sem.at[3]),
        pltpu.make_async_copy(query_act, qact_raw.at[me], local_sem.at[4]),
        pltpu.make_async_copy(
            query_grad.at[:, pl.ds(pl.multiple_of(me * cols, 128), cols)], qgrad_raw.at[me], local_sem.at[5]),
    ]
    for copy in locals_in:
        copy.start()
    pl.semaphore_wait(barrier, len(masks) + len(others))

    def remote(src, dst, send, recv, dp, mp):
        return pltpu.make_async_remote_copy(
            src_ref=src, dst_ref=dst, send_sem=send, recv_sem=recv,
            device_id={"dp": dp, "mp": mp}, device_id_type=MESH)

    sends = []

    def begin(copy):
        copy.start()
        sends.append(copy)

    act_masks = [k for k in masks if k == 1 or k % 2 == 0]

    def send_acts(src, raw, send, recv):
        for k in reversed(act_masks):
            begin(remote(src, raw.at[me], send.at[k], recv.at[k], peers[k], mine))

    def part_of(owner, rows):
        return pl.ds(pl.multiple_of(owner * (rows // mp_count), 16), rows // mp_count)

    def send_shared(src, raw, send, recv, shared):
        rows = part_of(mine, src.shape[0])
        for k in reversed(shared):
            there = pl.ds(pl.multiple_of(peers[k] * cols, 128), cols)
            begin(remote(
                src.at[rows, there], raw.at[me, rows, :], send.at[0, k], recv.at[0, k], peers[k], mine))

    def send_grads(src, raw, send, recv, shared, start, width, slot):
        for k in reversed(masks):
            if k not in shared:
                there = pl.ds(pl.multiple_of(peers[k] * cols + start, 128), width)
                begin(remote(
                    src.at[:, there], raw.at[me, :, pl.ds(start, width)],
                    send.at[slot, k], recv.at[slot, k], peers[k], mine))

    send_acts(act_in, act_raw, act_send, act_recv)
    send_shared(grad_in, grad_raw, grad_send, grad_recv, shared_train)
    send_shared(query_grad, qgrad_raw, qgrad_send, qgrad_recv, shared_query)
    send_grads(grad_in, grad_raw, grad_send, grad_recv, shared_train, 0, cols, 0)
    send_acts(query_act, qact_raw, qact_send, qact_recv)
    for c in range(chunks):
        send_grads(query_grad, qgrad_raw, qgrad_send, qgrad_recv, shared_query, c * chunk_cols, chunk_cols, c)

    def arrived(ref, send, recv):
        remote(ref, ref, send, recv, peers[1], mine).wait_recv()

    def relay_acts(raw, send, recv):
        for k in reversed(act_masks):
            arrived(raw.at[peers[k]], send.at[k], recv.at[k])
            if k > 1:
                here = raw.at[peers[k]]
                begin(remote(here, here, send.at[k + 1], recv.at[k + 1], peers[1], mine))

    def finish_acts(raw, send, recv):
        for k in masks:
            if k not in act_masks:
                arrived(raw.at[peers[k]], send.at[k], recv.at[k])

    def relay_grads(raw, send, recv, fsend, frecv, shared):
        for n, k in enumerate(reversed(shared)):
            here = raw.at[peers[k], part_of(mine, raw.shape[1]), :]
            arrived(here, send.at[0, k], recv.at[0, k])
            for step, other in enumerate(others):
                begin(remote(here, here, fsend.at[n, step], frecv.at[n, step], me, other))

    def finish_grads(raw, send, recv, shared, start, width, slot):
        for k in reversed(masks):
            if k not in shared:
                arrived(raw.at[peers[k], :, pl.ds(start, width)], send.at[slot, k], recv.at[slot, k])

    def finish_shared(raw, fsend, frecv, shared):
        for n, k in enumerate(reversed(shared)):
            for step in range(mp_count - 1):
                owner = lax.rem(mine + (mp_count - 1 - step), mp_count)
                arrived(
                    raw.at[peers[k], part_of(owner, raw.shape[1]), :], fsend.at[n, step], frecv.at[n, step])

    relay_acts(act_raw, act_send, act_recv)
    finish_acts(act_raw, act_send, act_recv)
    relay_grads(grad_raw, grad_send, grad_recv, pass_send, pass_recv, shared_train)
    relay_grads(qgrad_raw, qgrad_send, qgrad_recv, qpass_send, qpass_recv, shared_query)
    for copy in locals_in:
        copy.wait()

    limits = [lengths[s] for s in range(seq_count)]
    counted = limits[0]
    for s in range(1, seq_count):
        counted = counted + limits[s]
    inverse = 1.0 / jnp.full((1, tile), counted.astype(jnp.float32), jnp.float32)

    @pl.loop(0, dp_count)
    def _(e):
        where_tok = e * tok_dev + lax.broadcasted_iota(jnp.int32, (block, tok_dev), 1)
        live = jnp.zeros((block, tok_dev), jnp.float32)
        for s in range(seq_count):
            inside = (where_tok >= s * seq_len) & (where_tok < s * seq_len + limits[s])
            live = jnp.where(inside, 1.0, live)
        for b in range(act_width // block):
            span = pl.ds(b * block, block)
            turned = lax.dot_general(
                act_basis[span, :].T, act_raw[e, :, span], (((1,), (1,)), ((), ())),
                preferred_element_type=jnp.float32)
            act_t[span, pl.ds(pl.multiple_of(e * tok_dev, 128), tok_dev)] = (turned * live).astype(jnp.bfloat16)

    def wide_basis(jt):
        first = grad_basis[pl.ds(pl.multiple_of(jt * tile, 128), block), :]
        rows = []
        count = tile // block
        zero = jnp.zeros_like(first)
        for h in range(count):
            own = grad_basis[pl.ds(pl.multiple_of(jt * tile + h * block, 128), block), :]
            rows.append(jnp.concatenate([own if g == h else zero for g in range(count)], axis=1))
        return jnp.concatenate(rows, axis=0)

    def turned_grads(raw, jt, rows):
        span = pl.ds(pl.multiple_of(jt * tile, 128), tile)
        whole = raw[:, :, span].reshape(rows, tile)
        return jnp.dot(whole, wide_basis(jt), preferred_element_type=jnp.float32).astype(jnp.bfloat16)

    finish_shared(grad_raw, pass_send, pass_recv, shared_train)
    finish_grads(grad_raw, grad_send, grad_recv, shared_train, 0, cols, 0)

    def out_copy(jt):
        span = pl.ds(pl.multiple_of(jt * tile, 128), tile)
        return pltpu.make_async_copy(staged.at[jt], moments.at[:, span], out_sem.at[jt])

    per_chunk = tiles // chunks

    def first_phase(jt):
        grads = turned_grads(grad_raw, jt, tokens)
        total = jnp.zeros((act_width, tile), jnp.float32)
        for s in range(seq_count):
            a = act_t[:, s * seq_len:(s + 1) * seq_len]
            g = grads[s * seq_len:(s + 1) * seq_len, :]
            total = total + jnp.dot(a * a, g * g, preferred_element_type=jnp.float32)
        total = total * inverse
        moments[:, pl.ds(pl.multiple_of(jt * tile, 128), tile)] = total
        weights = 1.0 / (total + damping)
        for s in range(seq_count):
            a = act_t[:, s * seq_len:(s + 1) * seq_len]
            g = grads[s * seq_len:(s + 1) * seq_len, :]
            precond[s, jt] = (weights * jnp.dot(a, g, preferred_element_type=jnp.float32)).astype(jnp.bfloat16)

    half = tiles // 2
    pl.loop(0, half)(first_phase)
    relay_acts(qact_raw, qact_send, qact_recv)
    pl.loop(half, tiles)(first_phase)
    finish_acts(qact_raw, qact_send, qact_recv)

    @pl.loop(0, dp_count)
    def _(e):
        for b in range(act_width // block):
            span = pl.ds(b * block, block)
            turned = jnp.dot(qact_raw[e, :, span], act_basis[span, :], preferred_element_type=jnp.float32)
            q_rot[pl.ds(pl.multiple_of(e * q_dev, 16), q_dev), span] = turned.astype(jnp.bfloat16)

    totals[...] = jnp.zeros_like(totals)
    finish_shared(qgrad_raw, qpass_send, qpass_recv, shared_query)

    def second_phase(jt):
        grads = turned_grads(qgrad_raw, jt, q_rows).astype(jnp.float32)
        for s in range(seq_count):
            mapped = jnp.dot(q_rot[...], precond[s, jt], preferred_element_type=jnp.float32) * grads
            folded = mapped[:, :128]
            for h in range(1, tile // 128):
                folded = folded + mapped[:, h * 128:(h + 1) * 128]
            totals[s] += folded.reshape(QUERIES, q_rows // QUERIES // 8, 8, 128).sum(axis=1)

    for c in range(chunks):
        finish_grads(qgrad_raw, qgrad_send, qgrad_recv, shared_query, c * chunk_cols, chunk_cols, c)
        pl.loop(c * per_chunk, (c + 1) * per_chunk)(second_phase)

    lane = lax.broadcasted_iota(jnp.int32, (QUERIES, 128), 1)
    answer = jnp.zeros((QUERIES, 128), jnp.float32)
    for s in range(seq_count):
        row = jnp.sum(jnp.sum(totals[s], axis=1), axis=1, keepdims=True)
        answer = jnp.where(lane == s, row, answer)
    lens = jnp.ones((QUERIES, 128), jnp.float32)
    for s in range(seq_count):
        lens = jnp.where(lane == s, limits[s].astype(jnp.float32), lens)
    shares[me] = answer * lax.rsqrt(lens) / math.sqrt(QUERY_LEN * D * FF)

    for copy in sends:
        copy.wait_send()
    sends.clear()

    for k in masks:
        begin(remote(shares.at[me], shares.at[me], share_send.at[k], share_recv.at[k], peers[k], mine))
    for k in masks:
        arrived(shares.at[peers[k]], share_send.at[k], share_recv.at[k])
    summed = shares[0]
    for e in range(1, dp_count):
        summed = summed + shares[e]
    crossing[mine] = summed
    for step, other in enumerate(others):
        begin(remote(
            crossing.at[mine], crossing.at[mine], cross_send.at[step], cross_recv.at[step], me, other))
    for step in range(mp_count - 1):
        owner = lax.rem(mine + (mp_count - 1 - step), mp_count)
        arrived(crossing.at[owner], cross_send.at[step], cross_recv.at[step])
    summed = crossing[0]
    for e in range(1, mp_count):
        summed = summed + crossing[e]
    partial[...] = across(summed)
    for copy in sends:
        copy.wait_send()


NEAR = (2, 4, 3, 5)
FAR = (6, 7)
TRAIN_CUTS = (0, 2, 4, 6, 8)
QUERY_CUTS = (0, 1, 2, 3, 4, 5, 6, 7, 8)
TRAIN_SPLITS = ((5, 7), (5, 7), (5, 7), (5, 7))
PLAN = (
    ("lead", 0, 0),
    ("lead", 0, 1),
    ("acts", 0),
    ("trail", 0, 0),
    ("lead", 0, 2),
    ("side", 0),
    ("relay", 0, 0),
    ("relay", 0, 1),
    ("pass", 0),
    ("lead", 0, 3),
    ("trail", 0, 1),
    ("lead", 1, 0),
    ("trail", 0, 2),
    ("acts", 1),
    ("trail", 0, 3),
    ("lead", 1, 1),
    ("side", 1),
    ("relay", 0, 2),
    ("first", 0),
    ("all", 0),
    ("sided", 0),
    ("rest", 0, 0),
    ("tiles", 0, 0, 2),
    ("relay", 0, 3),
    ("rest", 0, 1),
    ("tiles", 0, 2, 4),
    ("relay", 1, 0),
    ("rest", 0, 2),
    ("tiles", 0, 4, 6),
    ("pass", 1),
    ("lead", 1, 2),
    ("trail", 1, 0),
    ("lead", 1, 3),
    ("trail", 1, 1),
    ("lead", 1, 4),
    ("trail", 1, 2),
    ("lead", 1, 5),
    ("trail", 1, 3),
    ("lead", 1, 6),
    ("trail", 1, 4),
    ("lead", 1, 7),
    ("trail", 1, 5),
    ("trail", 1, 6),
    ("trail", 1, 7),
    ("rest", 0, 3),
    ("tiles", 0, 6, 8),
    ("relay", 1, 1),
    ("first", 1),
    ("all", 1),
    ("sided", 1),
    ("relay", 1, 2),
    ("rest", 1, 0),
    ("tiles", 1, 0, 1),
    ("relay", 1, 3),
    ("rest", 1, 1),
    ("tiles", 1, 1, 2),
    ("relay", 1, 4),
    ("rest", 1, 2),
    ("tiles", 1, 2, 3),
    ("relay", 1, 5),
    ("rest", 1, 3),
    ("tiles", 1, 3, 4),
    ("relay", 1, 6),
    ("rest", 1, 4),
    ("tiles", 1, 4, 5),
    ("relay", 1, 7),
    ("rest", 1, 5),
    ("tiles", 1, 5, 6),
    ("rest", 1, 6),
    ("tiles", 1, 6, 7),
    ("rest", 1, 7),
    ("tiles", 1, 7, 8),
)
QUERY_SPLITS = ((5, 7), (5, 7), (4, 8), (4, 8), (4, 8), (3, 8), (3, 8), (3, 8))


def routed_kernel(
    lengths, act_in, grad_in, query_act, query_grad, act_basis_in, grad_basis_in,
    moments, partial,
    act_raw, qact_raw, grad_raw, qgrad_raw, act_basis, grad_basis,
    act_t, act_sq, q_rot, precond, totals, shares,
    act_send, act_recv, grad_send, lead_recv, rest_recv, side_send, side_recv, local_sem,
    share_send, share_recv, ready,
):
    me = lax.axis_index("dp")
    mine = lax.axis_index("mp")
    dp_count = lax.axis_size("dp")
    mp_count = lax.axis_size("mp")
    tok_dev, act_width = act_in.shape
    seq_count = lengths.shape[0]
    q_dev = query_act.shape[0]
    cols = grad_raw.shape[1]
    block = act_basis.shape[1]
    tile = cols // TRAIN_CUTS[-1]
    tokens = tok_dev * dp_count
    seq_len = tokens // seq_count
    q_rows = q_dev * dp_count
    masks = list(range(1, dp_count))
    peers = {k: flipped(me, k) for k in masks}
    others = [lax.rem(mine + step, mp_count) for step in range(1, mp_count)]

    is_end = (mine == 0) | (mine == mp_count - 1)
    is_mid = jnp.logical_not(is_end)
    partner = flipped(mine, 1)
    half = lax.rem(mine + 1, 2)
    far_planes = [partner, mp_count - 1 - mine, mp_count - 1 - partner]

    barrier = pltpu.get_barrier_semaphore()
    for k in masks:
        pl.semaphore_signal(barrier, inc=1, device_id={"dp": peers[k], "mp": mine}, device_id_type=MESH)
    for other in others:
        pl.semaphore_signal(barrier, inc=1, device_id={"dp": me, "mp": other}, device_id_type=MESH)

    own = pl.ds(pl.multiple_of(me * cols, 128), cols)
    own_tok = pl.ds(pl.multiple_of(me * tok_dev, 128), tok_dev)
    own_q = pl.ds(pl.multiple_of(me * q_dev, 128), q_dev)
    locals_in = [
        pltpu.make_async_copy(act_in, act_raw.at[own_tok], local_sem.at[0]),
        pltpu.make_async_copy(act_basis_in, act_basis, local_sem.at[1]),
        pltpu.make_async_copy(grad_basis_in, grad_basis, local_sem.at[2]),
        pltpu.make_async_copy(grad_in.at[:, own], grad_raw.at[own_tok], local_sem.at[3]),
        pltpu.make_async_copy(query_act, qact_raw.at[own_q], local_sem.at[4]),
        pltpu.make_async_copy(query_grad.at[:, own], qgrad_raw.at[own_q], local_sem.at[5]),
    ]
    for copy in locals_in:
        copy.start()
    pl.semaphore_wait(barrier, len(masks) + len(others))

    def remote(src, dst, send, recv, dp, mp):
        return pltpu.make_async_remote_copy(
            src_ref=src, dst_ref=dst, send_sem=send, recv_sem=recv,
            device_id={"dp": dp, "mp": mp}, device_id_type=MESH)

    def arrived(ref, recv):
        remote(ref, ref, side_send.at[0], recv, peers[1], mine).wait_recv()

    def left(ref, send):
        remote(ref, ref, send, side_recv.at[0], peers[1], mine).wait_send()

    def by_role(act):
        @pl.when(is_end)
        def _():
            act("end")

        @pl.when(is_mid)
        def _():
            act("mid")

    phases = (
        (grad_in, grad_raw, tok_dev, TRAIN_CUTS, TRAIN_SPLITS),
        (query_grad, qgrad_raw, q_dev, QUERY_CUTS, QUERY_SPLITS),
    )

    def span_of(phase, c):
        cuts = phases[phase][3]
        return cuts[c] * tile, (cuts[c + 1] - cuts[c]) * tile

    def count_of(phase, part, c):
        first, second = phases[phase][4][c]
        eighth = phases[phase][2] // 8
        return {"a": first, "b": second - first, "c": 8 - second, "own": 4}[part] * eighth

    def rows_of(phase, part, c):
        first, second = phases[phase][4][c]
        eighth = phases[phase][2] // 8
        low = {"a": 0, "b": first, "c": second, "own": half * 4}[part]
        return low * eighth, count_of(phase, part, c)

    def held(phase, k, part, c):
        start, width = span_of(phase, c)
        low, rows = rows_of(phase, part, c)
        here = pl.ds(pl.multiple_of(peers[k] * phases[phase][2] + low, 16), rows)
        return phases[phase][1].at[here, pl.ds(start, width)]

    def bulk(phase, rows, c):
        start, width = span_of(phase, c)
        return phases[phase][1].at[pl.ds(0, rows), pl.ds(start, width)]

    def hop(phase, part, c, ks, recv):
        src, raw, size, _, _ = phases[phase]
        start, width = span_of(phase, c)
        low, rows = rows_of(phase, part, c)
        if not rows:
            return
        taken = pl.ds(pl.multiple_of(low, 16), rows)
        put = pl.ds(pl.multiple_of(me * size + low, 16), rows)
        for k in ks:
            there = pl.ds(pl.multiple_of(peers[k] * cols + start, 128), width)
            remote(
                src.at[taken, there], raw.at[put, pl.ds(start, width)],
                grad_send.at[phase, c], recv, peers[k], mine).start()

    def lead(role, phase, c):
        if role == "end":
            hop(phase, "a", c, NEAR[:2], lead_recv.at[phase, c, 0])
            hop(phase, "a", c, NEAR[2:], lead_recv.at[phase, c, 1])
        else:
            hop(phase, "own", c, FAR, lead_recv.at[phase, c, 0])
            hop(phase, "c", c, NEAR, lead_recv.at[phase, c, 1])

    def trail(role, phase, c):
        hop(phase, "b", c, NEAR, rest_recv.at[phase, c])

    def relay(role, phase, c):
        def onward(k, part, to):
            here = held(phase, k, part, c)
            remote(here, here, grad_send.at[phase, c], rest_recv.at[phase, c], me, to).start()

        if role == "end":
            for g, ks in enumerate((NEAR[:2], NEAR[2:])):
                arrived(bulk(phase, 2 * count_of(phase, "a", c), c), lead_recv.at[phase, c, g])
                for k in ks:
                    onward(k, "a", partner)
        else:
            arrived(bulk(phase, 2 * count_of(phase, "own", c), c), lead_recv.at[phase, c, 0])
            for to in far_planes:
                for k in FAR:
                    onward(k, "own", to)
            if count_of(phase, "c", c):
                arrived(bulk(phase, 4 * count_of(phase, "c", c), c), lead_recv.at[phase, c, 1])
                for k in NEAR:
                    onward(k, "c", partner)

    def rest(role, phase, c):
        a, b, d, own_half = [count_of(phase, part, c) for part in ("a", "b", "c", "own")]
        rows = 4 * (b + d) + 4 * own_half if role == "end" else 4 * (a + b) + 2 * own_half
        arrived(bulk(phase, rows, c), rest_recv.at[phase, c])

    def gone(role, phase):
        for c in range(len(phases[phase][4])):
            a, b, d, own_half = [count_of(phase, part, c) for part in ("a", "b", "c", "own")]
            rows = 4 * (a + b) + 4 * a if role == "end" else 4 * (b + d) + 2 * own_half + 6 * own_half + 4 * d
            left(bulk(phase, rows, c), grad_send.at[phase, c])

    def side(phase):
        src, raw, size, _, _ = phases[phase]
        there = pl.ds(pl.multiple_of(peers[1] * cols, 128), cols)
        put = pl.ds(pl.multiple_of(me * size, 128), size)
        remote(src.at[:, there], raw.at[put], side_send.at[phase], side_recv.at[phase], peers[1], mine).start()

    def finish_side(phase):
        arrived(phases[phase][1].at[pl.ds(0, phases[phase][2])], side_recv.at[phase])

    acts = ((act_in, act_raw, tok_dev), (query_act, qact_raw, q_dev))

    def act_rows(phase, k, low, rows):
        size = acts[phase][2]
        return acts[phase][1].at[pl.ds(pl.multiple_of(peers[k] * size + low, 16), rows)]

    def act_go(phase, src, dst, recv_slot, k):
        remote(src, dst, act_send.at[phase], act_recv.at[phase, recv_slot], peers[k], mine).start()

    def send_acts(phase):
        src, raw, size = acts[phase]
        put = raw.at[pl.ds(pl.multiple_of(me * size, 16), size)]
        for k, slot in ((2, 0), (4, 1), (1, 3)):
            act_go(phase, src, put, slot, k)

    def pass_acts(phase):
        _, raw, size = acts[phase]
        for n, (k, onward) in enumerate(((2, 4), (4, 2))):
            arrived(raw.at[pl.ds(0, size)], act_recv.at[phase, n])
            part = act_rows(phase, k, n * (size // 2), size // 2)
            act_go(phase, part, part, 2, onward)
        for k in (2, 4):
            whole = act_rows(phase, k, 0, size)
            act_go(phase, whole, whole, 3, 1)

    def finish_acts(phase):
        _, raw, size = acts[phase]
        arrived(raw.at[pl.ds(0, size)], act_recv.at[phase, 2])
        whole = act_rows(phase, 6, 0, size)
        act_go(phase, whole, whole, 4, 1)

    def near_acts(phase):
        _, raw, size = acts[phase]
        arrived(raw.at[pl.ds(0, 3 * size)], act_recv.at[phase, 3])

    def last_acts(phase):
        _, raw, size = acts[phase]
        arrived(raw.at[pl.ds(0, size)], act_recv.at[phase, 4])

    def acts_gone(phase):
        _, raw, size = acts[phase]
        left(raw.at[pl.ds(0, 7 * size)], act_send.at[phase])

    for other in others:
        pl.semaphore_signal(ready, inc=1, device_id={"dp": me, "mp": other}, device_id_type=MESH)

    limits = [lengths[s] for s in range(seq_count)]
    counted = limits[0]
    for s in range(1, seq_count):
        counted = counted + limits[s]
    inverse = 1.0 / jnp.full((1, tile), counted.astype(jnp.float32), jnp.float32)

    def chip_rows(p, rows):
        place, result = 1, 0
        chip = lax.div(me, 2)
        while place < dp_count // 2:
            result = result + place * lax.rem(lax.div(chip, place) + lax.div(p, place), 2)
            place *= 2
        return result * rows

    def wide(basis, start, count):
        rows = []
        zero = jnp.zeros((block, block), jnp.bfloat16)
        for h in range(count):
            piece = basis[pl.ds(start + h * block, block), :]
            rows.append(jnp.concatenate([piece if g == h else zero for g in range(count)], axis=1))
        return jnp.concatenate(rows, axis=0)

    def turn_acts(low, high):
        rows = 2 * tok_dev

        @pl.loop(low // 2, high // 2)
        def _(p):
            first = chip_rows(p, rows)
            where_tok = first + lax.broadcasted_iota(jnp.int32, (2 * block, rows), 1)
            live = jnp.zeros((2 * block, rows), jnp.float32)
            for s in range(seq_count):
                inside = (where_tok >= s * seq_len) & (where_tok < s * seq_len + limits[s])
                live = jnp.where(inside, 1.0, live)
            to = pl.ds(pl.multiple_of(first, 128), rows)
            for b in range(act_width // (2 * block)):
                span = pl.ds(b * 2 * block, 2 * block)
                turned = lax.dot_general(
                    wide(act_basis, b * 2 * block, 2).T, act_raw[to, span], (((1,), (1,)), ((), ())),
                    preferred_element_type=jnp.float32)
                kept = (turned * live).astype(jnp.bfloat16)
                act_t[span, to] = kept
                act_sq[span, to] = kept * kept

    def turn_query_acts(low, high):
        rows = 2 * q_dev

        @pl.loop(low // 2, high // 2)
        def _(p):
            here = pl.ds(pl.multiple_of(chip_rows(p, rows), 128), rows)
            for b in range(act_width // (2 * block)):
                span = pl.ds(b * 2 * block, 2 * block)
                turned = jnp.dot(
                    qact_raw[here, span], wide(act_basis, b * 2 * block, 2), preferred_element_type=jnp.float32)
                q_rot[here, span] = turned.astype(jnp.bfloat16)

    def turned_grads(raw, jt):
        start = pl.multiple_of(jt * tile, 128)
        whole = raw[:, pl.ds(start, tile)]
        return jnp.dot(
            whole, wide(grad_basis, start, tile // block), preferred_element_type=jnp.float32).astype(jnp.bfloat16)

    def train_tile(jt):
        grads = turned_grads(grad_raw, jt)
        total = jnp.dot(act_sq[...], grads * grads, preferred_element_type=jnp.float32) * inverse
        moments[:, pl.ds(pl.multiple_of(jt * tile, 128), tile)] = total
        weights = 1.0 / (total + damping)
        for s in range(seq_count):
            a = act_t[:, s * seq_len:(s + 1) * seq_len]
            g = grads[s * seq_len:(s + 1) * seq_len, :]
            precond[s, :, pl.ds(pl.multiple_of(jt * tile, 128), tile)] = (
                weights * jnp.dot(a, g, preferred_element_type=jnp.float32)).astype(jnp.bfloat16)

    def query_tiles(low, high):
        grads = [turned_grads(qgrad_raw, jt).astype(jnp.float32) for jt in range(low, high)]
        grads = jnp.concatenate(grads, axis=1)
        for s in range(seq_count):
            weights = precond[s, :, pl.ds(low * tile, (high - low) * tile)]
            mapped = jnp.dot(q_rot[...], weights, preferred_element_type=jnp.float32) * grads
            folded = mapped[:, :128]
            for h in range(1, mapped.shape[1] // 128):
                folded = folded + mapped[:, h * 128:(h + 1) * 128]
            totals[s] += folded.reshape(QUERIES, q_rows // QUERIES // 8, 8, 128).sum(axis=1)

    turn = (turn_acts, turn_query_acts)

    def first_acts(phase):
        near_acts(phase)
        if phase == 0:
            for copy in locals_in:
                copy.wait()
            totals[...] = jnp.zeros_like(totals)
        turn[phase](0, 6)

    def all_acts(phase):
        finish_acts(phase)
        last_acts(phase)
        turn[phase](6, dp_count)

    def tiles_now(phase, low, high):
        if phase:
            query_tiles(low, high)
        else:
            pl.loop(low, high)(train_tile)

    by_roles = {"lead": lead, "trail": trail, "relay": relay, "rest": rest}
    plain = {
        "acts": send_acts, "pass": pass_acts, "first": first_acts, "all": all_acts,
        "side": side, "sided": finish_side, "tiles": tiles_now}
    for shared, group in itertools.groupby(PLAN, lambda step: step[0] in by_roles):
        group = list(group)
        if shared:
            by_role(lambda role: [by_roles[name](role, *where) for name, *where in group])
        else:
            for name, *where in group:
                plain[name](*where)

    lane = lax.broadcasted_iota(jnp.int32, (QUERIES, 128), 1)
    answer = jnp.zeros((QUERIES, 128), jnp.float32)
    for s in range(seq_count):
        row = jnp.sum(jnp.sum(totals[s], axis=1), axis=1, keepdims=True)
        answer = jnp.where(lane == s, row, answer)
    lens = jnp.ones((QUERIES, 128), jnp.float32)
    for s in range(seq_count):
        lens = jnp.where(lane == s, limits[s].astype(jnp.float32), lens)
    slot = mine * dp_count + me
    shares[slot] = across(answer * lax.rsqrt(lens) / math.sqrt(QUERY_LEN * D * FF))

    pl.semaphore_wait(ready, len(others))
    mine_there = shares.at[slot]
    for step in reversed(range(mp_count)):
        plane = lax.rem(mine + step, mp_count)
        for k in reversed(range(dp_count)):
            if k or step:
                remote(
                    mine_there, mine_there, share_send.at[0], share_recv.at[0],
                    peers[k] if k else me, plane).start()

    def ended(role):
        gone(role, 0)
        gone(role, 1)

    by_role(ended)
    for phase in range(2):
        acts_gone(phase)
        left(phases[phase][1].at[pl.ds(0, phases[phase][2])], side_send.at[phase])
    every = shares.at[pl.ds(0, dp_count * mp_count - 1)]
    left(every, share_send.at[0])
    arrived(every, share_recv.at[0])
    summed = shares[0]
    for e in range(1, dp_count * mp_count):
        summed = summed + shares[e]
    partial[...] = summed


def routed(act_in, grad_in, query_act, query_grad, act_basis, grad_basis, seq_lengths):
    dp_count = lax.axis_size("dp")
    mp_count = lax.axis_size("mp")
    tok_dev, act_width = act_in.shape
    q_dev = query_act.shape[0]
    cols = grad_in.shape[1] // dp_count
    seq_count = seq_lengths.shape[0]
    tokens, q_rows = tok_dev * dp_count, q_dev * dp_count
    dma = pltpu.SemaphoreType.DMA
    any_space = pl.BlockSpec(memory_space=pl.ANY)
    bf16 = jnp.bfloat16
    chunks = max(len(TRAIN_SPLITS), len(QUERY_SPLITS))
    return pl.pallas_call(
        routed_kernel,
        out_shape=(
            pltpu.VMEM((act_width, cols), jnp.float32),
            pltpu.VMEM((8, 128), jnp.float32),
        ),
        in_specs=[pl.BlockSpec(memory_space=pltpu.SMEM)] + [any_space] * 6,
        out_specs=(pl.BlockSpec(memory_space=pltpu.VMEM), pl.BlockSpec(memory_space=pltpu.VMEM)),
        scratch_shapes=[
            pltpu.VMEM((tokens, act_width), bf16),
            pltpu.VMEM((q_rows, act_width), bf16),
            pltpu.VMEM((tokens, cols), bf16),
            pltpu.VMEM((q_rows, cols), bf16),
            pltpu.VMEM(act_basis.shape, bf16),
            pltpu.VMEM((cols, grad_basis.shape[1]), bf16),
            pltpu.VMEM((act_width, tokens), bf16),
            pltpu.VMEM((act_width, tokens), bf16),
            pltpu.VMEM((q_rows, act_width), bf16),
            pltpu.VMEM((seq_count, act_width, cols), bf16),
            pltpu.VMEM((seq_count, QUERIES, 8, 128), jnp.float32),
            pltpu.VMEM((dp_count * mp_count, 8, 128), jnp.float32),
            dma((2,)), dma((2, 5)), dma((2, chunks)), dma((2, chunks, 2)), dma((2, chunks)),
            dma((2,)), dma((2,)), dma((6,)), dma((1,)), dma((1,)), pltpu.SemaphoreType.REGULAR,
        ],
        compiler_params=pltpu.CompilerParams(
            collective_id=1, has_side_effects=True, vmem_limit_bytes=54 * 1024 * 1024),
    )(seq_lengths, act_in, grad_in, query_act, query_grad, act_basis, grad_basis)


def local(act_in, grad_in, query_act, query_grad, act_basis, grad_basis, seq_lengths):
    dp_count = lax.axis_size("dp")
    mp_count = lax.axis_size("mp")
    tok_dev, act_width = act_in.shape
    q_dev = query_act.shape[0]
    cols = grad_in.shape[1] // dp_count
    seq_count = seq_lengths.shape[0]
    tokens, q_rows = tok_dev * dp_count, q_dev * dp_count
    if dp_count == 8 and mp_count == 4 and tok_dev % 128 == 0 and q_dev % 128 == 0 and cols % 2048 == 0 and (
            2 * tok_dev * seq_count == tokens and act_width == q_rows):
        moments, scores = store(*routed(
            act_in, grad_in, query_act, query_grad, act_basis, grad_basis, seq_lengths), seq_count)
        return moments, scores.T
    tile = min(256, cols)
    tiles = cols // tile
    chunks = min(4, tiles)
    far = [k for k in range(1, dp_count) if bin(k >> 1).count("1") >= 2]
    shared_train = far if tok_dev % (16 * mp_count) == 0 and dp_count <= 2 * tiles else []
    shared_query = far if q_dev % (16 * mp_count) == 0 and dp_count <= 2 * tiles else []
    steps = max(1, mp_count - 1)
    dma = pltpu.SemaphoreType.DMA
    any_space = pl.BlockSpec(memory_space=pl.ANY)
    bf16 = jnp.bfloat16
    raw, scores = pl.pallas_call(
        functools.partial(kernel, dp_count, mp_count, chunks, shared_train, shared_query),
        out_shape=(
            pltpu.VMEM((act_width, cols), jnp.float32),
            pltpu.VMEM((8, 128), jnp.float32),
        ),
        in_specs=[pl.BlockSpec(memory_space=pltpu.SMEM)] + [any_space] * 6,
        out_specs=(pl.BlockSpec(memory_space=pltpu.VMEM), pl.BlockSpec(memory_space=pltpu.VMEM)),
        scratch_shapes=[
            pltpu.VMEM((dp_count, tok_dev, act_width), bf16),
            pltpu.VMEM((dp_count, q_dev, act_width), bf16),
            pltpu.VMEM((dp_count, tok_dev, cols), bf16),
            pltpu.VMEM((dp_count, q_dev, cols), bf16),
            pltpu.VMEM(act_basis.shape, bf16),
            pltpu.VMEM(grad_basis.shape, bf16),
            pltpu.VMEM((act_width, tokens), bf16),
            pltpu.VMEM((q_rows, act_width), bf16),
            pltpu.VMEM((seq_count, tiles, act_width, tile), bf16),
            pltpu.VMEM((tiles, 8, tile), jnp.float32),
            pltpu.VMEM((seq_count, QUERIES, 8, 128), jnp.float32),
            dma((dp_count,)), dma((dp_count,)), dma((dp_count,)), dma((dp_count,)),
            dma((1, dp_count)), dma((1, dp_count)), dma((chunks, dp_count)), dma((chunks, dp_count)),
            dma((max(1, len(shared_train)), steps)), dma((max(1, len(shared_train)), steps)),
            dma((max(1, len(shared_query)), steps)), dma((max(1, len(shared_query)), steps)),
            dma((6,)), dma((tiles,)),
            pltpu.VMEM((dp_count, QUERIES, 128), jnp.float32),
            pltpu.VMEM((mp_count, QUERIES, 128), jnp.float32),
            dma((dp_count,)), dma((dp_count,)), dma((steps,)), dma((steps,)),
        ],
        compiler_params=pltpu.CompilerParams(
            collective_id=0, has_side_effects=True, vmem_limit_bytes=54 * 1024 * 1024),
    )(seq_lengths, act_in, grad_in, query_act, query_grad, act_basis, grad_basis)
    moments, scores = store(raw, scores, seq_count)
    return moments, scores.T


def store_kernel(raw, scores_in, moments, scores, sems):
    n = sems.shape[0]
    rows = raw.shape[0] // n
    copies = [pltpu.make_async_copy(raw.at[pl.ds(i * rows, rows)], moments.at[pl.ds(i * rows, rows)], sems.at[i])
              for i in range(n)]
    for c in copies:
        c.start()
    scores[...] = scores_in[:scores.shape[0], :scores.shape[1]]
    for c in copies:
        c.wait()


def store(raw, scores, seq_count):
    n = 8
    vm = pl.BlockSpec(memory_space=pltpu.VMEM)
    return pl.pallas_call(
        store_kernel,
        out_shape=(jax.ShapeDtypeStruct(raw.shape, raw.dtype), jax.ShapeDtypeStruct((seq_count, QUERIES), scores.dtype)),
        in_specs=[vm, vm], out_specs=(pl.BlockSpec(memory_space=pltpu.HBM), vm),
        scratch_shapes=[pltpu.SemaphoreType.DMA((n,))],
        compiler_params=pltpu.CompilerParams(vmem_limit_bytes=1024*1024),
    )(pltpu.with_memory_space_constraint(raw, pltpu.VMEM), pltpu.with_memory_space_constraint(scores, pltpu.VMEM))


def solution(mesh):
    return jax.shard_map(
        local,
        mesh=mesh,
        in_specs=(
            P("dp", "mp"),
            P("dp", None),
            P("dp", "mp"),
            P("dp", None),
            P("mp", None),
            P("dp", None),
            P(),
        ),
        out_specs=(P("mp", "dp"), P()),
        check_vma=False,
    )
```

```python
import functools
import itertools
import math

import jax
import jax.numpy as jnp
from jax import lax
from jax.experimental import pallas as pl
from jax.experimental.pallas import tpu as pltpu
from jax.sharding import PartitionSpec as P

D = 4096
FF = 16384
QUERIES = 64
QUERY_LEN = 16

damping = 0.1
MESH = pl.DeviceIdType.MESH


def flipped(index, mask):
    bit = 1
    while bit <= mask:
        if mask & bit:
            index = index + bit * (1 - 2 * ((index // bit) % 2))
        bit *= 2
    return index


def across(columns):
    square = jnp.concatenate([columns, jnp.zeros((128 - columns.shape[0], 128), jnp.float32)], axis=0)
    return square.T[:8, :]


def kernel(
    dp_count, mp_count, chunks, shared_train, shared_query,
    lengths, act_in, grad_in, query_act, query_grad, act_basis_in, grad_basis_in,
    moments, partial,
    act_raw, qact_raw, grad_raw, qgrad_raw, act_basis, grad_basis,
    act_t, q_rot, precond, staged, totals,
    act_send, act_recv, qact_send, qact_recv, grad_send, grad_recv, qgrad_send, qgrad_recv,
    pass_send, pass_recv, qpass_send, qpass_recv, local_sem, out_sem,
    shares, crossing, share_send, share_recv, cross_send, cross_recv,
):
    me = lax.axis_index("dp")
    mine = lax.axis_index("mp")
    seq_count = lengths.shape[0]
    tok_dev, act_width = act_in.shape
    q_dev = query_act.shape[0]
    cols = grad_raw.shape[2]
    block = act_basis_in.shape[1]
    tiles, _, tile = staged.shape
    tokens = tok_dev * dp_count
    seq_len = tokens // seq_count
    q_rows = q_dev * dp_count
    chunk_cols = cols // chunks
    masks = list(range(1, dp_count))
    peers = {k: flipped(me, k) for k in masks}

    barrier = pltpu.get_barrier_semaphore()
    for k in masks:
        pl.semaphore_signal(barrier, inc=1, device_id={"dp": peers[k], "mp": mine}, device_id_type=MESH)
    others = [lax.rem(mine + step, mp_count) for step in range(1, mp_count)]
    for other in others:
        pl.semaphore_signal(barrier, inc=1, device_id={"dp": me, "mp": other}, device_id_type=MESH)

    locals_in = [
        pltpu.make_async_copy(act_in, act_raw.at[me], local_sem.at[0]),
        pltpu.make_async_copy(act_basis_in, act_basis, local_sem.at[1]),
        pltpu.make_async_copy(grad_basis_in, grad_basis, local_sem.at[2]),
        pltpu.make_async_copy(
            grad_in.at[:, pl.ds(pl.multiple_of(me * cols, 128), cols)], grad_raw.at[me], local_sem.at[3]),
        pltpu.make_async_copy(query_act, qact_raw.at[me], local_sem.at[4]),
        pltpu.make_async_copy(
            query_grad.at[:, pl.ds(pl.multiple_of(me * cols, 128), cols)], qgrad_raw.at[me], local_sem.at[5]),
    ]
    for copy in locals_in:
        copy.start()
    pl.semaphore_wait(barrier, len(masks) + len(others))

    def remote(src, dst, send, recv, dp, mp):
        return pltpu.make_async_remote_copy(
            src_ref=src, dst_ref=dst, send_sem=send, recv_sem=recv,
            device_id={"dp": dp, "mp": mp}, device_id_type=MESH)

    sends = []

    def begin(copy):
        copy.start()
        sends.append(copy)

    act_masks = [k for k in masks if k == 1 or k % 2 == 0]

    def send_acts(src, raw, send, recv):
        for k in reversed(act_masks):
            begin(remote(src, raw.at[me], send.at[k], recv.at[k], peers[k], mine))

    def part_of(owner, rows):
        return pl.ds(pl.multiple_of(owner * (rows // mp_count), 16), rows // mp_count)

    def send_shared(src, raw, send, recv, shared):
        rows = part_of(mine, src.shape[0])
        for k in reversed(shared):
            there = pl.ds(pl.multiple_of(peers[k] * cols, 128), cols)
            begin(remote(
                src.at[rows, there], raw.at[me, rows, :], send.at[0, k], recv.at[0, k], peers[k], mine))

    def send_grads(src, raw, send, recv, shared, start, width, slot):
        for k in reversed(masks):
            if k not in shared:
                there = pl.ds(pl.multiple_of(peers[k] * cols + start, 128), width)
                begin(remote(
                    src.at[:, there], raw.at[me, :, pl.ds(start, width)],
                    send.at[slot, k], recv.at[slot, k], peers[k], mine))

    send_acts(act_in, act_raw, act_send, act_recv)
    send_shared(grad_in, grad_raw, grad_send, grad_recv, shared_train)
    send_shared(query_grad, qgrad_raw, qgrad_send, qgrad_recv, shared_query)
    send_grads(grad_in, grad_raw, grad_send, grad_recv, shared_train, 0, cols, 0)
    send_acts(query_act, qact_raw, qact_send, qact_recv)
    for c in range(chunks):
        send_grads(query_grad, qgrad_raw, qgrad_send, qgrad_recv, shared_query, c * chunk_cols, chunk_cols, c)

    def arrived(ref, send, recv):
        remote(ref, ref, send, recv, peers[1], mine).wait_recv()

    def relay_acts(raw, send, recv):
        for k in reversed(act_masks):
            arrived(raw.at[peers[k]], send.at[k], recv.at[k])
            if k > 1:
                here = raw.at[peers[k]]
                begin(remote(here, here, send.at[k + 1], recv.at[k + 1], peers[1], mine))

    def finish_acts(raw, send, recv):
        for k in masks:
            if k not in act_masks:
                arrived(raw.at[peers[k]], send.at[k], recv.at[k])

    def relay_grads(raw, send, recv, fsend, frecv, shared):
        for n, k in enumerate(reversed(shared)):
            here = raw.at[peers[k], part_of(mine, raw.shape[1]), :]
            arrived(here, send.at[0, k], recv.at[0, k])
            for step, other in enumerate(others):
                begin(remote(here, here, fsend.at[n, step], frecv.at[n, step], me, other))

    def finish_grads(raw, send, recv, shared, start, width, slot):
        for k in reversed(masks):
            if k not in shared:
                arrived(raw.at[peers[k], :, pl.ds(start, width)], send.at[slot, k], recv.at[slot, k])

    def finish_shared(raw, fsend, frecv, shared):
        for n, k in enumerate(reversed(shared)):
            for step in range(mp_count - 1):
                owner = lax.rem(mine + (mp_count - 1 - step), mp_count)
                arrived(
                    raw.at[peers[k], part_of(owner, raw.shape[1]), :], fsend.at[n, step], frecv.at[n, step])

    relay_acts(act_raw, act_send, act_recv)
    finish_acts(act_raw, act_send, act_recv)
    relay_grads(grad_raw, grad_send, grad_recv, pass_send, pass_recv, shared_train)
    relay_grads(qgrad_raw, qgrad_send, qgrad_recv, qpass_send, qpass_recv, shared_query)
    for copy in locals_in:
        copy.wait()

    limits = [lengths[s] for s in range(seq_count)]
    counted = limits[0]
    for s in range(1, seq_count):
        counted = counted + limits[s]
    inverse = 1.0 / jnp.full((1, tile), counted.astype(jnp.float32), jnp.float32)

    @pl.loop(0, dp_count)
    def _(e):
        where_tok = e * tok_dev + lax.broadcasted_iota(jnp.int32, (block, tok_dev), 1)
        live = jnp.zeros((block, tok_dev), jnp.float32)
        for s in range(seq_count):
            inside = (where_tok >= s * seq_len) & (where_tok < s * seq_len + limits[s])
            live = jnp.where(inside, 1.0, live)
        for b in range(act_width // block):
            span = pl.ds(b * block, block)
            turned = lax.dot_general(
                act_basis[span, :].T, act_raw[e, :, span], (((1,), (1,)), ((), ())),
                preferred_element_type=jnp.float32)
            act_t[span, pl.ds(pl.multiple_of(e * tok_dev, 128), tok_dev)] = (turned * live).astype(jnp.bfloat16)

    def wide_basis(jt):
        first = grad_basis[pl.ds(pl.multiple_of(jt * tile, 128), block), :]
        rows = []
        count = tile // block
        zero = jnp.zeros_like(first)
        for h in range(count):
            own = grad_basis[pl.ds(pl.multiple_of(jt * tile + h * block, 128), block), :]
            rows.append(jnp.concatenate([own if g == h else zero for g in range(count)], axis=1))
        return jnp.concatenate(rows, axis=0)

    def turned_grads(raw, jt, rows):
        span = pl.ds(pl.multiple_of(jt * tile, 128), tile)
        whole = raw[:, :, span].reshape(rows, tile)
        return jnp.dot(whole, wide_basis(jt), preferred_element_type=jnp.float32).astype(jnp.bfloat16)

    finish_shared(grad_raw, pass_send, pass_recv, shared_train)
    finish_grads(grad_raw, grad_send, grad_recv, shared_train, 0, cols, 0)

    def out_copy(jt):
        span = pl.ds(pl.multiple_of(jt * tile, 128), tile)
        return pltpu.make_async_copy(staged.at[jt], moments.at[:, span], out_sem.at[jt])

    per_chunk = tiles // chunks

    def first_phase(jt):
        grads = turned_grads(grad_raw, jt, tokens)
        total = jnp.zeros((act_width, tile), jnp.float32)
        for s in range(seq_count):
            a = act_t[:, s * seq_len:(s + 1) * seq_len]
            g = grads[s * seq_len:(s + 1) * seq_len, :]
            total = total + jnp.dot(a * a, g * g, preferred_element_type=jnp.float32)
        total = total * inverse
        moments[:, pl.ds(pl.multiple_of(jt * tile, 128), tile)] = total
        weights = 1.0 / (total + damping)
        for s in range(seq_count):
            a = act_t[:, s * seq_len:(s + 1) * seq_len]
            g = grads[s * seq_len:(s + 1) * seq_len, :]
            precond[s, jt] = (weights * jnp.dot(a, g, preferred_element_type=jnp.float32)).astype(jnp.bfloat16)

    half = tiles // 2
    pl.loop(0, half)(first_phase)
    relay_acts(qact_raw, qact_send, qact_recv)
    pl.loop(half, tiles)(first_phase)
    finish_acts(qact_raw, qact_send, qact_recv)

    @pl.loop(0, dp_count)
    def _(e):
        for b in range(act_width // block):
            span = pl.ds(b * block, block)
            turned = jnp.dot(qact_raw[e, :, span], act_basis[span, :], preferred_element_type=jnp.float32)
            q_rot[pl.ds(pl.multiple_of(e * q_dev, 16), q_dev), span] = turned.astype(jnp.bfloat16)

    totals[...] = jnp.zeros_like(totals)
    finish_shared(qgrad_raw, qpass_send, qpass_recv, shared_query)

    def second_phase(jt):
        grads = turned_grads(qgrad_raw, jt, q_rows).astype(jnp.float32)
        for s in range(seq_count):
            mapped = jnp.dot(q_rot[...], precond[s, jt], preferred_element_type=jnp.float32) * grads
            folded = mapped[:, :128]
            for h in range(1, tile // 128):
                folded = folded + mapped[:, h * 128:(h + 1) * 128]
            totals[s] += folded.reshape(QUERIES, q_rows // QUERIES // 8, 8, 128).sum(axis=1)

    for c in range(chunks):
        finish_grads(qgrad_raw, qgrad_send, qgrad_recv, shared_query, c * chunk_cols, chunk_cols, c)
        pl.loop(c * per_chunk, (c + 1) * per_chunk)(second_phase)

    lane = lax.broadcasted_iota(jnp.int32, (QUERIES, 128), 1)
    answer = jnp.zeros((QUERIES, 128), jnp.float32)
    for s in range(seq_count):
        row = jnp.sum(jnp.sum(totals[s], axis=1), axis=1, keepdims=True)
        answer = jnp.where(lane == s, row, answer)
    lens = jnp.ones((QUERIES, 128), jnp.float32)
    for s in range(seq_count):
        lens = jnp.where(lane == s, limits[s].astype(jnp.float32), lens)
    shares[me] = answer * lax.rsqrt(lens) / math.sqrt(QUERY_LEN * D * FF)

    for copy in sends:
        copy.wait_send()
    sends.clear()

    for k in masks:
        begin(remote(shares.at[me], shares.at[me], share_send.at[k], share_recv.at[k], peers[k], mine))
    for k in masks:
        arrived(shares.at[peers[k]], share_send.at[k], share_recv.at[k])
    summed = shares[0]
    for e in range(1, dp_count):
        summed = summed + shares[e]
    crossing[mine] = summed
    for step, other in enumerate(others):
        begin(remote(
            crossing.at[mine], crossing.at[mine], cross_send.at[step], cross_recv.at[step], me, other))
    for step in range(mp_count - 1):
        owner = lax.rem(mine + (mp_count - 1 - step), mp_count)
        arrived(crossing.at[owner], cross_send.at[step], cross_recv.at[step])
    summed = crossing[0]
    for e in range(1, mp_count):
        summed = summed + crossing[e]
    partial[...] = across(summed)[:seq_count, :QUERIES]
    for copy in sends:
        copy.wait_send()


NEAR = (2, 4, 3, 5)
FAR = (6, 7)
TRAIN_CUTS = (0, 2, 4, 6, 8)
QUERY_CUTS = (0, 1, 2, 3, 4, 5, 6, 7, 8)
TRAIN_SPLITS = ((5, 7), (5, 7), (5, 7), (5, 7))
PLAN = (
    ("lead", 0, 0),
    ("lead", 0, 1),
    ("acts", 0),
    ("trail", 0, 0),
    ("lead", 0, 2),
    ("side", 0),
    ("relay", 0, 0),
    ("relay", 0, 1),
    ("pass", 0),
    ("lead", 0, 3),
    ("trail", 0, 1),
    ("lead", 1, 0),
    ("trail", 0, 2),
    ("acts", 1),
    ("trail", 0, 3),
    ("lead", 1, 1),
    ("side", 1),
    ("relay", 0, 2),
    ("first", 0),
    ("all", 0),
    ("sided", 0),
    ("rest", 0, 0),
    ("tiles", 0, 0, 2),
    ("relay", 0, 3),
    ("rest", 0, 1),
    ("tiles", 0, 2, 4),
    ("relay", 1, 0),
    ("rest", 0, 2),
    ("tiles", 0, 4, 6),
    ("pass", 1),
    ("lead", 1, 2),
    ("trail", 1, 0),
    ("lead", 1, 3),
    ("trail", 1, 1),
    ("lead", 1, 4),
    ("trail", 1, 2),
    ("lead", 1, 5),
    ("trail", 1, 3),
    ("lead", 1, 6),
    ("trail", 1, 4),
    ("lead", 1, 7),
    ("trail", 1, 5),
    ("trail", 1, 6),
    ("trail", 1, 7),
    ("rest", 0, 3),
    ("tiles", 0, 6, 8),
    ("relay", 1, 1),
    ("first", 1),
    ("all", 1),
    ("sided", 1),
    ("relay", 1, 2),
    ("rest", 1, 0),
    ("tiles", 1, 0, 1),
    ("relay", 1, 3),
    ("rest", 1, 1),
    ("tiles", 1, 1, 2),
    ("relay", 1, 4),
    ("rest", 1, 2),
    ("tiles", 1, 2, 3),
    ("relay", 1, 5),
    ("rest", 1, 3),
    ("tiles", 1, 3, 4),
    ("relay", 1, 6),
    ("rest", 1, 4),
    ("tiles", 1, 4, 5),
    ("relay", 1, 7),
    ("rest", 1, 5),
    ("tiles", 1, 5, 6),
    ("rest", 1, 6),
    ("tiles", 1, 6, 7),
    ("rest", 1, 7),
    ("tiles", 1, 7, 8),
)
QUERY_SPLITS = ((5, 7), (5, 7), (4, 8), (4, 8), (4, 8), (3, 8), (3, 8), (3, 8))


def routed_kernel(
    lengths, act_in, grad_in, query_act, query_grad, act_basis_in, grad_basis_in,
    moments, partial,
    act_raw, qact_raw, grad_raw, qgrad_raw, act_basis, grad_basis,
    act_t, act_sq, q_rot, precond, totals, shares,
    act_send, act_recv, grad_send, lead_recv, rest_recv, side_send, side_recv, local_sem,
    share_send, share_recv, ready,
):
    me = lax.axis_index("dp")
    mine = lax.axis_index("mp")
    dp_count = lax.axis_size("dp")
    mp_count = lax.axis_size("mp")
    tok_dev, act_width = act_in.shape
    seq_count = lengths.shape[0]
    q_dev = query_act.shape[0]
    cols = grad_raw.shape[1]
    block = act_basis.shape[1]
    tile = cols // TRAIN_CUTS[-1]
    tokens = tok_dev * dp_count
    seq_len = tokens // seq_count
    q_rows = q_dev * dp_count
    masks = list(range(1, dp_count))
    peers = {k: flipped(me, k) for k in masks}
    others = [lax.rem(mine + step, mp_count) for step in range(1, mp_count)]

    is_end = (mine == 0) | (mine == mp_count - 1)
    is_mid = jnp.logical_not(is_end)
    partner = flipped(mine, 1)
    half = lax.rem(mine + 1, 2)
    far_planes = [partner, mp_count - 1 - mine, mp_count - 1 - partner]

    barrier = pltpu.get_barrier_semaphore()
    for k in masks:
        pl.semaphore_signal(barrier, inc=1, device_id={"dp": peers[k], "mp": mine}, device_id_type=MESH)
    for other in others:
        pl.semaphore_signal(barrier, inc=1, device_id={"dp": me, "mp": other}, device_id_type=MESH)

    own = pl.ds(pl.multiple_of(me * cols, 128), cols)
    own_tok = pl.ds(pl.multiple_of(me * tok_dev, 128), tok_dev)
    own_q = pl.ds(pl.multiple_of(me * q_dev, 128), q_dev)
    locals_in = [
        pltpu.make_async_copy(act_in, act_raw.at[own_tok], local_sem.at[0]),
        pltpu.make_async_copy(act_basis_in, act_basis, local_sem.at[1]),
        pltpu.make_async_copy(grad_basis_in, grad_basis, local_sem.at[2]),
        pltpu.make_async_copy(grad_in.at[:, own], grad_raw.at[own_tok], local_sem.at[3]),
        pltpu.make_async_copy(query_act, qact_raw.at[own_q], local_sem.at[4]),
        pltpu.make_async_copy(query_grad.at[:, own], qgrad_raw.at[own_q], local_sem.at[5]),
    ]
    for copy in locals_in:
        copy.start()
    pl.semaphore_wait(barrier, len(masks) + len(others))

    def remote(src, dst, send, recv, dp, mp):
        return pltpu.make_async_remote_copy(
            src_ref=src, dst_ref=dst, send_sem=send, recv_sem=recv,
            device_id={"dp": dp, "mp": mp}, device_id_type=MESH)

    def arrived(ref, recv):
        remote(ref, ref, side_send.at[0], recv, peers[1], mine).wait_recv()

    def left(ref, send):
        remote(ref, ref, send, side_recv.at[0], peers[1], mine).wait_send()

    def by_role(act):
        @pl.when(is_end)
        def _():
            act("end")

        @pl.when(is_mid)
        def _():
            act("mid")

    phases = (
        (grad_in, grad_raw, tok_dev, TRAIN_CUTS, TRAIN_SPLITS),
        (query_grad, qgrad_raw, q_dev, QUERY_CUTS, QUERY_SPLITS),
    )

    def span_of(phase, c):
        cuts = phases[phase][3]
        return cuts[c] * tile, (cuts[c + 1] - cuts[c]) * tile

    def count_of(phase, part, c):
        first, second = phases[phase][4][c]
        eighth = phases[phase][2] // 8
        return {"a": first, "b": second - first, "c": 8 - second, "own": 4}[part] * eighth

    def rows_of(phase, part, c):
        first, second = phases[phase][4][c]
        eighth = phases[phase][2] // 8
        low = {"a": 0, "b": first, "c": second, "own": half * 4}[part]
        return low * eighth, count_of(phase, part, c)

    def held(phase, k, part, c):
        start, width = span_of(phase, c)
        low, rows = rows_of(phase, part, c)
        here = pl.ds(pl.multiple_of(peers[k] * phases[phase][2] + low, 16), rows)
        return phases[phase][1].at[here, pl.ds(start, width)]

    def bulk(phase, rows, c):
        start, width = span_of(phase, c)
        return phases[phase][1].at[pl.ds(0, rows), pl.ds(start, width)]

    def hop(phase, part, c, ks, recv):
        src, raw, size, _, _ = phases[phase]
        start, width = span_of(phase, c)
        low, rows = rows_of(phase, part, c)
        if not rows:
            return
        taken = pl.ds(pl.multiple_of(low, 16), rows)
        put = pl.ds(pl.multiple_of(me * size + low, 16), rows)
        for k in ks:
            there = pl.ds(pl.multiple_of(peers[k] * cols + start, 128), width)
            remote(
                src.at[taken, there], raw.at[put, pl.ds(start, width)],
                grad_send.at[phase, c], recv, peers[k], mine).start()

    def lead(role, phase, c):
        if role == "end":
            hop(phase, "a", c, NEAR[:2], lead_recv.at[phase, c, 0])
            hop(phase, "a", c, NEAR[2:], lead_recv.at[phase, c, 1])
        else:
            hop(phase, "own", c, FAR, lead_recv.at[phase, c, 0])
            hop(phase, "c", c, NEAR, lead_recv.at[phase, c, 1])

    def trail(role, phase, c):
        hop(phase, "b", c, NEAR, rest_recv.at[phase, c])

    def relay(role, phase, c):
        def onward(k, part, to):
            here = held(phase, k, part, c)
            remote(here, here, grad_send.at[phase, c], rest_recv.at[phase, c], me, to).start()

        if role == "end":
            for g, ks in enumerate((NEAR[:2], NEAR[2:])):
                arrived(bulk(phase, 2 * count_of(phase, "a", c), c), lead_recv.at[phase, c, g])
                for k in ks:
                    onward(k, "a", partner)
        else:
            arrived(bulk(phase, 2 * count_of(phase, "own", c), c), lead_recv.at[phase, c, 0])
            for to in far_planes:
                for k in FAR:
                    onward(k, "own", to)
            if count_of(phase, "c", c):
                arrived(bulk(phase, 4 * count_of(phase, "c", c), c), lead_recv.at[phase, c, 1])
                for k in NEAR:
                    onward(k, "c", partner)

    def rest(role, phase, c):
        a, b, d, own_half = [count_of(phase, part, c) for part in ("a", "b", "c", "own")]
        rows = 4 * (b + d) + 4 * own_half if role == "end" else 4 * (a + b) + 2 * own_half
        arrived(bulk(phase, rows, c), rest_recv.at[phase, c])

    def gone(role, phase):
        for c in range(len(phases[phase][4])):
            a, b, d, own_half = [count_of(phase, part, c) for part in ("a", "b", "c", "own")]
            rows = 4 * (a + b) + 4 * a if role == "end" else 4 * (b + d) + 2 * own_half + 6 * own_half + 4 * d
            left(bulk(phase, rows, c), grad_send.at[phase, c])

    def side(phase):
        src, raw, size, _, _ = phases[phase]
        there = pl.ds(pl.multiple_of(peers[1] * cols, 128), cols)
        put = pl.ds(pl.multiple_of(me * size, 128), size)
        remote(src.at[:, there], raw.at[put], side_send.at[phase], side_recv.at[phase], peers[1], mine).start()

    def finish_side(phase):
        arrived(phases[phase][1].at[pl.ds(0, phases[phase][2])], side_recv.at[phase])

    acts = ((act_in, act_raw, tok_dev), (query_act, qact_raw, q_dev))

    def act_rows(phase, k, low, rows):
        size = acts[phase][2]
        return acts[phase][1].at[pl.ds(pl.multiple_of(peers[k] * size + low, 16), rows)]

    def act_go(phase, src, dst, recv_slot, k):
        remote(src, dst, act_send.at[phase], act_recv.at[phase, recv_slot], peers[k], mine).start()

    def send_acts(phase):
        src, raw, size = acts[phase]
        put = raw.at[pl.ds(pl.multiple_of(me * size, 16), size)]
        for k, slot in ((2, 0), (4, 1), (1, 3)):
            act_go(phase, src, put, slot, k)

    def pass_acts(phase):
        _, raw, size = acts[phase]
        for n, (k, onward) in enumerate(((2, 4), (4, 2))):
            arrived(raw.at[pl.ds(0, size)], act_recv.at[phase, n])
            part = act_rows(phase, k, n * (size // 2), size // 2)
            act_go(phase, part, part, 2, onward)
        for k in (2, 4):
            whole = act_rows(phase, k, 0, size)
            act_go(phase, whole, whole, 3, 1)

    def finish_acts(phase):
        _, raw, size = acts[phase]
        arrived(raw.at[pl.ds(0, size)], act_recv.at[phase, 2])
        whole = act_rows(phase, 6, 0, size)
        act_go(phase, whole, whole, 4, 1)

    def near_acts(phase):
        _, raw, size = acts[phase]
        arrived(raw.at[pl.ds(0, 3 * size)], act_recv.at[phase, 3])

    def last_acts(phase):
        _, raw, size = acts[phase]
        arrived(raw.at[pl.ds(0, size)], act_recv.at[phase, 4])

    def acts_gone(phase):
        _, raw, size = acts[phase]
        left(raw.at[pl.ds(0, 7 * size)], act_send.at[phase])

    for other in others:
        pl.semaphore_signal(ready, inc=1, device_id={"dp": me, "mp": other}, device_id_type=MESH)

    limits = [lengths[s] for s in range(seq_count)]
    counted = limits[0]
    for s in range(1, seq_count):
        counted = counted + limits[s]
    inverse = 1.0 / jnp.full((1, tile), counted.astype(jnp.float32), jnp.float32)

    def chip_rows(p, rows):
        place, result = 1, 0
        chip = lax.div(me, 2)
        while place < dp_count // 2:
            result = result + place * lax.rem(lax.div(chip, place) + lax.div(p, place), 2)
            place *= 2
        return result * rows

    def wide(basis, start, count):
        rows = []
        zero = jnp.zeros((block, block), jnp.bfloat16)
        for h in range(count):
            piece = basis[pl.ds(start + h * block, block), :]
            rows.append(jnp.concatenate([piece if g == h else zero for g in range(count)], axis=1))
        return jnp.concatenate(rows, axis=0)

    def turn_acts(low, high):
        rows = 2 * tok_dev

        @pl.loop(low // 2, high // 2)
        def _(p):
            first = chip_rows(p, rows)
            where_tok = first + lax.broadcasted_iota(jnp.int32, (2 * block, rows), 1)
            live = jnp.zeros((2 * block, rows), jnp.float32)
            for s in range(seq_count):
                inside = (where_tok >= s * seq_len) & (where_tok < s * seq_len + limits[s])
                live = jnp.where(inside, 1.0, live)
            to = pl.ds(pl.multiple_of(first, 128), rows)
            for b in range(act_width // (2 * block)):
                span = pl.ds(b * 2 * block, 2 * block)
                turned = lax.dot_general(
                    wide(act_basis, b * 2 * block, 2).T, act_raw[to, span], (((1,), (1,)), ((), ())),
                    preferred_element_type=jnp.float32)
                kept = (turned * live).astype(jnp.bfloat16)
                act_t[span, to] = kept
                act_sq[span, to] = kept * kept

    def turn_query_acts(low, high):
        rows = 2 * q_dev

        @pl.loop(low // 2, high // 2)
        def _(p):
            here = pl.ds(pl.multiple_of(chip_rows(p, rows), 128), rows)
            for b in range(act_width // (2 * block)):
                span = pl.ds(b * 2 * block, 2 * block)
                turned = jnp.dot(
                    qact_raw[here, span], wide(act_basis, b * 2 * block, 2), preferred_element_type=jnp.float32)
                q_rot[here, span] = turned.astype(jnp.bfloat16)

    def turned_grads(raw, jt):
        start = pl.multiple_of(jt * tile, 128)
        whole = raw[:, pl.ds(start, tile)]
        return jnp.dot(
            whole, wide(grad_basis, start, tile // block), preferred_element_type=jnp.float32).astype(jnp.bfloat16)

    def train_tile(jt):
        grads = turned_grads(grad_raw, jt)
        total = jnp.dot(act_sq[...], grads * grads, preferred_element_type=jnp.float32) * inverse
        moments[:, pl.ds(pl.multiple_of(jt * tile, 128), tile)] = total
        weights = 1.0 / (total + damping)
        for s in range(seq_count):
            a = act_t[:, s * seq_len:(s + 1) * seq_len]
            g = grads[s * seq_len:(s + 1) * seq_len, :]
            precond[s, :, pl.ds(pl.multiple_of(jt * tile, 128), tile)] = (
                weights * jnp.dot(a, g, preferred_element_type=jnp.float32)).astype(jnp.bfloat16)

    def query_tiles(low, high):
        grads = [turned_grads(qgrad_raw, jt).astype(jnp.float32) for jt in range(low, high)]
        grads = jnp.concatenate(grads, axis=1)
        for s in range(seq_count):
            weights = precond[s, :, pl.ds(low * tile, (high - low) * tile)]
            mapped = jnp.dot(q_rot[...], weights, preferred_element_type=jnp.float32) * grads
            folded = mapped[:, :128]
            for h in range(1, mapped.shape[1] // 128):
                folded = folded + mapped[:, h * 128:(h + 1) * 128]
            totals[s] += folded.reshape(QUERIES, q_rows // QUERIES // 8, 8, 128).sum(axis=1)

    turn = (turn_acts, turn_query_acts)

    def first_acts(phase):
        near_acts(phase)
        if phase == 0:
            for copy in locals_in:
                copy.wait()
            totals[...] = jnp.zeros_like(totals)
        turn[phase](0, 6)

    def all_acts(phase):
        finish_acts(phase)
        last_acts(phase)
        turn[phase](6, dp_count)

    def tiles_now(phase, low, high):
        if phase:
            query_tiles(low, high)
        else:
            pl.loop(low, high)(train_tile)

    by_roles = {"lead": lead, "trail": trail, "relay": relay, "rest": rest}
    plain = {
        "acts": send_acts, "pass": pass_acts, "first": first_acts, "all": all_acts,
        "side": side, "sided": finish_side, "tiles": tiles_now}
    for shared, group in itertools.groupby(PLAN, lambda step: step[0] in by_roles):
        group = list(group)
        if shared:
            by_role(lambda role: [by_roles[name](role, *where) for name, *where in group])
        else:
            for name, *where in group:
                plain[name](*where)

    lane = lax.broadcasted_iota(jnp.int32, (QUERIES, 128), 1)
    answer = jnp.zeros((QUERIES, 128), jnp.float32)
    for s in range(seq_count):
        row = jnp.sum(jnp.sum(totals[s], axis=1), axis=1, keepdims=True)
        answer = jnp.where(lane == s, row, answer)
    lens = jnp.ones((QUERIES, 128), jnp.float32)
    for s in range(seq_count):
        lens = jnp.where(lane == s, limits[s].astype(jnp.float32), lens)
    slot = mine * dp_count + me
    shares[slot] = across(answer * lax.rsqrt(lens) / math.sqrt(QUERY_LEN * D * FF))

    pl.semaphore_wait(ready, len(others))
    mine_there = shares.at[slot]
    for step in reversed(range(mp_count)):
        plane = lax.rem(mine + step, mp_count)
        for k in reversed(range(dp_count)):
            if k or step:
                remote(
                    mine_there, mine_there, share_send.at[0], share_recv.at[0],
                    peers[k] if k else me, plane).start()

    def ended(role):
        gone(role, 0)
        gone(role, 1)

    by_role(ended)
    for phase in range(2):
        acts_gone(phase)
        left(phases[phase][1].at[pl.ds(0, phases[phase][2])], side_send.at[phase])
    every = shares.at[pl.ds(0, dp_count * mp_count - 1)]
    left(every, share_send.at[0])
    arrived(every, share_recv.at[0])
    summed = shares[0]
    for e in range(1, dp_count * mp_count):
        summed = summed + shares[e]
    partial[...] = summed[:seq_count, :QUERIES]


def routed(act_in, grad_in, query_act, query_grad, act_basis, grad_basis, seq_lengths):
    dp_count = lax.axis_size("dp")
    mp_count = lax.axis_size("mp")
    tok_dev, act_width = act_in.shape
    q_dev = query_act.shape[0]
    cols = grad_in.shape[1] // dp_count
    seq_count = seq_lengths.shape[0]
    tokens, q_rows = tok_dev * dp_count, q_dev * dp_count
    dma = pltpu.SemaphoreType.DMA
    any_space = pl.BlockSpec(memory_space=pl.ANY)
    bf16 = jnp.bfloat16
    chunks = max(len(TRAIN_SPLITS), len(QUERY_SPLITS))
    return pl.pallas_call(
        routed_kernel,
        out_shape=(
            pltpu.VMEM((act_width, cols), jnp.float32),
            pltpu.VMEM((seq_count, QUERIES), jnp.float32),
        ),
        in_specs=[pl.BlockSpec(memory_space=pltpu.SMEM)] + [any_space] * 6,
        out_specs=(pl.BlockSpec(memory_space=pltpu.VMEM), pl.BlockSpec(memory_space=pltpu.VMEM)),
        scratch_shapes=[
            pltpu.VMEM((tokens, act_width), bf16),
            pltpu.VMEM((q_rows, act_width), bf16),
            pltpu.VMEM((tokens, cols), bf16),
            pltpu.VMEM((q_rows, cols), bf16),
            pltpu.VMEM(act_basis.shape, bf16),
            pltpu.VMEM((cols, grad_basis.shape[1]), bf16),
            pltpu.VMEM((act_width, tokens), bf16),
            pltpu.VMEM((act_width, tokens), bf16),
            pltpu.VMEM((q_rows, act_width), bf16),
            pltpu.VMEM((seq_count, act_width, cols), bf16),
            pltpu.VMEM((seq_count, QUERIES, 8, 128), jnp.float32),
            pltpu.VMEM((dp_count * mp_count, 8, 128), jnp.float32),
            dma((2,)), dma((2, 5)), dma((2, chunks)), dma((2, chunks, 2)), dma((2, chunks)),
            dma((2,)), dma((2,)), dma((6,)), dma((1,)), dma((1,)), pltpu.SemaphoreType.REGULAR,
        ],
        compiler_params=pltpu.CompilerParams(
            collective_id=1, has_side_effects=True, vmem_limit_bytes=54 * 1024 * 1024),
    )(seq_lengths, act_in, grad_in, query_act, query_grad, act_basis, grad_basis)


def local(act_in, grad_in, query_act, query_grad, act_basis, grad_basis, seq_lengths):
    dp_count = lax.axis_size("dp")
    mp_count = lax.axis_size("mp")
    tok_dev, act_width = act_in.shape
    q_dev = query_act.shape[0]
    cols = grad_in.shape[1] // dp_count
    seq_count = seq_lengths.shape[0]
    tokens, q_rows = tok_dev * dp_count, q_dev * dp_count
    if dp_count == 8 and mp_count == 4 and tok_dev % 128 == 0 and q_dev % 128 == 0 and cols % 2048 == 0 and (
            2 * tok_dev * seq_count == tokens and act_width == q_rows):
        moments, scores = store(*routed(
            act_in, grad_in, query_act, query_grad, act_basis, grad_basis, seq_lengths), seq_count)
        return moments, scores.T
    tile = min(256, cols)
    tiles = cols // tile
    chunks = min(4, tiles)
    far = [k for k in range(1, dp_count) if bin(k >> 1).count("1") >= 2]
    shared_train = far if tok_dev % (16 * mp_count) == 0 and dp_count <= 2 * tiles else []
    shared_query = far if q_dev % (16 * mp_count) == 0 and dp_count <= 2 * tiles else []
    steps = max(1, mp_count - 1)
    dma = pltpu.SemaphoreType.DMA
    any_space = pl.BlockSpec(memory_space=pl.ANY)
    bf16 = jnp.bfloat16
    raw, scores = pl.pallas_call(
        functools.partial(kernel, dp_count, mp_count, chunks, shared_train, shared_query),
        out_shape=(
            pltpu.VMEM((act_width, cols), jnp.float32),
            pltpu.VMEM((seq_count, QUERIES), jnp.float32),
        ),
        in_specs=[pl.BlockSpec(memory_space=pltpu.SMEM)] + [any_space] * 6,
        out_specs=(pl.BlockSpec(memory_space=pltpu.VMEM), pl.BlockSpec(memory_space=pltpu.VMEM)),
        scratch_shapes=[
            pltpu.VMEM((dp_count, tok_dev, act_width), bf16),
            pltpu.VMEM((dp_count, q_dev, act_width), bf16),
            pltpu.VMEM((dp_count, tok_dev, cols), bf16),
            pltpu.VMEM((dp_count, q_dev, cols), bf16),
            pltpu.VMEM(act_basis.shape, bf16),
            pltpu.VMEM(grad_basis.shape, bf16),
            pltpu.VMEM((act_width, tokens), bf16),
            pltpu.VMEM((q_rows, act_width), bf16),
            pltpu.VMEM((seq_count, tiles, act_width, tile), bf16),
            pltpu.VMEM((tiles, 8, tile), jnp.float32),
            pltpu.VMEM((seq_count, QUERIES, 8, 128), jnp.float32),
            dma((dp_count,)), dma((dp_count,)), dma((dp_count,)), dma((dp_count,)),
            dma((1, dp_count)), dma((1, dp_count)), dma((chunks, dp_count)), dma((chunks, dp_count)),
            dma((max(1, len(shared_train)), steps)), dma((max(1, len(shared_train)), steps)),
            dma((max(1, len(shared_query)), steps)), dma((max(1, len(shared_query)), steps)),
            dma((6,)), dma((tiles,)),
            pltpu.VMEM((dp_count, QUERIES, 128), jnp.float32),
            pltpu.VMEM((mp_count, QUERIES, 128), jnp.float32),
            dma((dp_count,)), dma((dp_count,)), dma((steps,)), dma((steps,)),
        ],
        compiler_params=pltpu.CompilerParams(
            collective_id=0, has_side_effects=True, vmem_limit_bytes=54 * 1024 * 1024),
    )(seq_lengths, act_in, grad_in, query_act, query_grad, act_basis, grad_basis)
    moments, scores = store(raw, scores, seq_count)
    return moments, scores.T


def store_kernel(raw, scores_in, moments, scores, sems):
    n = sems.shape[0] - 1
    rows = raw.shape[0] // n
    copies = [pltpu.make_async_copy(raw.at[pl.ds(i * rows, rows)], moments.at[pl.ds(i * rows, rows)], sems.at[i])
              for i in range(n)]
    copies.append(pltpu.make_async_copy(scores_in, scores, sems.at[n]))
    for c in copies:
        c.start()
    for c in copies:
        c.wait()


def store(raw, scores, seq_count):
    n = 8
    vm = pl.BlockSpec(memory_space=pltpu.VMEM)
    return pl.pallas_call(
        store_kernel,
        out_shape=(jax.ShapeDtypeStruct(raw.shape, raw.dtype), jax.ShapeDtypeStruct((seq_count, QUERIES), scores.dtype)),
        in_specs=[vm, vm], out_specs=(pl.BlockSpec(memory_space=pltpu.HBM), pl.BlockSpec(memory_space=pltpu.HBM)),
        scratch_shapes=[pltpu.SemaphoreType.DMA((n + 1,))],
        compiler_params=pltpu.CompilerParams(vmem_limit_bytes=1024*1024),
    )(pltpu.with_memory_space_constraint(raw, pltpu.VMEM), pltpu.with_memory_space_constraint(scores, pltpu.VMEM))


def solution(mesh):
    return jax.shard_map(
        local,
        mesh=mesh,
        in_specs=(
            P("dp", "mp"),
            P("dp", None),
            P("dp", "mp"),
            P("dp", None),
            P("mp", None),
            P("dp", None),
            P(),
        ),
        out_specs=(P("mp", "dp"), P()),
        check_vma=False,
    )
```
